32 devices in a mesh: dp: 8 (over y, x, core), shard: 4 (over z).
Axes of the slice: x: 2, y: 2, z: 4, core: 2. Of those that a mesh axis runs over, the one named last changes fastest.
Arguments:
- cell_tokens: bfloat16 [32, 1024, 512], P(('dp', 'shard')), may hold values from -6 to 6
- lengths: int32 [32], P(('dp', 'shard')), may hold values from 200 to 1024, as said below
- classes: int32 [32], P(('dp', 'shard')), may hold values 0 or 1
- cotangent: bfloat16 [32, 1024, 512], P(('dp', 'shard')), may hold values from -6 to 6
- weights: float32 [2, 6, 512, 512], P(None, None, 'shard')
- vectors: float32 [2, 9, 512], P(None, None, 'shard')
- first_weights: float32 [2, 6, 512, 512], P(None, None, 'shard'), as said below
- second_weights: float32 [2, 6, 512, 512], P(None, None, 'shard'), as said below
- first_vectors: float32 [2, 9, 512], P(None, None, 'shard'), as said below
- second_vectors: float32 [2, 9, 512], P(None, None, 'shard'), as said below
Outputs:
- activations: bfloat16 [32, 1024, 512], P(('dp', 'shard'))
- input_grad: float32 [32, 1024, 512], P(('dp', 'shard'))
- new_weights: float32 [2, 6, 512, 512], P(None, None, 'shard')
- weights_low: bfloat16 [2, 6, 512, 512], P(None, None, 'shard')
- new_first_weights: float32 [2, 6, 512, 512], P(None, None, 'shard')
- new_second_weights: float32 [2, 6, 512, 512], P(None, None, 'shard')
- new_vectors: float32 [2, 9, 512], P(None, None, 'shard')
- new_first_vectors: float32 [2, 9, 512], P(None, None, 'shard')
- new_second_vectors: float32 [2, 9, 512], P(None, None, 'shard')
- query_bias_grad: float32 [2, 512], P(None, 'shard')
The draws below stay inside these ranges and needn't reach their ends.
Inputs may be any that keep to these rules, and one draw needn't show every extreme that they name: `lengths`: each cell has 200 to 1024 gene tokens; some cell has exactly 1024. `first_weights`: entries have both signs. `second_weights`: entries are positive. `first_vectors`: entries have both signs. `second_vectors`: entries are positive.
All inputs are finite; a program needn't handle non-finite values. No bound on the sum of `classes` on one device may be relied on, other than what follows from the above.
Results may differ from the reference program's by a relative error of at most 0.022.
Values may be sent and summed in bfloat16 or wider, within the bound.
A program may use at most 256 MiB of HBM per device.

```python
import math
import jax
import jax.numpy as jnp
from jax import lax

D = 512
HEADS = 8
HEAD_DIM = 64
LAYERS = 2
LMAX = 1024
MINLEN = 200
CELLS = 32


beta_first = 0.5


beta_second = 0.55


def grad_size():
    return math.sqrt(CELLS * (MINLEN + LMAX) / 2.0)


def draw_lengths(key, part):
    drawn = jax.random.randint(key, (CELLS,), MINLEN, LMAX + 1, dtype=jnp.int32)
    chosen = jax.random.randint(jax.random.fold_in(key, 7), (), 0, CELLS, dtype=jnp.int32)
    cell_ids = jnp.arange(CELLS, dtype=jnp.int32)
    return jnp.where(cell_ids == chosen, LMAX, drawn).astype(jnp.int32)


def draw_weights(key, part):
    normal_part = jax.random.normal(key, (LAYERS, 6, D, D), jnp.float32)
    kind_ids = jnp.arange(6, dtype=jnp.int32)[None, :, None, None]
    factor = jnp.where(kind_ids == 3, 4.0, 1.0)
    return (normal_part * factor / math.sqrt(D)).astype(jnp.float32)


def draw_vectors(key, part):
    normal_part = jax.random.normal(key, (LAYERS, 9, D), jnp.float32) * 0.3
    gain_part = 1.0 + jax.random.uniform(jax.random.fold_in(key, 3), (LAYERS, 9, D), jnp.float32, -0.3, 0.3)
    row_ids = jnp.arange(9, dtype=jnp.int32)[None, :, None]
    is_gain = (row_ids == 5) | (row_ids == 7)
    return jnp.where(is_gain, gain_part, normal_part).astype(jnp.float32)


def first_moment(key, shape):
    scale = grad_size() * (1.0 - beta_first) / beta_first
    return (jax.random.normal(key, shape, jnp.float32) * scale).astype(jnp.float32)


def second_moment(key, shape):
    scale = grad_size() * grad_size() * (1.0 - beta_second) / beta_second
    return (jax.random.uniform(key, shape, jnp.float32, 1.0, 4.0) * scale).astype(jnp.float32)


def draw_first_weights(key, part):
    return first_moment(key, (LAYERS, 6, D, D))


def draw_second_weights(key, part):
    return second_moment(key, (LAYERS, 6, D, D))


def draw_first_vectors(key, part):
    return first_moment(key, (LAYERS, 9, D))


def draw_second_vectors(key, part):
    return second_moment(key, (LAYERS, 9, D))


def set_ends(array, stream_key, least, largest):
    place = [jax.random.randint(jax.random.fold_in(stream_key, axis), (), 0, length) for axis, length in enumerate(array.shape)]
    widest = array.shape.index(max(array.shape))
    next_to = place[:widest] + [(place[widest] + 1) % array.shape[widest]] + place[widest + 1:]
    return array.at[tuple(place)].set(least).at[tuple(next_to)].set(largest)


def steps_of(key, dims, split, low, top_value):
    level, own = 1.0, jax.random.fold_in(key, 6)
    for axis_at, shards_of in split:
        steps = jnp.exp(jax.random.uniform(jax.random.fold_in(own, axis_at), (shards_of,), jnp.float32, low / len(split), top_value / len(split)))
        level = level * jnp.repeat(steps, dims[axis_at] // shards_of).reshape([-1 if axis == axis_at else 1 for axis in range(len(dims))])
    return level


def bell_draw(key, shape, width, reach, split=(), held_as=jnp.bfloat16):
    values = width * jax.random.normal(key, shape, jnp.float32)
    if split:
        values = values * steps_of(key, shape, split, -0.22, 0.18)
    return jnp.clip(values, -reach, reach).astype(held_as)


def setup_inputs(seed: int = 0) -> dict:
    arg_keys = jax.random.split(jax.random.key(seed), 11)
    return {
        "cell_tokens": bell_draw(arg_keys[0], (CELLS, LMAX, D), 1.0, 6.0, ((0, 32),)),
        "lengths": draw_lengths(jax.random.fold_in(arg_keys[10], 71), 0),
        "classes": set_ends((jax.random.randint(arg_keys[2], (CELLS,), 0, 2) < 1).astype(jnp.int32), jax.random.fold_in(arg_keys[2], 1), 0, 1),
        "cotangent": bell_draw(arg_keys[3], (CELLS, LMAX, D), 1.0, 6.0, ((0, 32),)),
        "weights": draw_weights(jax.random.fold_in(arg_keys[10], 71), 0),
        "vectors": draw_vectors(jax.random.fold_in(arg_keys[10], 71), 0),
        "first_weights": draw_first_weights(jax.random.fold_in(arg_keys[10], 71), 0),
        "second_weights": draw_second_weights(jax.random.fold_in(arg_keys[10], 71), 0),
        "first_vectors": draw_first_vectors(jax.random.fold_in(arg_keys[10], 71), 0),
        "second_vectors": draw_second_vectors(jax.random.fold_in(arg_keys[10], 71), 0),
    }


@jax.custom_vjp
def low(v):
    return lax.optimization_barrier(v.astype(jnp.bfloat16)).astype(jnp.float32)

@jax.custom_vjp
def low_back(v):
    return v

def low_keep(v):
    return (low(v), None)

def low_pass(kept, grad):
    return (grad,)

def back_keep(v):
    return (v, None)

def back_low(kept, grad):
    return (low(grad),)
low.defvjp(low_keep, low_pass)
low_back.defvjp(back_keep, back_low)
beta_first = 0.5
beta_second = 0.55
learn_rate = 0.05
vector_rate = 0.25
decay_rate = 0.01
adam_eps = 1e-08
adam_step = 3.0
norm_eps = 1e-05

def both_round(value):
    return low_back(low(value))

def layer_norm(value, gain, shift):
    center = lax.optimization_barrier(jnp.mean(value, axis=-1, keepdims=True))
    centered = value - center
    spread = lax.optimization_barrier(jnp.mean(centered * centered, axis=-1, keepdims=True))
    return centered * lax.rsqrt(spread + norm_eps) * gain + shift

def matmul(left, right):
    return jnp.dot(left, right, precision=lax.Precision.HIGHEST, preferred_element_type=jnp.float32)

def allowed_mask(length, klass, token_count):
    row_ids = jnp.arange(token_count, dtype=jnp.int32)[:, None]
    col_ids = jnp.arange(token_count, dtype=jnp.int32)[None, :]
    known = (length + 1) // 2
    inside = (row_ids < length) & (col_ids < length) & ((klass == 0) | (col_ids < known))
    return inside | (row_ids == col_ids)

def cell_layer(inputs, mats, vecs, length, klass):
    token_count = inputs.shape[0]
    inputs_low = low(inputs)
    query = both_round(matmul(inputs_low, mats[0]) + vecs[0])
    keys = both_round(matmul(inputs_low, mats[1]))
    values = both_round(matmul(inputs_low, mats[2]) + vecs[1])
    query_heads = query.reshape(token_count, HEADS, HEAD_DIM)
    key_heads = keys.reshape(token_count, HEADS, HEAD_DIM)
    value_heads = values.reshape(token_count, HEADS, HEAD_DIM)
    scores = jnp.einsum('qhd,khd->hqk', query_heads, key_heads, precision=lax.Precision.HIGHEST)
    scores = low_back(scores * (1.0 / math.sqrt(HEAD_DIM)))
    allowed = allowed_mask(length, klass, token_count)
    scores = jnp.where(allowed[None], scores, -1e+30)
    probs = low(jax.nn.softmax(scores, axis=-1))
    mixed = jnp.einsum('hqk,khd->qhd', probs, value_heads, precision=lax.Precision.HIGHEST)
    mixed = both_round(mixed.reshape(token_count, D))
    branch = low_back(matmul(mixed, mats[3]) + vecs[2])
    first_out = layer_norm(inputs + branch, vecs[5], vecs[6])
    first_low = low(first_out)
    hidden_pre = low_back(matmul(first_low, mats[4]) + vecs[3])
    hidden_low = low(jax.nn.gelu(hidden_pre, approximate=False))
    feed = low_back(matmul(hidden_low, mats[5]) + vecs[4])
    return layer_norm(first_out + feed, vecs[7], vecs[8])

def adam_update(param, grad, first, second, rate):
    first_new = beta_first * first + (1.0 - beta_first) * grad
    second_new = beta_second * second + (1.0 - beta_second) * grad * grad
    first_hat = first_new / (1.0 - beta_first ** adam_step)
    second_hat = second_new / (1.0 - beta_second ** adam_step)
    param_new = param - rate * (first_hat / (jnp.sqrt(second_hat) + adam_eps) + decay_rate * param)
    return (param_new, first_new, second_new)

def reference(cell_tokens, lengths, classes, cotangent, weights, vectors, first_weights, second_weights, first_vectors, second_vectors):

    def forward(tokens_in, weights_in, vectors_in):
        mats_all = low(weights_in)
        vecs_all = low(vectors_in)

        def one_cell(packed):
            cell_input, length, klass = packed
            current = cell_input
            for layer_index in range(LAYERS):
                current = cell_layer(current, mats_all[layer_index], vecs_all[layer_index], length, klass)
            valid = (jnp.arange(LMAX, dtype=jnp.int32) < length).astype(current.dtype)[:, None]
            return current * valid
        return lax.map(jax.checkpoint(one_cell), (tokens_in, lengths, classes))
    tokens_wide = cell_tokens.astype(jnp.float32)
    outputs, pullback = jax.vjp(forward, tokens_wide, weights, vectors)
    grad_tokens, grad_weights, grad_vectors = pullback(cotangent.astype(jnp.float32))
    new_weights, new_first_weights, new_second_weights = adam_update(weights, grad_weights, first_weights, second_weights, learn_rate)
    new_vectors, new_first_vectors, new_second_vectors = adam_update(vectors, grad_vectors, first_vectors, second_vectors, vector_rate)
    return (outputs.astype(jnp.bfloat16), grad_tokens, new_weights, new_weights.astype(jnp.bfloat16), new_first_weights, new_second_weights, new_vectors, new_first_vectors, new_second_vectors, grad_vectors[:, 0])
```

```python
import functools
import math

import jax
import jax.numpy as jnp
from jax import lax
from jax.experimental import pallas as pl
from jax.experimental.pallas import tpu as pltpu
from jax.sharding import PartitionSpec as P

HEADS = 8
beta_first = 0.5
beta_second = 0.55
learn_rate = 0.05
vector_rate = 0.25
decay_rate = 0.01
adam_eps = 1e-08
adam_step = 3.0
norm_eps = 1e-05

LOG2E = 1.4426950408889634
LN2 = 0.6931471805599453
NEG = -1e30
f32 = jnp.float32
bf16 = jnp.bfloat16
PAIR = 128
RB = 256


def dot(left, right):
    return jnp.dot(left, right, preferred_element_type=f32)


def dot_nt(left, right):
    return lax.dot_general(left, right, (((1,), (1,)), ((), ())), preferred_element_type=f32)


def dot_tn(left, right):
    return lax.dot_general(left, right, (((0,), (0,)), ((), ())), preferred_element_type=f32)


def gelu_parts(value):
    size = jnp.abs(value) * (1.0 / math.sqrt(2.0))
    step = 1.0 / (1.0 + 0.3275911 * size)
    bell = jnp.exp2(value * value * (-0.5 * LOG2E))
    poly = step * (0.254829592 + step * (-0.284496736 + step * (1.421413741 + step * (-1.453152027 + step * 1.061405429))))
    tail = 0.5 * poly * bell
    below = jnp.where(value < 0.0, tail, 1.0 - tail)
    return value * below, below + value * bell * (1.0 / math.sqrt(2.0 * math.pi))


def normalize(value):
    center = jnp.mean(value, axis=-1, keepdims=True)
    centered = value - center
    spread = jnp.mean(centered * centered, axis=-1, keepdims=True)
    inverse = lax.rsqrt(spread + norm_eps)
    return centered * inverse, inverse


def norm_back(grad, normed, inverse, gain):
    scaled = grad * gain
    return inverse * (
        scaled
        - jnp.mean(scaled, axis=-1, keepdims=True)
        - normed * jnp.mean(scaled * normed, axis=-1, keepdims=True)
    )


def lane_masks(rows=1):
    lane = lax.broadcasted_iota(jnp.int32, (rows, PAIR), 1)
    low = jnp.where(lane < 64, 1.0, 0.0)
    return low.astype(bf16), (1.0 - low).astype(bf16)


class Refs:
    pass


def fill_bias(m, known):
    tokens = m.key_bias.shape[0]
    row = lax.broadcasted_iota(jnp.int32, (tokens, PAIR), 0)
    lane = lax.broadcasted_iota(jnp.int32, (tokens, PAIR), 1)
    m.key_bias[...] = jnp.where((lane == 0) & (row >= known), NEG, 0.0).astype(bf16)


def project(m, layer, xb):
    tokens = xb.shape[0]
    scale = LOG2E / 8.0

    def block(index, carry):
        rows = pl.ds(pl.multiple_of(index * 2 * RB, 2 * RB), 2 * RB)
        low = xb[rows, :]
        m.q[layer, rows, :] = ((dot(low, m.w[layer, 0]) + m.vec(layer, 0)) * scale).astype(bf16)
        m.k[layer, rows, :] = dot(low, m.w[layer, 1]).astype(bf16)
        m.v[layer, rows, :] = (dot(low, m.w[layer, 2]) + m.vec(layer, 1)).astype(bf16)
        return carry

    lax.fori_loop(0, tokens // (2 * RB), block, 0)


def probs_copy(m, layer, pair, slot, out):
    here, there = m.probs.at[slot], m.probs_hbm.at[layer, pair]
    if out:
        return pltpu.make_async_copy(here, there, m.probs_sem.at[slot])
    return pltpu.make_async_copy(there, here, m.probs_sem.at[slot])


def attend(m, layer, known):
    tokens, width = m.q.shape[1:]
    pairs = width // PAIR
    masks = lane_masks()
    lane = lax.broadcasted_iota(jnp.int32, (RB, PAIR), 1)
    ones_lane = jnp.where(lane == 0, 1.0, 0.0).astype(bf16)
    eye = lax.broadcasted_iota(jnp.int32, (RB, RB), 0) == lax.broadcasted_iota(jnp.int32, (RB, RB), 1)
    col = lax.broadcasted_iota(jnp.int32, (1, RB), 1)
    blocks = tokens // RB

    def one_pair(pair, carry):
        slot = lax.rem(pair, 2)
        cols = pl.ds(pl.multiple_of(pair * PAIR, PAIR), PAIR)

        @pl.when(pair >= 2)
        def _():
            probs_copy(m, layer, pair - 2, slot, True).wait()

        keys = m.k[layer, :, cols]
        keys_wide = jnp.concatenate([keys, m.key_bias[...]], axis=1)
        values = m.v[layer, :, cols]
        mixed = []
        for head in range(2):
            for block in range(blocks):
                rows = slice(block * RB, (block + 1) * RB)
                query = m.q[layer, rows, cols] * masks[head]
                query_wide = jnp.concatenate([query, ones_lane], axis=1)
                parts = []
                for other in range(blocks):
                    keys_rows = slice(other * RB, (other + 1) * RB)
                    if other == block:
                        part = dot_nt(query, keys[keys_rows])
                        hidden = jnp.where(col + block * RB >= known, NEG, 0.0)
                        part = jnp.where(eye, part, part + hidden)
                    else:
                        part = dot_nt(query_wide, keys_wide[keys_rows])
                    parts.append(part)
                scores = jnp.concatenate(parts, axis=1)
                peak = jnp.max(scores, axis=1, keepdims=True)
                m.probs[slot, head, rows, :] = jnp.exp2(scores - peak).astype(bf16)
            values_wide = values * masks[head] + masks[1 - head]
            mixed.append(dot(m.probs[slot, head], values_wide))
        probs_copy(m, layer, pair, slot, True).start()
        low = lax.broadcasted_iota(jnp.int32, (tokens, PAIR), 1) < 64
        raw = jnp.where(low, mixed[0], mixed[1])
        total = pltpu.roll(jnp.where(low, mixed[1], mixed[0]), 64, 1)
        inverse = 1.0 / total
        m.inv_total[layer, :, cols] = inverse
        m.o[layer, :, cols] = (raw * inverse).astype(bf16)
        return carry

    lax.fori_loop(0, pairs, one_pair, 0)
    for pair in (pairs - 2, pairs - 1):
        probs_copy(m, layer, pair, pair % 2, True).wait()


def feed_forward(m, layer, x_of, y_to):
    tokens = m.q.shape[1]

    def block(index, carry):
        rows = pl.ds(pl.multiple_of(index * RB, RB), RB)
        branch = dot(m.o[layer, rows, :], m.w[layer, 3]) + m.vec(layer, 2)
        normed, inverse = normalize(x_of(rows) + branch)
        m.n1[layer, rows, :] = normed.astype(bf16)
        m.inv1[layer, rows, :] = inverse
        first = normed * m.vec(layer, 5) + m.vec(layer, 6)
        pre = dot(first.astype(bf16), m.w[layer, 4]) + m.vec(layer, 3)
        hidden, slope = gelu_parts(pre)
        low = hidden.astype(bf16)
        m.r[layer, rows, :] = low
        m.slope[layer, rows, :] = slope.astype(bf16)
        feed = dot(low, m.w[layer, 5]) + m.vec(layer, 4)
        normed, inverse = normalize(first + feed)
        m.n2[layer, rows, :] = normed.astype(bf16)
        m.inv2[layer, rows, :] = inverse
        y_to(rows, normed * m.vec(layer, 7) + m.vec(layer, 8))
        return carry

    lax.fori_loop(0, tokens // RB, block, 0)


def column_sum(value):
    rows, width = value.shape
    return jnp.sum(value.reshape(rows // 8, 8, width), axis=0)


def rows_back(m, layer):
    tokens = m.q.shape[1]
    for row in range(8):
        m.sums[row] = jnp.zeros_like(m.sums[row])

    def block(index, carry):
        rows = pl.ds(pl.multiple_of(index * RB, RB), RB)
        grad = m.g[rows, :]
        normed = m.n2[layer, rows, :].astype(f32)
        m.sums[0] += column_sum(grad * normed)
        m.sums[1] += column_sum(grad)
        back = norm_back(grad, normed, m.inv2[layer, rows, :], m.vec(layer, 7))
        m.sums[2] += column_sum(back)
        low = back.astype(bf16)
        m.df[rows, :] = low
        pre = dot_nt(low, m.w[layer, 5]) * m.slope[layer, rows, :].astype(f32)
        m.sums[3] += column_sum(pre)
        low = pre.astype(bf16)
        m.du[rows, :] = low
        grad = back + dot_nt(low, m.w[layer, 4])
        normed = m.n1[layer, rows, :].astype(f32)
        m.sums[4] += column_sum(grad * normed)
        m.sums[5] += column_sum(grad)
        back = norm_back(grad, normed, m.inv1[layer, rows, :], m.vec(layer, 5))
        m.sums[6] += column_sum(back)
        m.g[rows, :] = back
        low = back.astype(bf16)
        m.da[rows, :] = low
        m.do[rows, :] = (dot_nt(low, m.w[layer, 3]) * m.inv_total[layer, rows, :]).astype(bf16)
        first = normed * m.vec(layer, 5) + m.vec(layer, 6)
        m.x1b[rows, :] = first.astype(bf16)
        return carry

    lax.fori_loop(0, tokens // RB, block, 0)
    for row, place in ((0, 7), (1, 8), (2, 4), (3, 3), (4, 5), (5, 6), (6, 2)):
        m.grad_vec(layer, place, jnp.sum(m.sums[row], axis=0, keepdims=True))
    m.grad_mat(layer, 5, dot_tn(m.r[layer], m.df[...]))
    m.grad_mat(layer, 4, dot_tn(m.x1b[...], m.du[...]))
    m.grad_mat(layer, 3, dot_tn(m.o[layer], m.da[...]))


def attend_back(m, layer):
    tokens, width = m.q.shape[1:]
    pairs = width // PAIR
    masks = lane_masks()
    blocks = tokens // RB
    probs_copy(m, layer, 0, 0, False).start()

    def one_pair(pair, carry):
        slot = lax.rem(pair, 2)
        cols = pl.ds(pl.multiple_of(pair * PAIR, PAIR), PAIR)
        probs_copy(m, layer, pair, slot, False).wait()

        @pl.when(pair + 1 < pairs)
        def _():
            probs_copy(m, layer, pair + 1, 1 - slot, False).start()

        grad = m.do[:, cols]
        turned = pltpu.roll(grad.astype(f32) * m.o[layer, :, cols].astype(f32), 64, 1).astype(bf16)
        values = m.v[layer, :, cols]
        keys = m.k[layer, :, cols]
        query_turned = m.q[layer, :, cols].T
        grad_turned = grad.T
        grad_query, grad_keys, grad_values = [], [], []
        for head in range(2):
            part = slice(head * 64, (head + 1) * 64)
            wide = grad * masks[head] - turned * masks[1 - head]
            values_wide = values * masks[head] + masks[1 - head]
            for block in range(blocks):
                rows = slice(block * RB, (block + 1) * RB)
                score = dot_nt(wide[rows], values_wide)
                m.ds[head, rows, :] = score.astype(bf16) * m.probs[slot, head, rows, :]
            grad_values.append(dot(grad_turned[part], m.probs[slot, head]))
            grad_keys.append(dot(query_turned[part], m.ds[head]))
            grad_query.append(dot(m.ds[head], keys))
        low = lax.broadcasted_iota(jnp.int32, (tokens, PAIR), 1) < 64
        m.q[layer, :, cols] = (jnp.where(low, grad_query[0], grad_query[1]) * 0.125).astype(bf16)
        m.k[layer, :, cols] = (jnp.concatenate(grad_keys, axis=0) * LN2).astype(bf16).T
        m.v[layer, :, cols] = jnp.concatenate(grad_values, axis=0).astype(bf16).T
        return carry

    lax.fori_loop(0, pairs, one_pair, 0)


def project_back(m, layer, xb):
    tokens = m.q.shape[1]
    ones = jnp.ones((8, tokens), bf16)
    m.grad_vec(layer, 0, dot(ones, m.q[layer])[0:1])
    m.grad_vec(layer, 1, dot(ones, m.v[layer])[0:1])
    m.grad_mat(layer, 0, dot_tn(xb[...], m.q[layer]))
    m.grad_mat(layer, 1, dot_tn(xb[...], m.k[layer]))
    m.grad_mat(layer, 2, dot_tn(xb[...], m.v[layer]))

    def block(index, carry):
        rows = pl.ds(pl.multiple_of(index * RB, RB), RB)
        m.g[rows, :] = (
            m.g[rows, :]
            + dot_nt(m.q[layer, rows, :], m.w[layer, 0])
            + dot_nt(m.k[layer, rows, :], m.w[layer, 1])
            + dot_nt(m.v[layer, rows, :], m.w[layer, 2])
        )
        return carry

    lax.fori_loop(0, tokens // RB, block, 0)


def kernel(length_ref, class_ref, x_ref, cot_ref, w_ref, vec_ref, act_ref, dx_ref, mats_ref, vecs_ref, probs_hbm,
           q, k, v, o, inv_total, n1, n2, inv1, inv2, r, slope, g, x1, df, du, da, do, x1b, sums, key_bias,
           probs, ds, probs_sem, out_sem):
    m = Refs()
    m.w, m.q, m.k, m.v, m.o, m.inv_total = w_ref, q, k, v, o, inv_total
    m.n1, m.n2, m.inv1, m.inv2, m.r, m.slope, m.g = n1, n2, inv1, inv2, r, slope, g
    m.df, m.du, m.da, m.do, m.x1b, m.sums, m.key_bias = df, du, da, do, x1b, sums, key_bias
    m.probs, m.ds, m.probs_hbm, m.probs_sem = probs, ds, probs_hbm, probs_sem
    m.vec = lambda layer, place: vec_ref[layer, place : place + 1, :]

    def grad_mat(layer, place, value):
        mats_ref[layer, place] = value.astype(bf16)

    def grad_vec(layer, place, value):
        vecs_ref[layer, place : place + 1, :] = value

    m.grad_mat, m.grad_vec = grad_mat, grad_vec
    length, klass = length_ref[0], class_ref[0]
    known = jnp.where(klass == 0, length, (length + 1) // 2)
    tokens = x_ref.shape[0]
    fill_bias(m, known)
    project(m, 0, x_ref)
    attend(m, 0, known)

    def keep_next(rows, value):
        g[rows, :] = value
        x1[rows, :] = value.astype(bf16)

    feed_forward(m, 0, lambda rows: x_ref[rows, :].astype(f32), keep_next)
    project(m, 1, x1)
    attend(m, 1, known)

    def finish(rows, value):
        start = rows.start
        valid = lax.broadcasted_iota(jnp.int32, (RB, 1), 0) + start < length
        act_ref[rows, :] = jnp.where(valid, value, 0.0).astype(bf16)
        g[rows, :] = jnp.where(valid, cot_ref[rows, :].astype(f32), 0.0)

    feed_forward(m, 1, lambda rows: g[rows, :], finish)
    for layer, xb in ((1, x1), (0, x_ref)):
        rows_back(m, layer)
        attend_back(m, layer)
        project_back(m, layer, xb)
    copy = pltpu.make_async_copy(g, dx_ref, out_sem)
    copy.start()
    copy.wait()


def cell_pass(lengths, classes, tokens, cotangent, mats, vecs):
    count, width = tokens.shape
    layers = mats.shape[0]
    pairs = width // PAIR
    vmem = pl.BlockSpec(memory_space=pltpu.VMEM)
    smem = pl.BlockSpec(memory_space=pltpu.SMEM)
    hbm = pl.BlockSpec(memory_space=pl.ANY)
    both = (layers, count, width)
    one = (count, width)
    scratch = [
        pltpu.VMEM(both, bf16), pltpu.VMEM(both, bf16), pltpu.VMEM(both, bf16), pltpu.VMEM(both, bf16),
        pltpu.VMEM(both, f32),
        pltpu.VMEM(both, bf16), pltpu.VMEM(both, bf16),
        pltpu.VMEM((layers, count, 1), f32), pltpu.VMEM((layers, count, 1), f32),
        pltpu.VMEM(both, bf16), pltpu.VMEM(both, bf16),
        pltpu.VMEM(one, f32), pltpu.VMEM(one, bf16),
        pltpu.VMEM(one, bf16), pltpu.VMEM(one, bf16), pltpu.VMEM(one, bf16), pltpu.VMEM(one, bf16), pltpu.VMEM(one, bf16),
        pltpu.VMEM((8, 8, width), f32),
        pltpu.VMEM((count, PAIR), bf16),
        pltpu.VMEM((2, 2, count, count), bf16),
        pltpu.VMEM((2, count, count), bf16),
        pltpu.SemaphoreType.DMA((2,)),
        pltpu.SemaphoreType.DMA,
    ]
    outs = pl.pallas_call(
        kernel,
        out_shape=[
            jax.ShapeDtypeStruct(one, bf16),
            jax.ShapeDtypeStruct(one, f32),
            jax.ShapeDtypeStruct(mats.shape, bf16),
            jax.ShapeDtypeStruct((layers, 16, width), f32),
            jax.ShapeDtypeStruct((layers, pairs, 2, count, count), bf16),
        ],
        in_specs=[smem, smem, vmem, vmem, vmem, vmem],
        out_specs=[vmem, hbm, vmem, vmem, hbm],
        scratch_shapes=scratch,
        compiler_params=pltpu.CompilerParams(vmem_limit_bytes=67043328),
    )(lengths, classes, tokens, cotangent, mats, vecs)
    return outs[:4]


def adam_update(param, grad, first, second, rate):
    first_new = beta_first * first + (1.0 - beta_first) * grad
    second_new = beta_second * second + (1.0 - beta_second) * grad * grad
    first_hat = first_new / (1.0 - beta_first**adam_step)
    second_hat = second_new / (1.0 - beta_second**adam_step)
    param_new = param - rate * (first_hat / (jnp.sqrt(second_hat) + adam_eps) + decay_rate * param)
    return (param_new, first_new, second_new)


def body(
    cell_tokens,
    lengths,
    classes,
    cotangent,
    weights,
    vectors,
    first_weights,
    second_weights,
    first_vectors,
    second_vectors,
):
    cell_count, token_count, model_width = cell_tokens.shape
    mats = lax.all_gather(weights.astype(bf16), "shard", axis=2, tiled=True)
    vecs = lax.all_gather(vectors.astype(bf16), "shard", axis=2, tiled=True).astype(f32)
    vecs = jnp.pad(vecs, ((0, 0), (0, 16 - vecs.shape[1]), (0, 0)))
    activations, input_grad, grad_mats, grad_vecs = cell_pass(
        lengths, classes, cell_tokens[0], cotangent[0], mats, vecs
    )
    grad_vecs = grad_vecs[:, : vectors.shape[1]]
    total_mats = lax.psum_scatter(grad_mats, "shard", scatter_dimension=2, tiled=True)
    total_vecs = lax.psum_scatter(grad_vecs.astype(bf16), "shard", scatter_dimension=2, tiled=True)
    total_mats = lax.psum(total_mats, "dp").astype(f32)
    total_vecs = lax.psum(total_vecs, "dp").astype(f32)
    new_weights, new_first_weights, new_second_weights = adam_update(
        weights, total_mats, first_weights, second_weights, learn_rate
    )
    new_vectors, new_first_vectors, new_second_vectors = adam_update(
        vectors, total_vecs, first_vectors, second_vectors, vector_rate
    )
    return (
        activations[None],
        input_grad[None],
        new_weights,
        new_weights.astype(bf16),
        new_first_weights,
        new_second_weights,
        new_vectors,
        new_first_vectors,
        new_second_vectors,
        total_vecs[:, 0],
    )


def solution(mesh):
    in_specs = (
        P(("dp", "shard"), None, None),
        P(("dp", "shard")),
        P(("dp", "shard")),
        P(("dp", "shard"), None, None),
        P(None, None, "shard", None),
        P(None, None, "shard"),
        P(None, None, "shard", None),
        P(None, None, "shard", None),
        P(None, None, "shard"),
        P(None, None, "shard"),
    )
    out_specs = (
        P(("dp", "shard"), None, None),
        P(("dp", "shard"), None, None),
        P(None, None, "shard", None),
        P(None, None, "shard", None),
        P(None, None, "shard", None),
        P(None, None, "shard", None),
        P(None, None, "shard"),
        P(None, None, "shard"),
        P(None, None, "shard"),
        P(None, "shard"),
    )
    return jax.shard_map(body, mesh=mesh, in_specs=in_specs, out_specs=out_specs, check_vma=False)
```

```python
import functools
import math

import jax
import jax.numpy as jnp
from jax import lax
from jax.experimental import pallas as pl
from jax.experimental.pallas import tpu as pltpu
from jax.sharding import PartitionSpec as P

HEADS = 8
beta_first = 0.5
beta_second = 0.55
learn_rate = 0.05
vector_rate = 0.25
decay_rate = 0.01
adam_eps = 1e-08
adam_step = 3.0
norm_eps = 1e-05

LOG2E = 1.4426950408889634
LN2 = 0.6931471805599453
NEG = -1e30
f32 = jnp.float32
bf16 = jnp.bfloat16
PAIR = 128
RB = 256


def dot(left, right):
    return jnp.dot(left, right, preferred_element_type=f32)


def dot_nt(left, right):
    return lax.dot_general(left, right, (((1,), (1,)), ((), ())), preferred_element_type=f32)


def dot_tn(left, right):
    return lax.dot_general(left, right, (((0,), (0,)), ((), ())), preferred_element_type=f32)


def gelu_parts(value):
    size = jnp.abs(value) * (1.0 / math.sqrt(2.0))
    step = 1.0 / (1.0 + 0.3275911 * size)
    bell = jnp.exp2(value * value * (-0.5 * LOG2E))
    poly = step * (0.254829592 + step * (-0.284496736 + step * (1.421413741 + step * (-1.453152027 + step * 1.061405429))))
    tail = 0.5 * poly * bell
    below = jnp.where(value < 0.0, tail, 1.0 - tail)
    return value * below, below + value * bell * (1.0 / math.sqrt(2.0 * math.pi))


def normalize(value):
    center = jnp.mean(value, axis=-1, keepdims=True)
    centered = value - center
    spread = jnp.mean(centered * centered, axis=-1, keepdims=True)
    inverse = lax.rsqrt(spread + norm_eps)
    return centered * inverse, inverse


def norm_back(grad, normed, inverse, gain):
    scaled = grad * gain
    return inverse * (
        scaled
        - jnp.mean(scaled, axis=-1, keepdims=True)
        - normed * jnp.mean(scaled * normed, axis=-1, keepdims=True)
    )


def lane_masks(rows=1):
    lane = lax.broadcasted_iota(jnp.int32, (rows, PAIR), 1)
    low = jnp.where(lane < 64, 1.0, 0.0)
    return low.astype(bf16), (1.0 - low).astype(bf16)


class Refs:
    pass


def fill_bias(m, known):
    tokens = m.key_bias.shape[0]
    row = lax.broadcasted_iota(jnp.int32, (tokens, PAIR), 0)
    lane = lax.broadcasted_iota(jnp.int32, (tokens, PAIR), 1)
    m.key_bias[...] = jnp.where((lane == 0) & (row >= known), NEG, 0.0).astype(bf16)


def project(m, layer, xb):
    tokens = xb.shape[0]
    scale = LOG2E / 8.0

    def block(index, carry):
        rows = pl.ds(pl.multiple_of(index * 2 * RB, 2 * RB), 2 * RB)
        low = xb[rows, :]
        m.q[layer, rows, :] = ((dot(low, m.mat(layer, 0)) + m.vec(layer, 0)) * scale).astype(bf16)
        m.k[layer, rows, :] = dot(low, m.mat(layer, 1)).astype(bf16)
        m.v[layer, rows, :] = (dot(low, m.mat(layer, 2)) + m.vec(layer, 1)).astype(bf16)
        return carry

    lax.fori_loop(0, tokens // (2 * RB), block, 0)


def probs_copy(m, layer, pair, slot, out):
    here, there = m.probs.at[slot], m.probs_hbm.at[layer, pair]
    if out:
        return pltpu.make_async_copy(here, there, m.probs_sem.at[slot])
    return pltpu.make_async_copy(there, here, m.probs_sem.at[slot])


def attend(m, layer, known, hook=None):
    tokens, width = m.q.shape[1:]
    pairs = width // PAIR
    masks = lane_masks()
    lane = lax.broadcasted_iota(jnp.int32, (RB, PAIR), 1)
    ones_lane = jnp.where(lane == 0, 1.0, 0.0).astype(bf16)
    eye = lax.broadcasted_iota(jnp.int32, (RB, RB), 0) == lax.broadcasted_iota(jnp.int32, (RB, RB), 1)
    col = lax.broadcasted_iota(jnp.int32, (1, RB), 1)
    blocks = tokens // RB

    def one_pair(pair, carry):
        if hook is not None:
            hook(pair)
        slot = lax.rem(pair, 2)
        cols = pl.ds(pl.multiple_of(pair * PAIR, PAIR), PAIR)

        @pl.when(pair >= 2)
        def _():
            probs_copy(m, layer, pair - 2, slot, True).wait()

        keys = m.k[layer, :, cols]
        keys_wide = jnp.concatenate([keys, m.key_bias[...]], axis=1)
        values = m.v[layer, :, cols]
        mixed = []
        for head in range(2):
            for block in range(blocks):
                rows = slice(block * RB, (block + 1) * RB)
                query = m.q[layer, rows, cols] * masks[head]
                query_wide = jnp.concatenate([query, ones_lane], axis=1)
                parts = []
                for other in range(blocks):
                    keys_rows = slice(other * RB, (other + 1) * RB)
                    if other == block:
                        part = dot_nt(query, keys[keys_rows])
                        hidden = jnp.where(col + block * RB >= known, NEG, 0.0)
                        part = jnp.where(eye, part, part + hidden)
                    else:
                        part = dot_nt(query_wide, keys_wide[keys_rows])
                    parts.append(part)
                scores = jnp.concatenate(parts, axis=1)
                peak = jnp.max(scores, axis=1, keepdims=True)
                m.probs[slot, head, rows, :] = jnp.exp2(scores - peak).astype(bf16)
            values_wide = values * masks[head] + masks[1 - head]
            mixed.append(dot(m.probs[slot, head], values_wide))
        probs_copy(m, layer, pair, slot, True).start()
        low = lax.broadcasted_iota(jnp.int32, (tokens, PAIR), 1) < 64
        raw = jnp.where(low, mixed[0], mixed[1])
        total = pltpu.roll(jnp.where(low, mixed[1], mixed[0]), 64, 1)
        inverse = 1.0 / total
        m.inv_total[layer, :, cols] = inverse.astype(bf16)
        mean = raw * inverse
        high = mean.astype(bf16)
        m.o[layer, :, cols] = high
        m.o_low[layer, :, cols] = (mean - high.astype(f32)).astype(bf16)
        return carry

    lax.fori_loop(0, pairs, one_pair, 0)
    for pair in (pairs - 2, pairs - 1):
        probs_copy(m, layer, pair, pair % 2, True).wait()


def feed_forward(m, layer, x_of, y_to):
    tokens = m.q.shape[1]

    def block(index, carry):
        rows = pl.ds(pl.multiple_of(index * RB, RB), RB)
        branch = dot(m.o[layer, rows, :], m.mat(layer, 3)) + m.vec(layer, 2)
        normed, inverse = normalize(x_of(rows) + branch)
        m.n1[layer, rows, :] = normed.astype(bf16)
        m.inv[rows, 2 * layer : 2 * layer + 1] = inverse
        first = normed * m.vec(layer, 5) + m.vec(layer, 6)
        pre = dot(first.astype(bf16), m.mat(layer, 4)) + m.vec(layer, 3)
        hidden, slope = gelu_parts(pre)
        low = hidden.astype(bf16)
        m.r[layer, rows, :] = low
        m.slope[layer, rows, :] = slope.astype(bf16)
        feed = dot(low, m.mat(layer, 5)) + m.vec(layer, 4)
        normed, inverse = normalize(first + feed)
        m.n2[layer, rows, :] = normed.astype(bf16)
        m.inv[rows, 2 * layer + 1 : 2 * layer + 2] = inverse
        y_to(rows, normed * m.vec(layer, 7) + m.vec(layer, 8))
        return carry

    lax.fori_loop(0, tokens // RB, block, 0)


def column_sum(value):
    rows, width = value.shape
    return jnp.sum(value.reshape(rows // 8, 8, width), axis=0)


def rows_back(m, layer, hook=None, ready=None):
    tokens = m.q.shape[1]
    for row in range(8):
        m.sums[row] = jnp.zeros_like(m.sums[row])

    def block(index, carry):
        if hook is not None:
            hook(index)
        rows = pl.ds(pl.multiple_of(index * RB, RB), RB)
        grad = m.g[rows, :]
        normed = m.n2[layer, rows, :].astype(f32)
        m.sums[0] += column_sum(grad * normed)
        m.sums[1] += column_sum(grad)
        back = norm_back(grad, normed, m.inv[rows, 2 * layer + 1 : 2 * layer + 2], m.vec(layer, 7))
        m.sums[2] += column_sum(back)
        low = back.astype(bf16)
        m.n2[layer, rows, :] = low
        pre = dot_nt(low, m.mat(layer, 5)) * m.slope[layer, rows, :].astype(f32)
        m.sums[3] += column_sum(pre)
        low = pre.astype(bf16)
        m.du[rows, :] = low
        grad = back + dot_nt(low, m.mat(layer, 4))
        normed = m.n1[layer, rows, :].astype(f32)
        m.sums[4] += column_sum(grad * normed)
        m.sums[5] += column_sum(grad)
        back = norm_back(grad, normed, m.inv[rows, 2 * layer : 2 * layer + 1], m.vec(layer, 5))
        m.sums[6] += column_sum(back)
        m.g[rows, :] = back
        low = back.astype(bf16)
        m.n1[layer, rows, :] = low
        m.inv_total[layer, rows, :] = (dot_nt(low, m.mat(layer, 3)) * m.inv_total[layer, rows, :].astype(f32)).astype(bf16)
        first = normed * m.vec(layer, 5) + m.vec(layer, 6)
        m.slope[layer, rows, :] = first.astype(bf16)
        return carry

    lax.fori_loop(0, tokens // RB, block, 0)
    for row, place in ((0, 7), (1, 8), (2, 4), (3, 3), (4, 5), (5, 6), (6, 2)):
        m.grad_vec(layer, place, jnp.sum(m.sums[row], axis=0, keepdims=True))
    if ready is not None:
        ready()
    m.grad_mat(layer, 5, dot_tn(m.r[layer], m.n2[layer]))
    m.grad_mat(layer, 4, dot_tn(m.slope[layer], m.du[...]))
    m.grad_mat(layer, 3, dot_tn(m.o[layer], m.n1[layer]))


def attend_back(m, layer, hook=None):
    tokens, width = m.q.shape[1:]
    pairs = width // PAIR
    masks = lane_masks()
    blocks = tokens // RB

    def one_pair(pair, carry):
        if hook is not None:
            hook(pair)
        slot = lax.rem(pair, 2)
        cols = pl.ds(pl.multiple_of(pair * PAIR, PAIR), PAIR)
        probs_copy(m, layer, pair, slot, False).wait()

        @pl.when(pair + 1 < pairs)
        def _():
            probs_copy(m, layer, pair + 1, 1 - slot, False).start()

        grad = m.inv_total[layer, :, cols]
        turned = pltpu.roll(
            grad.astype(f32) * (m.o[layer, :, cols].astype(f32) + m.o_low[layer, :, cols].astype(f32)), 64, 1
        )
        turned_high = turned.astype(bf16)
        turned_low = (turned - turned_high.astype(f32)).astype(bf16)
        values = m.v[layer, :, cols]
        keys = m.k[layer, :, cols]
        query_turned = m.q[layer, :, cols].T
        grad_turned = grad.T
        grad_query, grad_keys, grad_values = [], [], []
        for head in range(2):
            part = slice(head * 64, (head + 1) * 64)
            wide = jnp.concatenate(
                [grad * masks[head] - turned_high * masks[1 - head], -turned_low * masks[1 - head]], axis=1
            )
            values_wide = jnp.concatenate(
                [values * masks[head] + masks[1 - head], jnp.broadcast_to(masks[1 - head], values.shape)], axis=1
            )
            grad_values.append(dot(grad_turned[part], m.probs[slot, head]))
            for block in range(blocks):
                rows = slice(block * RB, (block + 1) * RB)
                score = dot_nt(wide[rows], values_wide)
                m.probs[slot, head, rows, :] = (score * m.probs[slot, head, rows, :].astype(f32)).astype(bf16)
            grad_keys.append(dot(query_turned[part], m.probs[slot, head]))
            grad_query.append(dot(m.probs[slot, head], keys))
        low = lax.broadcasted_iota(jnp.int32, (tokens, PAIR), 1) < 64
        m.q[layer, :, cols] = (jnp.where(low, grad_query[0], grad_query[1]) * 0.125).astype(bf16)
        m.k[layer, :, cols] = (jnp.concatenate(grad_keys, axis=0) * LN2).astype(bf16).T
        m.v[layer, :, cols] = jnp.concatenate(grad_values, axis=0).astype(bf16).T
        return carry

    lax.fori_loop(0, pairs, one_pair, 0)


def project_back(m, layer, xb, ready=None):
    tokens = m.q.shape[1]
    ones = jnp.ones((8, tokens), bf16)
    m.grad_vec(layer, 0, dot(ones, m.q[layer])[0:1])
    m.grad_vec(layer, 1, dot(ones, m.v[layer])[0:1])
    m.grad_mat(layer, 0, dot_tn(xb[...], m.q[layer]))
    m.grad_mat(layer, 1, dot_tn(xb[...], m.k[layer]))
    m.grad_mat(layer, 2, dot_tn(xb[...], m.v[layer]))
    if ready is not None:
        ready()

    def block(index, carry):
        rows = pl.ds(pl.multiple_of(index * RB, RB), RB)
        m.g[rows, :] = (
            m.g[rows, :]
            + dot_nt(m.q[layer, rows, :], m.mat(layer, 0))
            + dot_nt(m.k[layer, rows, :], m.mat(layer, 1))
            + dot_nt(m.v[layer, rows, :], m.mat(layer, 2))
        )
        return carry

    lax.fori_loop(0, tokens // RB, block, 0)


def start_refs(q, k, v, o, o_low, inv_total, n1, n2, inv, r, slope, g, x1, du, sums, key_bias,
               probs, probs_sem, probs_hbm):
    m = Refs()
    m.q, m.k, m.v, m.o, m.o_low, m.inv_total = q, k, v, o, o_low, inv_total
    m.n1, m.n2, m.inv, m.r, m.slope, m.g, m.x1 = n1, n2, inv, r, slope, g, x1
    m.du, m.sums, m.key_bias = du, sums, key_bias
    m.probs, m.probs_sem, m.probs_hbm = probs, probs_sem, probs_hbm
    return m


def shared_scratch(layers, count, width):
    both = (layers, count, width)
    one = (count, width)
    return [
        pltpu.VMEM(both, bf16), pltpu.VMEM(both, bf16), pltpu.VMEM(both, bf16), pltpu.VMEM(both, bf16),
        pltpu.VMEM(both, bf16), pltpu.VMEM(both, bf16), pltpu.VMEM(both, bf16), pltpu.VMEM(both, bf16),
        pltpu.VMEM((count, 2 * layers), f32),
        pltpu.VMEM(both, bf16), pltpu.VMEM(both, bf16),
        pltpu.VMEM(one, f32), pltpu.VMEM(one, bf16),
        pltpu.VMEM(one, bf16),
        pltpu.VMEM((8, 8, width), f32),
        pltpu.VMEM((count, PAIR), bf16),
        pltpu.VMEM((2, 2, count, count), bf16),
        pltpu.SemaphoreType.DMA((2,)),
    ]


SHARED = 18


def plain_kernel(length_ref, class_ref, x_ref, cot_ref, w_ref, vec_ref, act_ref, dx_ref, mats_ref, vecs_ref, probs_hbm, *rest):
    m = start_refs(*rest[:SHARED], probs_hbm)
    out_sem = rest[SHARED]
    m.mat = lambda layer, place: w_ref[layer, place]
    m.vec = lambda layer, place: vec_ref[layer, place : place + 1, :]

    def grad_mat(layer, place, value):
        mats_ref[layer, place] = value.astype(bf16)

    def grad_vec(layer, place, value):
        vecs_ref[layer, place : place + 1, :] = value

    m.grad_mat, m.grad_vec = grad_mat, grad_vec
    length, klass = length_ref[0], class_ref[0]
    known = jnp.where(klass == 0, length, (length + 1) // 2)
    fill_bias(m, known)
    project(m, 0, x_ref)
    attend(m, 0, known)

    def keep_next(rows, value):
        m.g[rows, :] = value
        m.x1[rows, :] = value.astype(bf16)

    feed_forward(m, 0, lambda rows: x_ref[rows, :].astype(f32), keep_next)
    project(m, 1, m.x1)
    attend(m, 1, known)
    probs_copy(m, 1, 0, 0, False).start()

    def finish(rows, value):
        valid = lax.broadcasted_iota(jnp.int32, (RB, 1), 0) + rows.start < length
        act_ref[rows, :] = jnp.where(valid, value, 0.0).astype(bf16)
        m.g[rows, :] = jnp.where(valid, cot_ref[rows, :].astype(f32), 0.0)

    feed_forward(m, 1, lambda rows: m.g[rows, :], finish)
    for layer, xb in ((1, m.x1), (0, x_ref)):
        rows_back(m, layer)
        attend_back(m, layer)
        if layer:
            probs_copy(m, layer - 1, 0, 0, False).start()
        project_back(m, layer, xb)
    copy = pltpu.make_async_copy(m.g, dx_ref, out_sem)
    copy.start()
    copy.wait()


def plain_pass(lengths, classes, tokens, cotangent, mats, vecs):
    count, width = tokens.shape
    layers = mats.shape[0]
    vmem = pl.BlockSpec(memory_space=pltpu.VMEM)
    smem = pl.BlockSpec(memory_space=pltpu.SMEM)
    hbm = pl.BlockSpec(memory_space=pl.ANY)
    outs = pl.pallas_call(
        plain_kernel,
        out_shape=[
            jax.ShapeDtypeStruct((count, width), bf16),
            jax.ShapeDtypeStruct((count, width), f32),
            jax.ShapeDtypeStruct(mats.shape, bf16),
            jax.ShapeDtypeStruct((layers, 16, width), f32),
            jax.ShapeDtypeStruct((layers, width // PAIR, 2, count, count), bf16),
        ],
        in_specs=[smem, smem, vmem, vmem, vmem, vmem],
        out_specs=[vmem, hbm, vmem, vmem, hbm],
        scratch_shapes=shared_scratch(layers, count, width) + [pltpu.SemaphoreType.DMA],
        compiler_params=pltpu.CompilerParams(vmem_limit_bytes=67043328),
    )(lengths, classes, tokens, cotangent, mats, vecs)
    return outs[:4]


def adam_update(param, grad, first, second, rate):
    first_new = beta_first * first + (1.0 - beta_first) * grad
    second_new = beta_second * second + (1.0 - beta_second) * grad * grad
    first_hat = first_new / (1.0 - beta_first**adam_step)
    second_hat = second_new / (1.0 - beta_second**adam_step)
    param_new = param - rate * (first_hat / (jnp.sqrt(second_hat) + adam_eps) + decay_rate * param)
    return (param_new, first_new, second_new)


def plain_body(tokens, lengths, classes, cotangent, weights, vectors, first_weights, second_weights, first_vectors, second_vectors):
    mats = lax.all_gather(weights.astype(bf16), "shard", axis=2, tiled=True)
    vecs = lax.all_gather(vectors.astype(bf16), "shard", axis=2, tiled=True).astype(f32)
    vecs = jnp.pad(vecs, ((0, 0), (0, 16 - vecs.shape[1]), (0, 0)))
    activations, input_grad, grad_mats, grad_vecs = plain_pass(lengths, classes, tokens[0], cotangent[0], mats, vecs)
    grad_vecs = grad_vecs[:, : vectors.shape[1]]
    total_mats = lax.psum_scatter(grad_mats, "shard", scatter_dimension=2, tiled=True)
    total_vecs = lax.psum_scatter(grad_vecs.astype(bf16), "shard", scatter_dimension=2, tiled=True)
    total_mats = lax.psum(total_mats, "dp").astype(f32)
    total_vecs = lax.psum(total_vecs, "dp").astype(f32)
    new_weights, new_first_weights, new_second_weights = adam_update(
        weights, total_mats, first_weights, second_weights, learn_rate
    )
    new_vectors, new_first_vectors, new_second_vectors = adam_update(
        vectors, total_vecs, first_vectors, second_vectors, vector_rate
    )
    return (
        activations[None], input_grad[None], new_weights, new_weights.astype(bf16), new_first_weights, new_second_weights,
        new_vectors, new_first_vectors, new_second_vectors, total_vecs[:, 0],
    )


MESH = pl.DeviceIdType.MESH


def remote(src, dst, sems, place, device):
    return pltpu.make_async_remote_copy(
        src_ref=src, dst_ref=dst, send_sem=sems[0].at[place], recv_sem=sems[1].at[place], device_id=device, device_id_type=MESH
    )


class Spot:
    def __init__(self, planes, shards):
        self.planes, self.shards = planes, shards
        self.d, self.z = lax.axis_index("dp"), lax.axis_index("shard")
        self.c, self.t = lax.rem(self.d, 2), lax.div(self.d, 2)

    def plane(self, step):
        return lax.rem(self.t + step, self.planes)

    def shard(self, step):
        return lax.rem(self.z + step, self.shards)

    def sibling(self):
        return (self.t * 2 + 1 - self.c, self.z)


class Weights:
    def __init__(self, spot, w, layer, first, index, z_sems, p_sems, c_sems):
        self.spot, self.index = spot, index
        self.z_sems, self.p_sems, self.c_sems = z_sems, p_sems, c_sems
        self.view = w.at[layer, first : first + 3]

    def z_copy(self, step):
        s = self.spot
        piece = self.view.at[:, s.z, s.t, s.c]
        return remote(piece, piece, self.z_sems, (self.index, step - 1), (s.d, s.shard(step)))

    def p_copy(self, z_step, t_step):
        s = self.spot
        piece = self.view.at[:, s.shard(s.shards - z_step), s.t, s.c]
        place = (self.index, z_step - 1, t_step - 1)
        return remote(piece, piece, self.p_sems, place, (s.plane(t_step) * 2 + s.c, s.z))

    def c_copy(self, z_step):
        s = self.spot
        piece = self.view.at[:, s.shard(s.shards - z_step), :, s.c]
        return remote(piece, piece, self.c_sems, (self.index, z_step - 1), s.sibling())

    def steps(self):
        return range(1, self.spot.shards)

    def send_z(self):
        for step in self.steps():
            self.z_copy(step).start()

    def send_p(self):
        for step in self.steps():
            self.z_copy(step).wait_recv()
            for other in range(1, self.spot.planes):
                self.p_copy(step, other).start()

    def send_c(self):
        for step in self.steps():
            for other in range(1, self.spot.planes):
                self.p_copy(step, other).wait_recv()
            self.c_copy(step).start()

    def arrive(self):
        for step in self.steps():
            self.c_copy(step).wait_recv()

    def close(self):
        for step in self.steps():
            self.z_copy(step).wait_send()
            self.c_copy(step).wait_send()
            for other in range(1, self.spot.planes):
                self.p_copy(step, other).wait_send()


class Piece:
    def __init__(self, spot, grads, from_core, from_plane, mine, from_shard, total, index, c_sems, p_sems, z_sems, a_sems):
        self.spot, self.index = spot, index
        self.grads, self.from_core, self.from_plane = grads, from_core, from_plane
        self.mine, self.from_shard, self.total = mine, from_shard, total
        self.c_sems, self.p_sems, self.z_sems, self.a_sems = c_sems, p_sems, z_sems, a_sems

    def c_copy(self):
        s = self.spot
        return remote(self.grads.at[:, :, 1 - s.c], self.from_core, self.c_sems, (self.index,), s.sibling())

    def p_copy(self, step):
        s = self.spot
        other = s.plane(step)
        return remote(
            self.from_core.at[:, :, other], self.from_plane.at[step - 1], self.p_sems, (self.index, step - 1), (other * 2 + s.c, s.z)
        )

    def z_copy(self, step):
        s = self.spot
        other = s.shard(step)
        return remote(self.mine.at[:, other], self.from_shard.at[step - 1], self.z_sems, (self.index, step - 1), (s.d, other))

    def a_copy(self, step):
        s = self.spot
        part = self.total.at[:, s.c, s.t]
        other = lax.rem(s.d + step, 2 * s.planes)
        return remote(part, part, self.a_sems, (self.index, step - 1), (other, s.z))

    def send_c(self):
        self.c_copy().start()

    def send_p(self):
        s = self.spot
        self.c_copy().wait_recv()
        for mat in range(self.grads.shape[0]):
            own = self.grads[mat, :, s.c].astype(f32)
            self.from_core[mat] = (self.from_core[mat].astype(f32) + own).astype(bf16)
        for step in range(1, s.planes):
            self.p_copy(step).start()

    def send_z(self):
        s = self.spot
        for step in range(1, s.planes):
            self.p_copy(step).wait_recv()
        total = self.from_core[:, :, s.t].astype(f32)
        for step in range(1, s.planes):
            total = total + self.from_plane[step - 1].astype(f32)
        self.mine[...] = total.astype(bf16)
        for step in range(1, s.shards):
            self.z_copy(step).start()

    def send_a(self):
        s = self.spot
        for step in range(1, s.shards):
            self.z_copy(step).wait_recv()
        total = self.mine[:, s.z].astype(f32)
        for step in range(1, s.shards):
            total = total + self.from_shard[step - 1].astype(f32)
        self.total[:, s.c, s.t] = total.astype(bf16)
        for step in range(1, 2 * s.planes):
            self.a_copy(step).start()

    def arrive(self):
        for step in range(1, 2 * self.spot.planes):
            self.a_copy(step).wait_recv()

    def close(self):
        for step in range(1, self.spot.planes):
            self.p_copy(step).wait_send()
        for step in range(1, self.spot.shards):
            self.z_copy(step).wait_send()
        for step in range(1, 2 * self.spot.planes):
            self.a_copy(step).wait_send()


def full_kernel(planes, shards,
                length_ref, class_ref, x_hbm, cot_hbm, w_hbm, first_hbm, second_hbm, vec_in, first_vec, second_vec,
                act_hbm, dx_hbm, new_w, low_w, new_first, new_second, vec_out, first_out, second_out, query_out, probs_hbm,
                *rest):
    m = start_refs(*rest[:SHARED], probs_hbm)
    (x_ref, w, vec_own, vec_all, grads, grad_vecs, grads_vec,
     core_in, plane_in, mine, shard_in, total,
     core_in_v, plane_in_v, mine_v, shard_in_v, total_v,
     adam, adam_low,
     x_sem, stage_sem, load_sem, store_sem, out_sem,
     vz0, vz1, wz0, wz1, wp0, wp1, wc0, wc1,
     gc0, gc1, gp0, gp1, gz0, gz1, ga0, ga1) = rest[SHARED:]
    spot = Spot(planes, shards)
    tokens, width = x_ref.shape
    layers = w.shape[0]
    share = width // shards

    def mat(layer, place):
        return w[layer, place].reshape(width, width)

    m.mat = mat
    m.vec = lambda layer, place: vec_all[layer, place : place + 1, :]

    def grad_mat(layer, place, value):
        slot = 1 if place < 3 else 0
        grads[slot, place % 3] = value.astype(bf16).reshape(grads.shape[2:])

    def grad_vec(layer, place, value):
        grad_vecs[layer, place : place + 1, :] = value

    m.grad_mat, m.grad_vec = grad_mat, grad_vec

    groups = [
        Weights(spot, w, layer, first, layer * 2 + first // 3, (wz0, wz1), (wp0, wp1), (wc0, wc1))
        for layer in range(layers) for first in (0, 3)
    ]
    sems = ((gc0, gc1), (gp0, gp1), (gz0, gz1), (ga0, ga1))

    def piece(index, slot):
        return Piece(spot, grads.at[slot], core_in.at[index], plane_in.at[index], mine.at[index], shard_in.at[index],
                     total.at[index], index, *sems)

    feed1, proj1, feed0, proj0 = piece(0, 0), piece(1, 1), piece(2, 0), piece(3, 1)
    vecs = Piece(spot, grads_vec, core_in_v, plane_in_v, mine_v, shard_in_v, total_v, 4, *sems)

    x_copy = pltpu.make_async_copy(x_hbm, x_ref, x_sem.at[0])
    cot_copy = pltpu.make_async_copy(cot_hbm, m.du, x_sem.at[1])
    stages = [
        pltpu.make_async_copy(w_hbm.at[g // 2, 3 * (g % 2) : 3 * (g % 2) + 3], adam.at[g % 2, g // 2], stage_sem.at[g])
        for g in range(4)
    ]
    for copy in stages:
        copy.start()
    x_copy.start()
    cot_copy.start()

    barrier = pltpu.get_barrier_semaphore()
    for step in range(1, 2 * planes):
        pl.semaphore_signal(barrier, inc=1, device_id=(lax.rem(spot.d + step, 2 * planes), spot.z), device_id_type=MESH)
    for step in range(1, shards):
        pl.semaphore_signal(barrier, inc=1, device_id=(spot.d, spot.shard(step)), device_id_type=MESH)

    def cast(g):
        stages[g].wait()
        for place in range(3):
            low = adam[g % 2, g // 2, place].astype(bf16)
            w[g // 2, 3 * (g % 2) + place, spot.z] = low.reshape(w.shape[3:])

    cast(0)
    for layer in range(layers):
        vec_own[spot.z, layer] = jnp.zeros(vec_own.shape[2:], bf16)
        vec_own[spot.z, layer, 0 : vec_in.shape[1]] = vec_in[layer].astype(bf16)
    pl.semaphore_wait(barrier, 2 * planes - 1 + shards - 1)
    groups[0].send_z()

    def v_copy(step):
        part = vec_own.at[spot.z]
        return remote(part, part, (vz0, vz1), (step - 1,), (spot.d, spot.shard(step)))

    for step in range(1, shards):
        v_copy(step).start()
    for g in range(1, 4):
        cast(g)
    length, klass = length_ref[0], class_ref[0]
    known = jnp.where(klass == 0, length, (length + 1) // 2)
    fill_bias(m, known)
    grad_vecs[...] = jnp.zeros_like(grad_vecs)
    grads_vec[...] = jnp.zeros_like(grads_vec)

    def adam_loads(layer, first, slot):
        here = (slice(first, first + 3),)
        return [
            pltpu.make_async_copy(source.at[layer, first : first + 3], adam.at[slot, which], load_sem.at[slot, which])
            for which, source in enumerate((w_hbm, first_hbm, second_hbm))
        ]

    def adam_stores(layer, first, slot):
        copies = [
            pltpu.make_async_copy(adam.at[slot, which], target.at[layer, first : first + 3], store_sem.at[slot, which])
            for which, target in enumerate((new_w, new_first, new_second))
        ]
        copies.append(pltpu.make_async_copy(adam_low.at[slot], low_w.at[layer, first : first + 3], store_sem.at[slot, 3]))
        return copies

    def start(copies):
        for copy in copies:
            copy.start()

    def wait(copies):
        for copy in copies:
            copy.wait()

    def adam_step_of(layer, first, slot, part):
        wait(adam_loads(layer, first, slot))
        part.arrive()

        def one(place, carry):
            grad = part.total[place].reshape(share, width).astype(f32)
            param, one_moment, two_moment = adam_update(
                adam[slot, 0, place], grad, adam[slot, 1, place], adam[slot, 2, place], learn_rate
            )
            adam[slot, 0, place] = param
            adam[slot, 1, place] = one_moment
            adam[slot, 2, place] = two_moment
            adam_low[slot, place] = param.astype(bf16)
            return carry

        lax.fori_loop(0, 3, one, 0)
        start(adam_stores(layer, first, slot))

    groups[0].send_p()
    groups[1].send_z()
    groups[0].send_c()
    groups[1].send_p()
    groups[2].send_z()
    start(adam_loads(1, 3, 0))
    start(adam_loads(1, 0, 1))
    for step in range(1, shards):
        v_copy(step).wait_recv()
    for other in range(shards):
        vec_all[:, :, other * share : (other + 1) * share] = vec_own[other].astype(f32)
    x_copy.wait()
    groups[0].arrive()
    project(m, 0, x_ref)

    def on(index, value, action):
        pl.when(index == value)(action)

    def hook_forward(pair):
        def first():
            groups[1].send_c()
            groups[2].send_p()
            groups[3].send_z()

        def second():
            groups[2].send_c()
            groups[3].send_p()

        on(pair, 1, first)
        on(pair, 2, second)
        on(pair, 3, groups[3].send_c)

    attend(m, 0, known, hook_forward)

    def keep_next(rows, value):
        m.g[rows, :] = value
        m.x1[rows, :] = value.astype(bf16)

    groups[1].arrive()
    feed_forward(m, 0, lambda rows: x_ref[rows, :].astype(f32), keep_next)
    groups[2].arrive()
    project(m, 1, m.x1)
    attend(m, 1, known)
    probs_copy(m, 1, 0, 0, False).start()
    cot_copy.wait()

    def finish(rows, value):
        valid = lax.broadcasted_iota(jnp.int32, (RB, 1), 0) + rows.start < length
        m.probs[1, 0, rows, 0:width] = jnp.where(valid, value, 0.0).astype(bf16)
        m.g[rows, :] = jnp.where(valid, m.du[rows, :].astype(f32), 0.0)

    groups[3].arrive()
    feed_forward(m, 1, lambda rows: m.g[rows, :], finish)
    act_copy = pltpu.make_async_copy(m.probs.at[1, 0, :, 0:width], act_hbm, x_sem.at[2])
    act_copy.start()

    rows_back(m, 1)
    feed1.send_c()
    act_copy.wait()

    def hook_one(pair):
        on(pair, 1, feed1.send_p)
        on(pair, 2, feed1.send_z)
        on(pair, 3, feed1.send_a)

    attend_back(m, 1, hook_one)
    probs_copy(m, 0, 0, 0, False).start()
    project_back(m, 1, m.x1, proj1.send_c)
    adam_step_of(1, 3, 0, feed1)
    proj1.send_p()

    def hook_rows(index):
        on(index, 2, proj1.send_z)

    def ready():
        feed1.c_copy().wait_send()
        proj1.send_a()

    rows_back(m, 0, hook_rows, ready)
    feed0.send_c()

    def hook_two(pair):
        def first():
            adam_step_of(1, 0, 1, proj1)
            feed0.send_p()
            wait(adam_stores(1, 3, 0))
            start(adam_loads(0, 3, 0))

        def third():
            feed0.send_a()
            wait(adam_stores(1, 0, 1))
            start(adam_loads(0, 0, 1))

        on(pair, 1, first)
        on(pair, 2, feed0.send_z)
        on(pair, 3, third)

    attend_back(m, 0, hook_two)
    proj1.c_copy().wait_send()

    def ready_last():
        for layer in range(layers):
            for other in range(shards):
                part = grad_vecs[layer, :, other * share : (other + 1) * share]
                grads_vec[0, other, layer, 0] = part.astype(bf16)
        proj0.send_c()
        vecs.send_c()

    project_back(m, 0, x_ref, ready_last)
    dx_copy = pltpu.make_async_copy(m.g, dx_hbm, out_sem)
    dx_copy.start()
    proj0.send_p()
    vecs.send_p()
    adam_step_of(0, 3, 0, feed0)
    proj0.send_z()
    vecs.send_z()
    proj0.send_a()
    vecs.send_a()
    adam_step_of(0, 0, 1, proj0)
    vecs.arrive()
    count = vec_in.shape[1]
    for layer in range(layers):
        grad = total_v[0, layer, 0].astype(f32)[0:count]
        query_out[layer : layer + 1] = grad[0:1]
        param, one_moment, two_moment = adam_update(vec_in[layer], grad, first_vec[layer], second_vec[layer], vector_rate)
        vec_out[layer] = param
        first_out[layer] = one_moment
        second_out[layer] = two_moment
    for group in groups:
        group.close()
    for step in range(1, shards):
        v_copy(step).wait_send()
    feed0.c_copy().wait_send()
    proj0.c_copy().wait_send()
    vecs.c_copy().wait_send()
    for part in (feed1, proj1, feed0, proj0, vecs):
        part.close()
    wait(adam_stores(0, 3, 0))
    wait(adam_stores(0, 0, 1))
    dx_copy.wait()


def full_body(planes, shards, tokens, lengths, classes, cotangent, weights, vectors, first_weights, second_weights, first_vectors,
              second_vectors):
    _, count, width = tokens.shape
    layers = weights.shape[0]
    rows = width // (2 * planes * shards)
    share = width // shards
    vmem = pl.BlockSpec(memory_space=pltpu.VMEM)
    smem = pl.BlockSpec(memory_space=pltpu.SMEM)
    hbm = pl.BlockSpec(memory_space=pl.ANY)
    dma = pltpu.SemaphoreType.DMA

    def pieces(lead, mats, columns):
        return [
            pltpu.VMEM(lead + (mats, shards, planes, rows, columns), bf16),
            pltpu.VMEM(lead + (planes - 1, mats, shards, rows, columns), bf16),
            pltpu.VMEM(lead + (mats, shards, rows, columns), bf16),
            pltpu.VMEM(lead + (shards - 1, mats, rows, columns), bf16),
            pltpu.VMEM(lead + (mats, 2, planes, rows, columns), bf16),
        ]

    def twice(*shape):
        return [dma(shape), dma(shape)]

    scratch = shared_scratch(layers, count, width) + [
        pltpu.VMEM((count, width), bf16),
        pltpu.VMEM((layers, 6, shards, planes, 2, rows, width), bf16),
        pltpu.VMEM((shards, layers, 16, share), bf16),
        pltpu.VMEM((layers, 16, width), f32),
        pltpu.VMEM((2, 3, shards, 2, planes, rows, width), bf16),
        pltpu.VMEM((layers, 16, width), f32),
        pltpu.VMEM((1, shards, 2, planes, rows, share), bf16),
        *pieces((4,), 3, width),
        *pieces((), 1, share),
        pltpu.VMEM((2, 3, 3, share, width), f32),
        pltpu.VMEM((2, 3, share, width), bf16),
        dma((3,)), dma((4,)), dma((2, 3)), dma((2, 4)), dma,
        *twice(shards - 1),
        *twice(4, shards - 1), *twice(4, shards - 1, planes - 1), *twice(4, shards - 1),
        *twice(5), *twice(5, planes - 1), *twice(5, shards - 1), *twice(5, 2 * planes - 1),
    ]
    shape = jax.ShapeDtypeStruct
    outs = pl.pallas_call(
        functools.partial(full_kernel, planes, shards),
        out_shape=[
            shape((count, width), bf16), shape((count, width), f32),
            shape(weights.shape, f32), shape(weights.shape, bf16), shape(weights.shape, f32), shape(weights.shape, f32),
            shape(vectors.shape, f32), shape(vectors.shape, f32), shape(vectors.shape, f32), shape((layers, share), f32),
            shape((layers, width // PAIR, 2, count, count), bf16),
        ],
        in_specs=[smem, smem] + [hbm] * 5 + [vmem] * 3,
        out_specs=[hbm] * 6 + [vmem] * 4 + [hbm],
        scratch_shapes=scratch,
        compiler_params=pltpu.CompilerParams(vmem_limit_bytes=67043328, collective_id=0, has_side_effects=True),
    )(lengths, classes, tokens[0], cotangent[0], weights, first_weights, second_weights, vectors, first_vectors, second_vectors)
    return (outs[0][None], outs[1][None]) + tuple(outs[2:10])


def solution(mesh):
    devices, shards = mesh.shape["dp"], mesh.shape["shard"]

    def body(*args):
        width = args[0].shape[-1]
        layers = args[4].shape[0]
        rows, left = divmod(width, devices * shards)
        if devices % 2 == 0 and devices > 2 and shards > 1 and left == 0 and rows % 16 == 0 and layers == 2 and width // shards % PAIR == 0:
            return full_body(devices // 2, shards, *args)
        return plain_body(*args)

    cell = P(("dp", "shard"), None, None)
    mats = P(None, None, "shard", None)
    vecs = P(None, None, "shard")
    one = P(("dp", "shard"))
    in_specs = (cell, one, one, cell, mats, vecs, mats, mats, vecs, vecs)
    out_specs = (cell, cell, mats, mats, mats, mats, vecs, vecs, vecs, P(None, "shard"))
    return jax.shard_map(body, mesh=mesh, in_specs=in_specs, out_specs=out_specs, check_vma=False)
```

```python
import functools
import math

import jax
import jax.numpy as jnp
from jax import lax
from jax.experimental import pallas as pl
from jax.experimental.pallas import tpu as pltpu
from jax.sharding import PartitionSpec as P

HEADS = 8
beta_first = 0.5
beta_second = 0.55
learn_rate = 0.05
vector_rate = 0.25
decay_rate = 0.01
adam_eps = 1e-08
adam_step = 3.0
norm_eps = 1e-05

LOG2E = 1.4426950408889634
LN2 = 0.6931471805599453
NEG = -1e30
f32 = jnp.float32
bf16 = jnp.bfloat16
PAIR = 128
RB = 256


def dot(left, right):
    return jnp.dot(left, right, preferred_element_type=f32)


def dot_nt(left, right):
    return lax.dot_general(left, right, (((1,), (1,)), ((), ())), preferred_element_type=f32)


def dot_tn(left, right):
    return lax.dot_general(left, right, (((0,), (0,)), ((), ())), preferred_element_type=f32)


def gelu_parts(value):
    size = jnp.abs(value) * (1.0 / math.sqrt(2.0))
    step = 1.0 / (1.0 + 0.3275911 * size)
    bell = jnp.exp2(value * value * (-0.5 * LOG2E))
    poly = step * (0.254829592 + step * (-0.284496736 + step * (1.421413741 + step * (-1.453152027 + step * 1.061405429))))
    tail = 0.5 * poly * bell
    below = jnp.where(value < 0.0, tail, 1.0 - tail)
    return value * below, below + value * bell * (1.0 / math.sqrt(2.0 * math.pi))


def normalize(value):
    center = jnp.mean(value, axis=-1, keepdims=True)
    centered = value - center
    spread = jnp.mean(centered * centered, axis=-1, keepdims=True)
    inverse = lax.rsqrt(spread + norm_eps)
    return centered * inverse, inverse


def norm_back(grad, normed, inverse, gain):
    scaled = grad * gain
    return inverse * (
        scaled
        - jnp.mean(scaled, axis=-1, keepdims=True)
        - normed * jnp.mean(scaled * normed, axis=-1, keepdims=True)
    )


def lane_masks(rows=1):
    lane = lax.broadcasted_iota(jnp.int32, (rows, PAIR), 1)
    low = jnp.where(lane < 64, 1.0, 0.0)
    return low.astype(bf16), (1.0 - low).astype(bf16)


class Refs:
    pass


def fill_bias(m, known):
    tokens = m.key_bias.shape[0]
    row = lax.broadcasted_iota(jnp.int32, (tokens, PAIR), 0)
    lane = lax.broadcasted_iota(jnp.int32, (tokens, PAIR), 1)
    m.key_bias[...] = jnp.where((lane == 0) & (row >= known), NEG, 0.0).astype(bf16)


def project_one(m, layer, place, xb):
    tokens = xb.shape[0]
    scale = LOG2E / 8.0

    def block(index, carry):
        rows = pl.ds(pl.multiple_of(index * 2 * RB, 2 * RB), 2 * RB)
        value = dot(xb[rows, :], m.mat(layer, place))
        if place == 0:
            m.q[layer, rows, :] = ((value + m.vec(layer, 0)) * scale).astype(bf16)
        elif place == 1:
            m.k[layer, rows, :] = value.astype(bf16)
        else:
            m.v[layer, rows, :] = (value + m.vec(layer, 1)).astype(bf16)
        return carry

    lax.fori_loop(0, tokens // (2 * RB), block, 0)


def project(m, layer, xb):
    tokens = xb.shape[0]
    scale = LOG2E / 8.0

    def block(index, carry):
        rows = pl.ds(pl.multiple_of(index * 2 * RB, 2 * RB), 2 * RB)
        low = xb[rows, :]
        m.q[layer, rows, :] = ((dot(low, m.mat(layer, 0)) + m.vec(layer, 0)) * scale).astype(bf16)
        m.k[layer, rows, :] = dot(low, m.mat(layer, 1)).astype(bf16)
        m.v[layer, rows, :] = (dot(low, m.mat(layer, 2)) + m.vec(layer, 1)).astype(bf16)
        return carry

    lax.fori_loop(0, tokens // (2 * RB), block, 0)


def probs_copy(m, layer, pair, slot, out):
    here, there = m.probs.at[slot], m.probs_hbm.at[layer, pair]
    if out:
        return pltpu.make_async_copy(here, there, m.probs_sem.at[slot])
    return pltpu.make_async_copy(there, here, m.probs_sem.at[slot])


def attend(m, layer, known, hook=None):
    tokens, width = m.q.shape[1:]
    pairs = width // PAIR
    masks = lane_masks()
    lane = lax.broadcasted_iota(jnp.int32, (RB, PAIR), 1)
    ones_lane = jnp.where(lane == 0, 1.0, 0.0).astype(bf16)
    eye = lax.broadcasted_iota(jnp.int32, (RB, RB), 0) == lax.broadcasted_iota(jnp.int32, (RB, RB), 1)
    col = lax.broadcasted_iota(jnp.int32, (1, RB), 1)
    blocks = tokens // RB

    def one_pair(pair, carry):
        if hook is not None:
            hook(pair)
        slot = lax.rem(pair, 2)
        cols = pl.ds(pl.multiple_of(pair * PAIR, PAIR), PAIR)

        @pl.when(pair >= 2)
        def _():
            probs_copy(m, layer, pair - 2, slot, True).wait()

        keys = m.k[layer, :, cols]
        keys_wide = jnp.concatenate([keys, m.key_bias[...]], axis=1)
        values = m.v[layer, :, cols]
        mixed = []
        for head in range(2):
            for block in range(blocks):
                rows = slice(block * RB, (block + 1) * RB)
                query = m.q[layer, rows, cols] * masks[head]
                query_wide = jnp.concatenate([query, ones_lane], axis=1)
                parts = []
                for other in range(blocks):
                    keys_rows = slice(other * RB, (other + 1) * RB)
                    if other == block:
                        part = dot_nt(query, keys[keys_rows])
                        hidden = jnp.where(col + block * RB >= known, NEG, 0.0)
                        part = jnp.where(eye, part, part + hidden)
                    else:
                        part = dot_nt(query_wide, keys_wide[keys_rows])
                    parts.append(part)
                scores = jnp.concatenate(parts, axis=1)
                peak = jnp.max(scores, axis=1, keepdims=True)
                m.probs[slot, head, rows, :] = jnp.exp2(scores - peak).astype(bf16)
            values_wide = values * masks[head] + masks[1 - head]
            mixed.append(dot(m.probs[slot, head], values_wide))
        probs_copy(m, layer, pair, slot, True).start()
        low = lax.broadcasted_iota(jnp.int32, (tokens, PAIR), 1) < 64
        raw = jnp.where(low, mixed[0], mixed[1])
        total = pltpu.roll(jnp.where(low, mixed[1], mixed[0]), 64, 1)
        inverse = 1.0 / total
        m.inv_total[layer, :, cols] = inverse.astype(bf16)
        mean = raw * inverse
        high = mean.astype(bf16)
        m.o[layer, :, cols] = high
        m.o_low[layer, :, cols] = (mean - high.astype(f32)).astype(bf16)
        return carry

    lax.fori_loop(0, pairs, one_pair, 0)
    for pair in (pairs - 2, pairs - 1):
        probs_copy(m, layer, pair, pair % 2, True).wait()


def feed_forward(m, layer, x_of, y_to):
    tokens = m.q.shape[1]

    def block(index, carry):
        rows = pl.ds(pl.multiple_of(index * RB, RB), RB)
        branch = dot(m.o[layer, rows, :], m.mat(layer, 3)) + m.vec(layer, 2)
        normed, inverse = normalize(x_of(rows) + branch)
        m.n1[layer, rows, :] = normed.astype(bf16)
        m.inv[rows, 2 * layer : 2 * layer + 1] = inverse
        first = normed * m.vec(layer, 5) + m.vec(layer, 6)
        pre = dot(first.astype(bf16), m.mat(layer, 4)) + m.vec(layer, 3)
        hidden, slope = gelu_parts(pre)
        low = hidden.astype(bf16)
        m.r[layer, rows, :] = low
        m.slope[layer, rows, :] = slope.astype(bf16)
        feed = dot(low, m.mat(layer, 5)) + m.vec(layer, 4)
        normed, inverse = normalize(first + feed)
        m.n2[layer, rows, :] = normed.astype(bf16)
        m.inv[rows, 2 * layer + 1 : 2 * layer + 2] = inverse
        y_to(rows, normed * m.vec(layer, 7) + m.vec(layer, 8))
        return carry

    lax.fori_loop(0, tokens // RB, block, 0)


def column_sum(value):
    rows, width = value.shape
    return jnp.sum(value.reshape(rows // 8, 8, width), axis=0)


def rows_back(m, layer, hook=None, ready=None):
    tokens = m.q.shape[1]
    for row in range(8):
        m.sums[row] = jnp.zeros_like(m.sums[row])

    def block(index, carry):
        if hook is not None:
            hook(index)
        rows = pl.ds(pl.multiple_of(index * RB, RB), RB)
        grad = m.g[rows, :]
        normed = m.n2[layer, rows, :].astype(f32)
        m.sums[0] += column_sum(grad * normed)
        m.sums[1] += column_sum(grad)
        back = norm_back(grad, normed, m.inv[rows, 2 * layer + 1 : 2 * layer + 2], m.vec(layer, 7))
        m.sums[2] += column_sum(back)
        low = back.astype(bf16)
        m.n2[layer, rows, :] = low
        pre = dot_nt(low, m.mat(layer, 5)) * m.slope[layer, rows, :].astype(f32)
        m.sums[3] += column_sum(pre)
        low = pre.astype(bf16)
        m.du[rows, :] = low
        grad = back + dot_nt(low, m.mat(layer, 4))
        normed = m.n1[layer, rows, :].astype(f32)
        m.sums[4] += column_sum(grad * normed)
        m.sums[5] += column_sum(grad)
        back = norm_back(grad, normed, m.inv[rows, 2 * layer : 2 * layer + 1], m.vec(layer, 5))
        m.sums[6] += column_sum(back)
        m.g[rows, :] = back
        low = back.astype(bf16)
        m.n1[layer, rows, :] = low
        m.inv_total[layer, rows, :] = (dot_nt(low, m.mat(layer, 3)) * m.inv_total[layer, rows, :].astype(f32)).astype(bf16)
        first = normed * m.vec(layer, 5) + m.vec(layer, 6)
        m.slope[layer, rows, :] = first.astype(bf16)
        return carry

    lax.fori_loop(0, tokens // RB, block, 0)
    for row, place in ((0, 7), (1, 8), (2, 4), (3, 3), (4, 5), (5, 6), (6, 2)):
        m.grad_vec(layer, place, jnp.sum(m.sums[row], axis=0, keepdims=True))
    if ready is not None:
        ready()
    m.grad_mat(layer, 5, dot_tn(m.r[layer], m.n2[layer]))
    m.grad_mat(layer, 4, dot_tn(m.slope[layer], m.du[...]))
    m.grad_mat(layer, 3, dot_tn(m.o[layer], m.n1[layer]))


def attend_back(m, layer, hook=None, xb=None):
    tokens, width = m.q.shape[1:]
    pairs = width // PAIR
    masks = lane_masks()
    blocks = tokens // RB

    def one_pair(pair, carry):
        slot = lax.rem(pair, 2)
        cols = pl.ds(pl.multiple_of(pair * PAIR, PAIR), PAIR)
        probs_copy(m, layer, pair, slot, False).wait()

        @pl.when(pair + 1 < pairs)
        def _():
            probs_copy(m, layer, pair + 1, 1 - slot, False).start()

        grad = m.inv_total[layer, :, cols]
        turned = pltpu.roll(
            grad.astype(f32) * (m.o[layer, :, cols].astype(f32) + m.o_low[layer, :, cols].astype(f32)), 64, 1
        )
        turned_high = turned.astype(bf16)
        turned_low = (turned - turned_high.astype(f32)).astype(bf16)
        values = m.v[layer, :, cols]
        keys = m.k[layer, :, cols]
        query_turned = m.q[layer, :, cols].T
        grad_turned = grad.T
        grad_query, grad_keys, grad_values = [], [], []
        for head in range(2):
            part = slice(head * 64, (head + 1) * 64)
            wide = jnp.concatenate(
                [grad * masks[head] - turned_high * masks[1 - head], -turned_low * masks[1 - head]], axis=1
            )
            values_wide = jnp.concatenate(
                [values * masks[head] + masks[1 - head], jnp.broadcast_to(masks[1 - head], values.shape)], axis=1
            )
            grad_values.append(dot(grad_turned[part], m.probs[slot, head]))
            for block in range(blocks):
                rows = slice(block * RB, (block + 1) * RB)
                score = dot_nt(wide[rows], values_wide)
                m.probs[slot, head, rows, :] = (score * m.probs[slot, head, rows, :].astype(f32)).astype(bf16)
            grad_keys.append(dot(query_turned[part], m.probs[slot, head]))
            grad_query.append(dot(m.probs[slot, head], keys))
            if hook is not None and head == 0:
                hook(pair, 0)
        low = lax.broadcasted_iota(jnp.int32, (tokens, PAIR), 1) < 64
        back_query = (jnp.where(low, grad_query[0], grad_query[1]) * 0.125).astype(bf16)
        back_keys = (jnp.concatenate(grad_keys, axis=0) * LN2).astype(bf16)
        back_values = jnp.concatenate(grad_values, axis=0).astype(bf16)
        m.q[layer, :, cols] = back_query
        m.k[layer, :, cols] = back_keys.T
        m.v[layer, :, cols] = back_values.T
        if xb is not None:
            m.grad_pair(layer, pair, dot(jnp.concatenate([back_query.T, back_keys, back_values], axis=0), xb[...]))
        if hook is not None:
            hook(pair, 1)
        return carry

    lax.fori_loop(0, pairs, one_pair, 0)


def project_back(m, layer, xb=None, ready=None, hook=None):
    tokens = m.q.shape[1]
    ones = jnp.ones((8, tokens), bf16)
    m.grad_vec(layer, 0, dot(ones, m.q[layer])[0:1])
    m.grad_vec(layer, 1, dot(ones, m.v[layer])[0:1])
    if xb is not None:
        m.grad_mat(layer, 0, dot_tn(xb[...], m.q[layer]))
        m.grad_mat(layer, 1, dot_tn(xb[...], m.k[layer]))
        m.grad_mat(layer, 2, dot_tn(xb[...], m.v[layer]))
    if ready is not None:
        ready()

    def block(index, carry):
        if hook is not None:
            hook(index)
        rows = pl.ds(pl.multiple_of(index * RB, RB), RB)
        m.g[rows, :] = (
            m.g[rows, :]
            + dot_nt(m.q[layer, rows, :], m.mat(layer, 0))
            + dot_nt(m.k[layer, rows, :], m.mat(layer, 1))
            + dot_nt(m.v[layer, rows, :], m.mat(layer, 2))
        )
        return carry

    lax.fori_loop(0, tokens // RB, block, 0)


def start_refs(q, k, v, o, o_low, inv_total, n1, n2, inv, r, slope, g, x1, du, sums, key_bias,
               probs, probs_sem, probs_hbm):
    m = Refs()
    m.q, m.k, m.v, m.o, m.o_low, m.inv_total = q, k, v, o, o_low, inv_total
    m.n1, m.n2, m.inv, m.r, m.slope, m.g, m.x1 = n1, n2, inv, r, slope, g, x1
    m.du, m.sums, m.key_bias = du, sums, key_bias
    m.probs, m.probs_sem, m.probs_hbm = probs, probs_sem, probs_hbm
    return m


def shared_scratch(layers, count, width):
    both = (layers, count, width)
    one = (count, width)
    return [
        pltpu.VMEM(both, bf16), pltpu.VMEM(both, bf16), pltpu.VMEM(both, bf16), pltpu.VMEM(both, bf16),
        pltpu.VMEM(both, bf16), pltpu.VMEM(both, bf16), pltpu.VMEM(both, bf16), pltpu.VMEM(both, bf16),
        pltpu.VMEM((count, 2 * layers), f32),
        pltpu.VMEM(both, bf16), pltpu.VMEM(both, bf16),
        pltpu.VMEM(one, f32), pltpu.VMEM(one, bf16),
        pltpu.VMEM(one, bf16),
        pltpu.VMEM((8, 8, width), f32),
        pltpu.VMEM((count, PAIR), bf16),
        pltpu.VMEM((2, 2, count, count), bf16),
        pltpu.SemaphoreType.DMA((2,)),
    ]


SHARED = 18


def plain_kernel(length_ref, class_ref, x_ref, cot_ref, w_ref, vec_ref, act_ref, dx_ref, mats_ref, vecs_ref, probs_hbm, *rest):
    m = start_refs(*rest[:SHARED], probs_hbm)
    out_sem = rest[SHARED]
    m.mat = lambda layer, place: w_ref[layer, place]
    m.vec = lambda layer, place: vec_ref[layer, place : place + 1, :]

    def grad_mat(layer, place, value):
        mats_ref[layer, place] = value.astype(bf16)

    def grad_vec(layer, place, value):
        vecs_ref[layer, place : place + 1, :] = value

    m.grad_mat, m.grad_vec = grad_mat, grad_vec
    length, klass = length_ref[0], class_ref[0]
    known = jnp.where(klass == 0, length, (length + 1) // 2)
    fill_bias(m, known)
    project(m, 0, x_ref)
    attend(m, 0, known)

    def keep_next(rows, value):
        m.g[rows, :] = value
        m.x1[rows, :] = value.astype(bf16)

    feed_forward(m, 0, lambda rows: x_ref[rows, :].astype(f32), keep_next)
    project(m, 1, m.x1)
    attend(m, 1, known)
    probs_copy(m, 1, 0, 0, False).start()

    def finish(rows, value):
        valid = lax.broadcasted_iota(jnp.int32, (RB, 1), 0) + rows.start < length
        act_ref[rows, :] = jnp.where(valid, value, 0.0).astype(bf16)
        m.g[rows, :] = jnp.where(valid, cot_ref[rows, :].astype(f32), 0.0)

    feed_forward(m, 1, lambda rows: m.g[rows, :], finish)
    for layer, xb in ((1, m.x1), (0, x_ref)):
        rows_back(m, layer)
        attend_back(m, layer)
        if layer:
            probs_copy(m, layer - 1, 0, 0, False).start()
        project_back(m, layer, xb)
    copy = pltpu.make_async_copy(m.g, dx_ref, out_sem)
    copy.start()
    copy.wait()


def plain_pass(lengths, classes, tokens, cotangent, mats, vecs):
    count, width = tokens.shape
    layers = mats.shape[0]
    vmem = pl.BlockSpec(memory_space=pltpu.VMEM)
    smem = pl.BlockSpec(memory_space=pltpu.SMEM)
    hbm = pl.BlockSpec(memory_space=pl.ANY)
    outs = pl.pallas_call(
        plain_kernel,
        out_shape=[
            jax.ShapeDtypeStruct((count, width), bf16),
            jax.ShapeDtypeStruct((count, width), f32),
            jax.ShapeDtypeStruct(mats.shape, bf16),
            jax.ShapeDtypeStruct((layers, 16, width), f32),
            jax.ShapeDtypeStruct((layers, width // PAIR, 2, count, count), bf16),
        ],
        in_specs=[smem, smem, vmem, vmem, vmem, vmem],
        out_specs=[vmem, hbm, vmem, vmem, hbm],
        scratch_shapes=shared_scratch(layers, count, width) + [pltpu.SemaphoreType.DMA],
        compiler_params=pltpu.CompilerParams(vmem_limit_bytes=67043328),
    )(lengths, classes, tokens, cotangent, mats, vecs)
    return outs[:4]


def adam_update(param, grad, first, second, rate):
    first_new = beta_first * first + (1.0 - beta_first) * grad
    second_new = beta_second * second + (1.0 - beta_second) * grad * grad
    first_hat = first_new / (1.0 - beta_first**adam_step)
    second_hat = second_new / (1.0 - beta_second**adam_step)
    param_new = param - rate * (first_hat / (jnp.sqrt(second_hat) + adam_eps) + decay_rate * param)
    return (param_new, first_new, second_new)


def plain_body(tokens, lengths, classes, cotangent, weights, vectors, first_weights, second_weights, first_vectors, second_vectors):
    mats = lax.all_gather(weights.astype(bf16), "shard", axis=2, tiled=True)
    vecs = lax.all_gather(vectors.astype(bf16), "shard", axis=2, tiled=True).astype(f32)
    vecs = jnp.pad(vecs, ((0, 0), (0, 16 - vecs.shape[1]), (0, 0)))
    activations, input_grad, grad_mats, grad_vecs = plain_pass(lengths, classes, tokens[0], cotangent[0], mats, vecs)
    grad_vecs = grad_vecs[:, : vectors.shape[1]]
    total_mats = lax.psum_scatter(grad_mats, "shard", scatter_dimension=2, tiled=True)
    total_vecs = lax.psum_scatter(grad_vecs.astype(bf16), "shard", scatter_dimension=2, tiled=True)
    total_mats = lax.psum(total_mats, "dp").astype(f32)
    total_vecs = lax.psum(total_vecs, "dp").astype(f32)
    new_weights, new_first_weights, new_second_weights = adam_update(
        weights, total_mats, first_weights, second_weights, learn_rate
    )
    new_vectors, new_first_vectors, new_second_vectors = adam_update(
        vectors, total_vecs, first_vectors, second_vectors, vector_rate
    )
    return (
        activations[None], input_grad[None], new_weights, new_weights.astype(bf16), new_first_weights, new_second_weights,
        new_vectors, new_first_vectors, new_second_vectors, total_vecs[:, 0],
    )


MESH = pl.DeviceIdType.MESH


def remote(src, dst, sems, place, device):
    return pltpu.make_async_remote_copy(
        src_ref=src, dst_ref=dst, send_sem=sems[0].at[place], recv_sem=sems[1].at[place], device_id=device, device_id_type=MESH
    )


class Spot:
    def __init__(self, planes, shards):
        self.planes, self.shards = planes, shards
        self.d, self.z = lax.axis_index("dp"), lax.axis_index("shard")
        self.c, self.t = lax.rem(self.d, 2), lax.div(self.d, 2)

    def plane(self, step):
        return lax.rem(self.t + step, self.planes)

    def shard(self, step):
        return lax.rem(self.z + step, self.shards)

    def sibling(self):
        return (self.t * 2 + 1 - self.c, self.z)


class Weights:
    def __init__(self, spot, w, layer, first, count, index, z_sems, p_sems, c_sems):
        self.spot, self.index = spot, index
        self.z_sems, self.p_sems, self.c_sems = z_sems, p_sems, c_sems
        self.view = w.at[layer, first : first + count]

    def z_copy(self, step):
        s = self.spot
        piece = self.view.at[:, s.z, s.t, s.c]
        return remote(piece, piece, self.z_sems, (self.index, step - 1), (s.d, s.shard(step)))

    def p_copy(self, z_step, t_step):
        s = self.spot
        piece = self.view.at[:, s.shard(s.shards - z_step), s.t, s.c]
        place = (self.index, z_step - 1, t_step - 1)
        return remote(piece, piece, self.p_sems, place, (s.plane(t_step) * 2 + s.c, s.z))

    def c_copy(self, z_step):
        s = self.spot
        piece = self.view.at[:, s.shard(s.shards - z_step), :, s.c]
        return remote(piece, piece, self.c_sems, (self.index, z_step - 1), s.sibling())

    def steps(self):
        return range(1, self.spot.shards)

    def send_z(self):
        for step in self.steps():
            self.z_copy(step).start()

    def send_p(self):
        for step in self.steps():
            self.z_copy(step).wait_recv()
            for other in range(1, self.spot.planes):
                self.p_copy(step, other).start()

    def send_c(self):
        for step in self.steps():
            for other in range(1, self.spot.planes):
                self.p_copy(step, other).wait_recv()
            self.c_copy(step).start()

    def arrive(self):
        for step in self.steps():
            self.c_copy(step).wait_recv()

    def close(self):
        for step in self.steps():
            self.z_copy(step).wait_send()
            self.c_copy(step).wait_send()
            for other in range(1, self.spot.planes):
                self.p_copy(step, other).wait_send()


class Piece:
    def __init__(self, spot, grads, from_core, from_plane, mine, from_shard, total, index, c_sems, p_sems, z_sems, a_sems, b_sems):
        self.spot, self.index = spot, index
        self.grads, self.from_core, self.from_plane = grads, from_core, from_plane
        self.mine, self.from_shard, self.total = mine, from_shard, total
        self.c_sems, self.p_sems, self.z_sems, self.a_sems, self.b_sems = c_sems, p_sems, z_sems, a_sems, b_sems

    def c_copy(self):
        s = self.spot
        return remote(self.grads.at[:, :, 1 - s.c], self.from_core, self.c_sems, (self.index,), s.sibling())

    def p_copy(self, step):
        s = self.spot
        other = s.plane(step)
        return remote(
            self.from_core.at[:, :, other], self.from_plane.at[step - 1], self.p_sems, (self.index, step - 1), (other * 2 + s.c, s.z)
        )

    def z_copy(self, step):
        s = self.spot
        other = s.shard(step)
        return remote(self.mine.at[:, other], self.from_shard.at[step - 1], self.z_sems, (self.index, step - 1), (s.d, other))

    def a_copy(self, step):
        s = self.spot
        part = self.total.at[:, s.c, s.t]
        return remote(part, part, self.a_sems, (self.index, step - 1), (s.plane(step) * 2 + s.c, s.z))

    def b_copy(self):
        s = self.spot
        part = self.total.at[:, s.c]
        return remote(part, part, self.b_sems, (self.index,), s.sibling())

    def send_c(self):
        self.c_copy().start()

    def send_p(self):
        s = self.spot
        self.c_copy().wait()
        for mat in range(self.grads.shape[0]):
            own = self.grads[mat, :, s.c].astype(f32)
            self.from_core[mat] = (self.from_core[mat].astype(f32) + own).astype(bf16)
        for step in range(1, s.planes):
            self.p_copy(step).start()

    def send_z(self):
        s = self.spot
        for step in range(1, s.planes):
            self.p_copy(step).wait_recv()
        total = self.from_core[:, :, s.t].astype(f32)
        for step in range(1, s.planes):
            total = total + self.from_plane[step - 1].astype(f32)
        self.mine[...] = total.astype(bf16)
        for step in range(1, s.shards):
            self.z_copy(step).start()

    def send_a(self):
        s = self.spot
        for step in range(1, s.shards):
            self.z_copy(step).wait_recv()
        total = self.mine[:, s.z].astype(f32)
        for step in range(1, s.shards):
            total = total + self.from_shard[step - 1].astype(f32)
        self.total[:, s.c, s.t] = total.astype(bf16)
        for step in range(1, s.planes):
            self.a_copy(step).start()

    def send_b(self):
        for step in range(1, self.spot.planes):
            self.a_copy(step).wait_recv()
        self.b_copy().start()

    def arrive(self):
        self.b_copy().wait_recv()

    def close(self):
        for step in range(1, self.spot.planes):
            self.p_copy(step).wait_send()
            self.a_copy(step).wait_send()
        for step in range(1, self.spot.shards):
            self.z_copy(step).wait_send()
        self.b_copy().wait_send()


def full_kernel(planes, shards,
                length_ref, class_ref, x_hbm, cot_hbm, w_hbm, vec_in, act_hbm, dx_hbm, tot_hbm, tot_vec, probs_hbm, *rest):
    m = start_refs(*rest[:SHARED], probs_hbm)
    (x_ref, w, vec_own, vec_all, grads, pair_grads, grad_vecs, grads_vec,
     core_in, plane_in, mine, shard_in, total,
     core_in_p, plane_in_p, mine_p, shard_in_p, total_p,
     core_in_v, plane_in_v, mine_v, shard_in_v, total_v,
     stage,
     x_sem, stage_sem, feed_sem, pair_sem, vec_sem, out_sem,
     vz0, vz1, wz0, wz1, wp0, wp1, wc0, wc1,
     gc0, gc1, gp0, gp1, gz0, gz1, ga0, ga1, gb0, gb1) = rest[SHARED:]
    spot = Spot(planes, shards)
    tokens, width = x_ref.shape
    layers = w.shape[0]
    share = width // shards

    def mat(layer, place):
        return w[layer, place].reshape(width, width)

    m.mat = mat
    m.vec = lambda layer, place: vec_all[layer, place : place + 1, :]

    def grad_mat(layer, place, value):
        grads[place - 3] = value.astype(bf16).reshape(grads.shape[1:])

    def grad_pair(layer, pair, value):
        turned = value.astype(bf16).T
        for place in range(3):
            part = turned[:, place * PAIR : (place + 1) * PAIR]
            pair_grads[pair, place] = part.reshape(pair_grads.shape[2:])

    def grad_vec(layer, place, value):
        grad_vecs[layer, place : place + 1, :] = value

    m.grad_mat, m.grad_vec, m.grad_pair = grad_mat, grad_vec, grad_pair

    groups = [
        Weights(spot, w, layer, first, count, index, (wz0, wz1), (wp0, wp1), (wc0, wc1))
        for index, (layer, first, count) in enumerate(((0, 0, 1), (0, 1, 1), (0, 2, 1), (0, 3, 3), (1, 0, 3), (1, 3, 3)))
    ]
    sems = ((gc0, gc1), (gp0, gp1), (gz0, gz1), (ga0, ga1), (gb0, gb1))

    pairs = width // PAIR

    def feed_piece(layer):
        i = layers - 1 - layer
        return Piece(spot, grads, core_in.at[i], plane_in.at[i], mine.at[i], shard_in.at[i], total.at[i], i, *sems)

    def pair_piece(layer, pair):
        i = (layers - 1 - layer) * pairs + pair
        return Piece(spot, pair_grads.at[pair], core_in_p.at[i], plane_in_p.at[i], mine_p.at[i], shard_in_p.at[i],
                     total_p.at[i], layers + i, *sems)

    def feed_out(layer):
        i = layers - 1 - layer
        return pltpu.make_async_copy(total.at[i], tot_hbm.at[layer, 3:6], feed_sem.at[i])

    def pair_out(layer, pair):
        i = (layers - 1 - layer) * pairs + pair
        cols = pl.ds(pl.multiple_of(pair * PAIR, PAIR), PAIR)
        return pltpu.make_async_copy(total_p.at[i], tot_hbm.at[layer, 0:3, :, :, :, cols], pair_sem.at[i])

    feed1, feed0 = feed_piece(1), feed_piece(0)
    vecs = Piece(spot, grads_vec, core_in_v, plane_in_v, mine_v, shard_in_v, total_v, layers * (pairs + 1), *sems)

    x_copy = pltpu.make_async_copy(x_hbm, x_ref, x_sem.at[0])
    cot_copy = pltpu.make_async_copy(cot_hbm, m.du, x_sem.at[1])
    stages = [
        pltpu.make_async_copy(w_hbm.at[g // 2, 3 * (g % 2) : 3 * (g % 2) + 3], stage.at[g], stage_sem.at[g])
        for g in range(4)
    ]
    for copy in stages:
        copy.start()
    x_copy.start()
    cot_copy.start()

    barrier = pltpu.get_barrier_semaphore()
    for step in range(1, 2 * planes):
        pl.semaphore_signal(barrier, inc=1, device_id=(lax.rem(spot.d + step, 2 * planes), spot.z), device_id_type=MESH)
    for step in range(1, shards):
        pl.semaphore_signal(barrier, inc=1, device_id=(spot.d, spot.shard(step)), device_id_type=MESH)

    def cast(g):
        stages[g].wait()
        for place in range(3):
            low = stage[g, place].astype(bf16)
            w[g // 2, 3 * (g % 2) + place, spot.z] = low.reshape(w.shape[3:])

    cast(0)
    vec_all[...] = jnp.zeros_like(vec_all)
    for layer in range(layers):
        for place in range(vec_in.shape[0]):
            vec_all[layer, place : place + 1, 0:share] = vec_in[place, layer : layer + 1, :]
        vec_own[spot.z, layer] = vec_all[layer, :, 0:share].astype(bf16)
    pl.semaphore_wait(barrier, 2 * planes - 1 + shards - 1)
    for g in range(3):
        groups[g].send_z()

    def v_copy(step):
        part = vec_own.at[spot.z]
        return remote(part, part, (vz0, vz1), (step - 1,), (spot.d, spot.shard(step)))

    for step in range(1, shards):
        v_copy(step).start()
    for g in range(1, 4):
        cast(g)
    length, klass = length_ref[0], class_ref[0]
    known = jnp.where(klass == 0, length, (length + 1) // 2)
    fill_bias(m, known)
    grad_vecs[...] = jnp.zeros_like(grad_vecs)
    grads_vec[...] = jnp.zeros_like(grads_vec)

    groups[0].send_p()
    groups[1].send_p()
    groups[0].send_c()
    groups[2].send_p()
    groups[1].send_c()
    groups[3].send_z()
    groups[2].send_c()
    for step in range(1, shards):
        v_copy(step).wait_recv()
    for other in range(shards):
        vec_all[:, :, other * share : (other + 1) * share] = vec_own[other].astype(f32)
    x_copy.wait()
    for place in range(3):
        groups[place].arrive()
        project_one(m, 0, place, x_ref)
    groups[3].send_p()
    groups[4].send_z()

    def on(index, value, action):
        pl.when(index == value)(action)

    def hook_forward(pair):
        def first():
            groups[3].send_c()
            groups[4].send_p()

        def third():
            groups[4].send_c()
            groups[5].send_p()

        on(pair, 1, first)
        on(pair, 2, groups[5].send_z)
        on(pair, 3, third)

    attend(m, 0, known, hook_forward)

    def keep_next(rows, value):
        m.g[rows, :] = value
        m.x1[rows, :] = value.astype(bf16)

    groups[3].arrive()
    feed_forward(m, 0, lambda rows: x_ref[rows, :].astype(f32), keep_next)
    groups[5].send_c()
    groups[4].arrive()
    project(m, 1, m.x1)
    attend(m, 1, known)
    probs_copy(m, 1, 0, 0, False).start()
    cot_copy.wait()

    def finish(rows, value):
        valid = lax.broadcasted_iota(jnp.int32, (RB, 1), 0) + rows.start < length
        m.probs[1, 0, rows, 0:width] = jnp.where(valid, value, 0.0).astype(bf16)
        m.g[rows, :] = jnp.where(valid, m.du[rows, :].astype(f32), 0.0)

    groups[5].arrive()
    feed_forward(m, 1, lambda rows: m.g[rows, :], finish)
    act_copy = pltpu.make_async_copy(m.probs.at[1, 0, :, 0:width], act_hbm, x_sem.at[2])
    act_copy.start()

    rows_back(m, 1)
    feed1.send_c()
    act_copy.wait()

    def hook_of(layer, feed):
        def hook(pair, place):
            if place == 0:
                on(pair, 0, feed.send_p)
                on(pair, 3, feed.send_a)
                pl.when(pair >= 1)(pair_piece(layer, pair - 1).send_p)
                pl.when(pair >= 2)(pair_piece(layer, pair - 2).send_z)
                pl.when(pair >= 3)(pair_piece(layer, pair - 3).send_a)
                if layer == 0:
                    on(pair, 0, feed1.send_b)
            else:
                pair_piece(layer, pair).send_c()
                on(pair, 1, feed.send_z)
                if layer == 0:
                    pair_piece(1, pair).send_b()

        return hook

    last = pairs - 1
    attend_back(m, 1, hook_of(1, feed1), m.x1)
    probs_copy(m, 0, 0, 0, False).start()

    def hook_dx1(index):
        def second():
            pair_piece(1, last).send_p()
            pair_piece(1, last - 1).send_z()
            pair_piece(1, last - 2).send_a()

        on(index, 2, second)

    project_back(m, 1, hook=hook_dx1)

    def hook_rows(index):
        def first():
            pair_piece(1, last).send_z()
            pair_piece(1, last - 1).send_a()

        on(index, 1, first)
        on(index, 3, pair_piece(1, last).send_a)

    rows_back(m, 0, hook_rows)
    feed0.send_c()
    attend_back(m, 0, hook_of(0, feed0), x_ref)

    def ready_last():
        for layer in range(layers):
            for other in range(shards):
                part = grad_vecs[layer, :, other * share : (other + 1) * share]
                grads_vec[0, other, layer, 0] = part.astype(bf16)
        vecs.send_c()

    def hook_dx0(index):
        def first():
            vecs.send_p()
            pair_piece(0, last - 1).send_z()
            pair_piece(0, last - 2).send_a()
            feed0.send_b()

        def third():
            pair_piece(0, last).send_z()
            vecs.send_z()
            pair_piece(0, last - 1).send_a()

        on(index, 0, pair_piece(0, last).send_p)
        on(index, 1, first)
        on(index, 3, third)

    project_back(m, 0, ready=ready_last, hook=hook_dx0)
    dx_copy = pltpu.make_async_copy(m.g, dx_hbm, out_sem)
    dx_copy.start()
    for pair in range(last):
        pair_piece(0, pair).send_b()
    pair_piece(0, last).send_a()
    vecs.send_a()
    pair_piece(0, last).send_b()
    vecs.send_b()
    for layer, feed in ((1, feed1), (0, feed0)):
        feed.arrive()
        feed_out(layer).start()
        for pair in range(pairs):
            pair_piece(layer, pair).arrive()
            pair_out(layer, pair).start()
    vecs.arrive()
    vec_copy = pltpu.make_async_copy(total_v.at[0, :, 0], tot_vec, vec_sem)
    vec_copy.start()
    for group in groups:
        group.close()
    for step in range(1, shards):
        v_copy(step).wait_send()
    for layer, feed in ((1, feed1), (0, feed0)):
        feed.close()
        for pair in range(pairs):
            pair_piece(layer, pair).close()
    vecs.close()
    for layer in (1, 0):
        feed_out(layer).wait()
        for pair in range(pairs):
            pair_out(layer, pair).wait()
    vec_copy.wait()
    dx_copy.wait()


def full_body(planes, shards, tokens, lengths, classes, cotangent, weights, vectors, first_weights, second_weights, first_vectors,
              second_vectors):
    _, count, width = tokens.shape
    layers = weights.shape[0]
    rows = width // (2 * planes * shards)
    share = width // shards
    pairs = width // PAIR
    sent = layers * (pairs + 1) + 1
    vmem = pl.BlockSpec(memory_space=pltpu.VMEM)
    smem = pl.BlockSpec(memory_space=pltpu.SMEM)
    hbm = pl.BlockSpec(memory_space=pl.ANY)
    dma = pltpu.SemaphoreType.DMA

    def pieces(lead, mats, columns):
        return [
            pltpu.VMEM(lead + (mats, shards, planes, rows, columns), bf16),
            pltpu.VMEM(lead + (planes - 1, mats, shards, rows, columns), bf16),
            pltpu.VMEM(lead + (mats, shards, rows, columns), bf16),
            pltpu.VMEM(lead + (shards - 1, mats, rows, columns), bf16),
            pltpu.VMEM(lead + (mats, 2, planes, rows, columns), bf16),
        ]

    def twice(*shape):
        return [dma(shape), dma(shape)]

    scratch = shared_scratch(layers, count, width) + [
        pltpu.VMEM((count, width), bf16),
        pltpu.VMEM((layers, 6, shards, planes, 2, rows, width), bf16),
        pltpu.VMEM((shards, layers, 16, share), bf16),
        pltpu.VMEM((layers, 16, width), f32),
        pltpu.VMEM((3, shards, 2, planes, rows, width), bf16),
        pltpu.VMEM((pairs, 3, shards, 2, planes, rows, PAIR), bf16),
        pltpu.VMEM((layers, 16, width), f32),
        pltpu.VMEM((1, shards, 2, planes, rows, share), bf16),
        *pieces((layers,), 3, width),
        *pieces((layers * pairs,), 3, PAIR),
        *pieces((), 1, share),
        pltpu.VMEM((4, 3, share, width), f32),
        dma((3,)), dma((4,)), dma((layers,)), dma((layers * pairs,)), dma, dma,
        *twice(shards - 1),
        *twice(6, shards - 1), *twice(6, shards - 1, planes - 1), *twice(6, shards - 1),
        *twice(sent), *twice(sent, planes - 1), *twice(sent, shards - 1), *twice(sent, planes - 1), *twice(sent),
    ]
    shape = jax.ShapeDtypeStruct
    outs = pl.pallas_call(
        functools.partial(full_kernel, planes, shards),
        out_shape=[
            shape((count, width), bf16), shape((count, width), f32), shape((layers, 6, 2, planes, rows, width), bf16),
            shape((layers, rows, share), bf16), shape((layers, pairs, 2, count, count), bf16),
        ],
        in_specs=[smem, smem] + [hbm] * 3 + [vmem],
        out_specs=[hbm] * 5,
        scratch_shapes=scratch,
        compiler_params=pltpu.CompilerParams(vmem_limit_bytes=67043328, collective_id=0, has_side_effects=True),
    )(lengths, classes, tokens[0], cotangent[0], weights, jnp.transpose(vectors, (1, 0, 2)))
    total_mats = outs[2].reshape(weights.shape).astype(f32)
    total_vecs = outs[3][:, : vectors.shape[1]].astype(f32)
    new_weights, new_first_weights, new_second_weights = adam_update(
        weights, total_mats, first_weights, second_weights, learn_rate
    )
    new_vectors, new_first_vectors, new_second_vectors = adam_update(
        vectors, total_vecs, first_vectors, second_vectors, vector_rate
    )
    return (
        outs[0][None], outs[1][None], new_weights, new_weights.astype(bf16), new_first_weights, new_second_weights,
        new_vectors, new_first_vectors, new_second_vectors, total_vecs[:, 0],
    )


def solution(mesh):
    devices, shards = mesh.shape["dp"], mesh.shape["shard"]

    def body(*args):
        width = args[0].shape[-1]
        layers = args[4].shape[0]
        rows, left = divmod(width, devices * shards)
        if devices % 2 == 0 and devices > 2 and shards > 1 and left == 0 and rows == 16 and layers == 2 and width // shards % PAIR == 0:
            return full_body(devices // 2, shards, *args)
        return plain_body(*args)

    cell = P(("dp", "shard"), None, None)
    mats = P(None, None, "shard", None)
    vecs = P(None, None, "shard")
    one = P(("dp", "shard"))
    in_specs = (cell, one, one, cell, mats, vecs, mats, mats, vecs, vecs)
    out_specs = (cell, cell, mats, mats, mats, mats, vecs, vecs, vecs, P(None, "shard"))
    return jax.shard_map(body, mesh=mesh, in_specs=in_specs, out_specs=out_specs, check_vma=False)
```

```python
import functools
import math

import jax
import jax.numpy as jnp
from jax import lax
from jax.experimental import pallas as pl
from jax.experimental.pallas import tpu as pltpu
from jax.sharding import PartitionSpec as P

HEADS = 8
beta_first = 0.5
beta_second = 0.55
learn_rate = 0.05
vector_rate = 0.25
decay_rate = 0.01
adam_eps = 1e-08
adam_step = 3.0
norm_eps = 1e-05

LOG2E = 1.4426950408889634
LN2 = 0.6931471805599453
NEG = -1e30
f32 = jnp.float32
bf16 = jnp.bfloat16
PAIR = 128
RB = 256


def dot(left, right):
    return jnp.dot(left, right, preferred_element_type=f32)


def dot_nt(left, right):
    return lax.dot_general(left, right, (((1,), (1,)), ((), ())), preferred_element_type=f32)


def dot_tn(left, right):
    return lax.dot_general(left, right, (((0,), (0,)), ((), ())), preferred_element_type=f32)


def gelu_parts(value):
    size = jnp.abs(value) * (1.0 / math.sqrt(2.0))
    step = 1.0 / (1.0 + 0.3275911 * size)
    bell = jnp.exp2(value * value * (-0.5 * LOG2E))
    poly = step * (0.254829592 + step * (-0.284496736 + step * (1.421413741 + step * (-1.453152027 + step * 1.061405429))))
    tail = 0.5 * poly * bell
    below = jnp.where(value < 0.0, tail, 1.0 - tail)
    return value * below, below + value * bell * (1.0 / math.sqrt(2.0 * math.pi))


def normalize(value):
    center = jnp.mean(value, axis=-1, keepdims=True)
    centered = value - center
    spread = jnp.mean(centered * centered, axis=-1, keepdims=True)
    inverse = lax.rsqrt(spread + norm_eps)
    return centered * inverse, inverse


def norm_back(grad, normed, inverse, gain):
    scaled = grad * gain
    return inverse * (
        scaled
        - jnp.mean(scaled, axis=-1, keepdims=True)
        - normed * jnp.mean(scaled * normed, axis=-1, keepdims=True)
    )


def lane_masks(rows=1):
    lane = lax.broadcasted_iota(jnp.int32, (rows, PAIR), 1)
    low = jnp.where(lane < 64, 1.0, 0.0)
    return low.astype(bf16), (1.0 - low).astype(bf16)


class Refs:
    pass


def fill_bias(m, known):
    tokens = m.key_bias.shape[0]
    row = lax.broadcasted_iota(jnp.int32, (tokens, PAIR), 0)
    lane = lax.broadcasted_iota(jnp.int32, (tokens, PAIR), 1)
    m.key_bias[...] = jnp.where((lane == 0) & (row >= known), NEG, 0.0).astype(bf16)


def project_one(m, layer, place, xb):
    tokens = xb.shape[0]
    scale = LOG2E / 8.0

    def block(index, carry):
        rows = pl.ds(pl.multiple_of(index * 2 * RB, 2 * RB), 2 * RB)
        value = dot(xb[rows, :], m.mat(layer, place))
        if place == 0:
            m.q[layer, rows, :] = ((value + m.vec(layer, 0)) * scale).astype(bf16)
        elif place == 1:
            m.k[layer, rows, :] = value.astype(bf16)
        else:
            m.v[layer, rows, :] = (value + m.vec(layer, 1)).astype(bf16)
        return carry

    lax.fori_loop(0, tokens // (2 * RB), block, 0)


def project(m, layer, xb):
    tokens = xb.shape[0]
    scale = LOG2E / 8.0

    def block(index, carry):
        rows = pl.ds(pl.multiple_of(index * 2 * RB, 2 * RB), 2 * RB)
        low = xb[rows, :]
        m.q[layer, rows, :] = ((dot(low, m.mat(layer, 0)) + m.vec(layer, 0)) * scale).astype(bf16)
        m.k[layer, rows, :] = dot(low, m.mat(layer, 1)).astype(bf16)
        m.v[layer, rows, :] = (dot(low, m.mat(layer, 2)) + m.vec(layer, 1)).astype(bf16)
        return carry

    lax.fori_loop(0, tokens // (2 * RB), block, 0)


def probs_copy(m, layer, pair, slot, out):
    here, there = m.probs.at[slot], m.probs_hbm.at[layer, pair]
    if out:
        return pltpu.make_async_copy(here, there, m.probs_sem.at[slot])
    return pltpu.make_async_copy(there, here, m.probs_sem.at[slot])


def attend(m, layer, known, hook=None):
    tokens, width = m.q.shape[1:]
    pairs = width // PAIR
    masks = lane_masks()
    lane = lax.broadcasted_iota(jnp.int32, (RB, PAIR), 1)
    ones_lane = jnp.where(lane == 0, 1.0, 0.0).astype(bf16)
    eye = lax.broadcasted_iota(jnp.int32, (RB, RB), 0) == lax.broadcasted_iota(jnp.int32, (RB, RB), 1)
    col = lax.broadcasted_iota(jnp.int32, (1, RB), 1)
    blocks = tokens // RB

    def one_pair(pair, carry):
        if hook is not None:
            hook(pair)
        slot = lax.rem(pair, 2)
        cols = pl.ds(pl.multiple_of(pair * PAIR, PAIR), PAIR)

        @pl.when(pair >= 2)
        def _():
            probs_copy(m, layer, pair - 2, slot, True).wait()

        keys = m.k[layer, :, cols]
        keys_wide = jnp.concatenate([keys, m.key_bias[...]], axis=1)
        values = m.v[layer, :, cols]
        mixed = []
        for head in range(2):
            for block in range(blocks):
                rows = slice(block * RB, (block + 1) * RB)
                query = m.q[layer, rows, cols] * masks[head]
                query_wide = jnp.concatenate([query, ones_lane], axis=1)
                parts = []
                for other in range(blocks):
                    keys_rows = slice(other * RB, (other + 1) * RB)
                    if other == block:
                        part = dot_nt(query, keys[keys_rows])
                        hidden = jnp.where(col + block * RB >= known, NEG, 0.0)
                        part = jnp.where(eye, part, part + hidden)
                    else:
                        part = dot_nt(query_wide, keys_wide[keys_rows])
                    parts.append(part)
                scores = jnp.concatenate(parts, axis=1)
                peak = jnp.max(scores, axis=1, keepdims=True)
                m.probs[slot, head, rows, :] = jnp.exp2(scores - peak).astype(bf16)
            values_wide = values * masks[head] + masks[1 - head]
            mixed.append(dot(m.probs[slot, head], values_wide))
        probs_copy(m, layer, pair, slot, True).start()
        low = lax.broadcasted_iota(jnp.int32, (tokens, PAIR), 1) < 64
        raw = jnp.where(low, mixed[0], mixed[1])
        total = pltpu.roll(jnp.where(low, mixed[1], mixed[0]), 64, 1)
        inverse = 1.0 / total
        m.inv_total[layer, :, cols] = inverse.astype(bf16)
        mean = raw * inverse
        high = mean.astype(bf16)
        m.o[layer, :, cols] = high
        m.o_low[layer, :, cols] = (mean - high.astype(f32)).astype(bf16)
        return carry

    lax.fori_loop(0, pairs, one_pair, 0)
    for pair in (pairs - 2, pairs - 1):
        probs_copy(m, layer, pair, pair % 2, True).wait()


def feed_forward(m, layer, x_of, y_to):
    tokens = m.q.shape[1]

    def block(index, carry):
        rows = pl.ds(pl.multiple_of(index * RB, RB), RB)
        branch = dot(m.o[layer, rows, :], m.mat(layer, 3)) + m.vec(layer, 2)
        normed, inverse = normalize(x_of(rows) + branch)
        m.n1[layer, rows, :] = normed.astype(bf16)
        m.inv[rows, 2 * layer : 2 * layer + 1] = inverse
        first = normed * m.vec(layer, 5) + m.vec(layer, 6)
        pre = dot(first.astype(bf16), m.mat(layer, 4)) + m.vec(layer, 3)
        hidden, slope = gelu_parts(pre)
        low = hidden.astype(bf16)
        m.r[layer, rows, :] = low
        m.slope[layer, rows, :] = slope.astype(bf16)
        feed = dot(low, m.mat(layer, 5)) + m.vec(layer, 4)
        normed, inverse = normalize(first + feed)
        m.n2[layer, rows, :] = normed.astype(bf16)
        m.inv[rows, 2 * layer + 1 : 2 * layer + 2] = inverse
        y_to(rows, normed * m.vec(layer, 7) + m.vec(layer, 8))
        return carry

    lax.fori_loop(0, tokens // RB, block, 0)


def column_sum(value):
    rows, width = value.shape
    return jnp.sum(value.reshape(rows // 8, 8, width), axis=0)


def rows_back(m, layer, hook=None, ready=None):
    tokens = m.q.shape[1]
    for row in range(8):
        m.sums[row] = jnp.zeros_like(m.sums[row])

    def block(index, carry):
        if hook is not None:
            hook(index)
        rows = pl.ds(pl.multiple_of(index * RB, RB), RB)
        grad = m.g[rows, :]
        normed = m.n2[layer, rows, :].astype(f32)
        m.sums[0] += column_sum(grad * normed)
        m.sums[1] += column_sum(grad)
        back = norm_back(grad, normed, m.inv[rows, 2 * layer + 1 : 2 * layer + 2], m.vec(layer, 7))
        m.sums[2] += column_sum(back)
        low = back.astype(bf16)
        m.n2[layer, rows, :] = low
        pre = dot_nt(low, m.mat(layer, 5)) * m.slope[layer, rows, :].astype(f32)
        m.sums[3] += column_sum(pre)
        low = pre.astype(bf16)
        m.du[rows, :] = low
        grad = back + dot_nt(low, m.mat(layer, 4))
        normed = m.n1[layer, rows, :].astype(f32)
        m.sums[4] += column_sum(grad * normed)
        m.sums[5] += column_sum(grad)
        back = norm_back(grad, normed, m.inv[rows, 2 * layer : 2 * layer + 1], m.vec(layer, 5))
        m.sums[6] += column_sum(back)
        m.g[rows, :] = back
        low = back.astype(bf16)
        m.n1[layer, rows, :] = low
        m.inv_total[layer, rows, :] = (dot_nt(low, m.mat(layer, 3)) * m.inv_total[layer, rows, :].astype(f32)).astype(bf16)
        first = normed * m.vec(layer, 5) + m.vec(layer, 6)
        m.slope[layer, rows, :] = first.astype(bf16)
        return carry

    lax.fori_loop(0, tokens // RB, block, 0)
    for row, place in ((0, 7), (1, 8), (2, 4), (3, 3), (4, 5), (5, 6), (6, 2)):
        m.grad_vec(layer, place, jnp.sum(m.sums[row], axis=0, keepdims=True))
    if ready is not None:
        ready()
    m.grad_mat(layer, 5, dot_tn(m.r[layer], m.n2[layer]))
    m.grad_mat(layer, 4, dot_tn(m.slope[layer], m.du[...]))
    m.grad_mat(layer, 3, dot_tn(m.o[layer], m.n1[layer]))


def attend_back(m, layer, hook=None, xb=None):
    tokens, width = m.q.shape[1:]
    pairs = width // PAIR
    masks = lane_masks()
    blocks = tokens // RB

    def one_pair(pair, carry):
        slot = lax.rem(pair, 2)
        cols = pl.ds(pl.multiple_of(pair * PAIR, PAIR), PAIR)
        probs_copy(m, layer, pair, slot, False).wait()

        @pl.when(pair + 1 < pairs)
        def _():
            probs_copy(m, layer, pair + 1, 1 - slot, False).start()

        grad = m.inv_total[layer, :, cols]
        turned = pltpu.roll(
            grad.astype(f32) * (m.o[layer, :, cols].astype(f32) + m.o_low[layer, :, cols].astype(f32)), 64, 1
        )
        turned_high = turned.astype(bf16)
        turned_low = (turned - turned_high.astype(f32)).astype(bf16)
        values = m.v[layer, :, cols]
        keys = m.k[layer, :, cols]
        query_turned = m.q[layer, :, cols].T
        grad_turned = grad.T
        grad_query, grad_keys, grad_values = [], [], []
        for head in range(2):
            part = slice(head * 64, (head + 1) * 64)
            wide = jnp.concatenate(
                [grad * masks[head] - turned_high * masks[1 - head], -turned_low * masks[1 - head]], axis=1
            )
            values_wide = jnp.concatenate(
                [values * masks[head] + masks[1 - head], jnp.broadcast_to(masks[1 - head], values.shape)], axis=1
            )
            grad_values.append(dot(grad_turned[part], m.probs[slot, head]))
            for block in range(blocks):
                rows = slice(block * RB, (block + 1) * RB)
                score = dot_nt(wide[rows], values_wide)
                m.probs[slot, head, rows, :] = (score * m.probs[slot, head, rows, :].astype(f32)).astype(bf16)
            grad_keys.append(dot(query_turned[part], m.probs[slot, head]))
            grad_query.append(dot(m.probs[slot, head], keys))
            if hook is not None and head == 0:
                hook(pair, 0)
        low = lax.broadcasted_iota(jnp.int32, (tokens, PAIR), 1) < 64
        back_query = (jnp.where(low, grad_query[0], grad_query[1]) * 0.125).astype(bf16)
        back_keys = (jnp.concatenate(grad_keys, axis=0) * LN2).astype(bf16)
        back_values = jnp.concatenate(grad_values, axis=0).astype(bf16)
        m.q[layer, :, cols] = back_query
        m.k[layer, :, cols] = back_keys.T
        m.v[layer, :, cols] = back_values.T
        if xb is not None:
            m.grad_pair(layer, pair, dot(jnp.concatenate([back_query.T, back_keys, back_values], axis=0), xb[...]))
        if hook is not None:
            hook(pair, 1)
        return carry

    lax.fori_loop(0, pairs, one_pair, 0)


def project_back(m, layer, xb=None, ready=None, hook=None):
    tokens = m.q.shape[1]
    ones = jnp.ones((8, tokens), bf16)
    m.grad_vec(layer, 0, dot(ones, m.q[layer])[0:1])
    m.grad_vec(layer, 1, dot(ones, m.v[layer])[0:1])
    if xb is not None:
        m.grad_mat(layer, 0, dot_tn(xb[...], m.q[layer]))
        m.grad_mat(layer, 1, dot_tn(xb[...], m.k[layer]))
        m.grad_mat(layer, 2, dot_tn(xb[...], m.v[layer]))
    if ready is not None:
        ready()

    def block(index, carry):
        if hook is not None:
            hook(index)
        rows = pl.ds(pl.multiple_of(index * RB, RB), RB)
        m.g[rows, :] = (
            m.g[rows, :]
            + dot_nt(m.q[layer, rows, :], m.mat(layer, 0))
            + dot_nt(m.k[layer, rows, :], m.mat(layer, 1))
            + dot_nt(m.v[layer, rows, :], m.mat(layer, 2))
        )
        return carry

    lax.fori_loop(0, tokens // RB, block, 0)


def start_refs(q, k, v, o, o_low, inv_total, n1, n2, inv, r, slope, g, x1, du, sums, key_bias,
               probs, probs_sem, probs_hbm):
    m = Refs()
    m.q, m.k, m.v, m.o, m.o_low, m.inv_total = q, k, v, o, o_low, inv_total
    m.n1, m.n2, m.inv, m.r, m.slope, m.g, m.x1 = n1, n2, inv, r, slope, g, x1
    m.du, m.sums, m.key_bias = du, sums, key_bias
    m.probs, m.probs_sem, m.probs_hbm = probs, probs_sem, probs_hbm
    return m


def shared_scratch(layers, count, width):
    both = (layers, count, width)
    one = (count, width)
    return [
        pltpu.VMEM(both, bf16), pltpu.VMEM(both, bf16), pltpu.VMEM(both, bf16), pltpu.VMEM(both, bf16),
        pltpu.VMEM(both, bf16), pltpu.VMEM(both, bf16), pltpu.VMEM(both, bf16), pltpu.VMEM(both, bf16),
        pltpu.VMEM((count, 2 * layers), f32),
        pltpu.VMEM(both, bf16), pltpu.VMEM(both, bf16),
        pltpu.VMEM(one, f32), pltpu.VMEM(one, bf16),
        pltpu.VMEM(one, bf16),
        pltpu.VMEM((8, 8, width), f32),
        pltpu.VMEM((count, PAIR), bf16),
        pltpu.VMEM((2, 2, count, count), bf16),
        pltpu.SemaphoreType.DMA((2,)),
    ]


SHARED = 18


def plain_kernel(length_ref, class_ref, x_ref, cot_ref, w_ref, vec_ref, act_ref, dx_ref, mats_ref, vecs_ref, probs_hbm, *rest):
    m = start_refs(*rest[:SHARED], probs_hbm)
    out_sem = rest[SHARED]
    m.mat = lambda layer, place: w_ref[layer, place]
    m.vec = lambda layer, place: vec_ref[layer, place : place + 1, :]

    def grad_mat(layer, place, value):
        mats_ref[layer, place] = value.astype(bf16)

    def grad_vec(layer, place, value):
        vecs_ref[layer, place : place + 1, :] = value

    m.grad_mat, m.grad_vec = grad_mat, grad_vec
    length, klass = length_ref[0], class_ref[0]
    known = jnp.where(klass == 0, length, (length + 1) // 2)
    fill_bias(m, known)
    project(m, 0, x_ref)
    attend(m, 0, known)

    def keep_next(rows, value):
        m.g[rows, :] = value
        m.x1[rows, :] = value.astype(bf16)

    feed_forward(m, 0, lambda rows: x_ref[rows, :].astype(f32), keep_next)
    project(m, 1, m.x1)
    attend(m, 1, known)
    probs_copy(m, 1, 0, 0, False).start()

    def finish(rows, value):
        valid = lax.broadcasted_iota(jnp.int32, (RB, 1), 0) + rows.start < length
        act_ref[rows, :] = jnp.where(valid, value, 0.0).astype(bf16)
        m.g[rows, :] = jnp.where(valid, cot_ref[rows, :].astype(f32), 0.0)

    feed_forward(m, 1, lambda rows: m.g[rows, :], finish)
    for layer, xb in ((1, m.x1), (0, x_ref)):
        rows_back(m, layer)
        attend_back(m, layer)
        if layer:
            probs_copy(m, layer - 1, 0, 0, False).start()
        project_back(m, layer, xb)
    copy = pltpu.make_async_copy(m.g, dx_ref, out_sem)
    copy.start()
    copy.wait()


def plain_pass(lengths, classes, tokens, cotangent, mats, vecs):
    count, width = tokens.shape
    layers = mats.shape[0]
    vmem = pl.BlockSpec(memory_space=pltpu.VMEM)
    smem = pl.BlockSpec(memory_space=pltpu.SMEM)
    hbm = pl.BlockSpec(memory_space=pl.ANY)
    outs = pl.pallas_call(
        plain_kernel,
        out_shape=[
            jax.ShapeDtypeStruct((count, width), bf16),
            jax.ShapeDtypeStruct((count, width), f32),
            jax.ShapeDtypeStruct(mats.shape, bf16),
            jax.ShapeDtypeStruct((layers, 16, width), f32),
            jax.ShapeDtypeStruct((layers, width // PAIR, 2, count, count), bf16),
        ],
        in_specs=[smem, smem, vmem, vmem, vmem, vmem],
        out_specs=[vmem, hbm, vmem, vmem, hbm],
        scratch_shapes=shared_scratch(layers, count, width) + [pltpu.SemaphoreType.DMA],
        compiler_params=pltpu.CompilerParams(vmem_limit_bytes=67043328),
    )(lengths, classes, tokens, cotangent, mats, vecs)
    return outs[:4]


def adam_update(param, grad, first, second, rate):
    first_new = beta_first * first + (1.0 - beta_first) * grad
    second_new = beta_second * second + (1.0 - beta_second) * grad * grad
    first_hat = first_new * (1.0 / (1.0 - beta_first**adam_step))
    second_hat = second_new * (1.0 / (1.0 - beta_second**adam_step))
    param_new = param - rate * (first_hat / (jnp.sqrt(second_hat) + adam_eps) + decay_rate * param)
    return (param_new, first_new, second_new)


def plain_body(tokens, lengths, classes, cotangent, weights, vectors, first_weights, second_weights, first_vectors, second_vectors):
    mats = lax.all_gather(weights.astype(bf16), "shard", axis=2, tiled=True)
    vecs = lax.all_gather(vectors.astype(bf16), "shard", axis=2, tiled=True).astype(f32)
    vecs = jnp.pad(vecs, ((0, 0), (0, 16 - vecs.shape[1]), (0, 0)))
    activations, input_grad, grad_mats, grad_vecs = plain_pass(lengths, classes, tokens[0], cotangent[0], mats, vecs)
    grad_vecs = grad_vecs[:, : vectors.shape[1]]
    total_mats = lax.psum_scatter(grad_mats, "shard", scatter_dimension=2, tiled=True)
    total_vecs = lax.psum_scatter(grad_vecs.astype(bf16), "shard", scatter_dimension=2, tiled=True)
    total_mats = lax.psum(total_mats, "dp").astype(f32)
    total_vecs = lax.psum(total_vecs, "dp").astype(f32)
    new_weights, new_first_weights, new_second_weights = adam_update(
        weights, total_mats, first_weights, second_weights, learn_rate
    )
    new_vectors, new_first_vectors, new_second_vectors = adam_update(
        vectors, total_vecs, first_vectors, second_vectors, vector_rate
    )
    return (
        activations[None], input_grad[None], new_weights, new_weights.astype(bf16), new_first_weights, new_second_weights,
        new_vectors, new_first_vectors, new_second_vectors, total_vecs[:, 0],
    )


MESH = pl.DeviceIdType.MESH


def remote(src, dst, sems, place, device):
    return pltpu.make_async_remote_copy(
        src_ref=src, dst_ref=dst, send_sem=sems[0].at[place], recv_sem=sems[1].at[place], device_id=device, device_id_type=MESH
    )


class Spot:
    def __init__(self, planes, shards):
        self.planes, self.shards = planes, shards
        self.d, self.z = lax.axis_index("dp"), lax.axis_index("shard")
        self.c, self.t = lax.rem(self.d, 2), lax.div(self.d, 2)

    def plane(self, step):
        return lax.rem(self.t + step, self.planes)

    def shard(self, step):
        return lax.rem(self.z + step, self.shards)

    def sibling(self):
        return (self.t * 2 + 1 - self.c, self.z)


class Weights:
    def __init__(self, spot, w, layer, first, count, index, z_sems, p_sems, c_sems):
        self.spot, self.index = spot, index
        self.z_sems, self.p_sems, self.c_sems = z_sems, p_sems, c_sems
        self.view = w.at[layer, first : first + count]

    def z_copy(self, step):
        s = self.spot
        piece = self.view.at[:, s.z, s.t, s.c]
        return remote(piece, piece, self.z_sems, (self.index, step - 1), (s.d, s.shard(step)))

    def p_copy(self, z_step, t_step):
        s = self.spot
        piece = self.view.at[:, s.shard(s.shards - z_step), s.t, s.c]
        place = (self.index, z_step - 1, t_step - 1)
        return remote(piece, piece, self.p_sems, place, (s.plane(t_step) * 2 + s.c, s.z))

    def c_copy(self, z_step):
        s = self.spot
        piece = self.view.at[:, s.shard(s.shards - z_step), :, s.c]
        return remote(piece, piece, self.c_sems, (self.index, z_step - 1), s.sibling())

    def steps(self):
        return range(1, self.spot.shards)

    def send_z(self):
        for step in self.steps():
            self.z_copy(step).start()

    def send_p(self):
        for step in self.steps():
            self.z_copy(step).wait_recv()
            for other in range(1, self.spot.planes):
                self.p_copy(step, other).start()

    def send_c(self):
        for step in self.steps():
            for other in range(1, self.spot.planes):
                self.p_copy(step, other).wait_recv()
            self.c_copy(step).start()

    def arrive(self):
        for step in self.steps():
            self.c_copy(step).wait_recv()

    def close(self):
        for step in self.steps():
            self.z_copy(step).wait_send()
            self.c_copy(step).wait_send()
            for other in range(1, self.spot.planes):
                self.p_copy(step, other).wait_send()


class Piece:
    def __init__(self, spot, grads, from_core, from_plane, mine, from_shard, total, index, c_sems, p_sems, z_sems, a_sems, b_sems):
        self.spot, self.index = spot, index
        self.grads, self.from_core, self.from_plane = grads, from_core, from_plane
        self.mine, self.from_shard, self.total = mine, from_shard, total
        self.c_sems, self.p_sems, self.z_sems, self.a_sems, self.b_sems = c_sems, p_sems, z_sems, a_sems, b_sems

    def c_copy(self):
        s = self.spot
        return remote(self.grads.at[:, :, 1 - s.c], self.from_core, self.c_sems, (self.index,), s.sibling())

    def p_copy(self, step):
        s = self.spot
        other = s.plane(step)
        return remote(
            self.from_core.at[:, :, other], self.from_plane.at[step - 1], self.p_sems, (self.index, step - 1), (other * 2 + s.c, s.z)
        )

    def z_copy(self, step):
        s = self.spot
        other = s.shard(step)
        return remote(self.mine.at[:, other], self.from_shard.at[step - 1], self.z_sems, (self.index, step - 1), (s.d, other))

    def a_copy(self, step):
        s = self.spot
        part = self.total.at[:, s.c, s.t]
        return remote(part, part, self.a_sems, (self.index, step - 1), (s.plane(step) * 2 + s.c, s.z))

    def b_copy(self):
        s = self.spot
        part = self.total.at[:, s.c]
        return remote(part, part, self.b_sems, (self.index,), s.sibling())

    def send_c(self):
        self.c_copy().start()

    def send_p(self):
        s = self.spot
        self.c_copy().wait()
        for mat in range(self.grads.shape[0]):
            own = self.grads[mat, :, s.c].astype(f32)
            self.from_core[mat] = (self.from_core[mat].astype(f32) + own).astype(bf16)
        for step in range(1, s.planes):
            self.p_copy(step).start()

    def send_z(self):
        s = self.spot
        for step in range(1, s.planes):
            self.p_copy(step).wait_recv()
        total = self.from_core[:, :, s.t].astype(f32)
        for step in range(1, s.planes):
            total = total + self.from_plane[step - 1].astype(f32)
        self.mine[...] = total.astype(bf16)
        for step in range(1, s.shards):
            self.z_copy(step).start()

    def send_a(self):
        s = self.spot
        for step in range(1, s.shards):
            self.z_copy(step).wait_recv()
        total = self.mine[:, s.z].astype(f32)
        for step in range(1, s.shards):
            total = total + self.from_shard[step - 1].astype(f32)
        self.total[:, s.c, s.t] = total.astype(bf16)
        for step in range(1, s.planes):
            self.a_copy(step).start()

    def send_b(self):
        for step in range(1, self.spot.planes):
            self.a_copy(step).wait_recv()
        self.b_copy().start()

    def arrive(self):
        self.b_copy().wait_recv()

    def close(self):
        for step in range(1, self.spot.planes):
            self.p_copy(step).wait_send()
            self.a_copy(step).wait_send()
        for step in range(1, self.spot.shards):
            self.z_copy(step).wait_send()
        self.b_copy().wait_send()


def full_kernel(planes, shards,
                length_ref, class_ref, x_hbm, cot_hbm, w_hbm, vec_in, act_hbm, dx_hbm, tot_hbm, tot_vec, probs_hbm, *rest):
    m = start_refs(*rest[:SHARED], probs_hbm)
    (x_ref, w, vec_own, vec_all, grads, pair_grads, grad_vecs, grads_vec,
     core_in, plane_in, mine, shard_in, total,
     core_in_p, plane_in_p, mine_p, shard_in_p, total_p,
     core_in_v, plane_in_v, mine_v, shard_in_v, total_v,
     stage,
     x_sem, stage_sem, feed_sem, pair_sem, vec_sem, out_sem,
     vz0, vz1, wz0, wz1, wp0, wp1, wc0, wc1,
     gc0, gc1, gp0, gp1, gz0, gz1, ga0, ga1, gb0, gb1) = rest[SHARED:]
    spot = Spot(planes, shards)
    tokens, width = x_ref.shape
    layers = w.shape[0]
    share = width // shards

    def mat(layer, place):
        return w[layer, place].reshape(width, width)

    m.mat = mat
    m.vec = lambda layer, place: vec_all[layer, place : place + 1, :]

    def grad_mat(layer, place, value):
        grads[place - 3] = value.astype(bf16).reshape(grads.shape[1:])

    def grad_pair(layer, pair, value):
        turned = value.astype(bf16).T
        for place in range(3):
            part = turned[:, place * PAIR : (place + 1) * PAIR]
            pair_grads[pair, place] = part.reshape(pair_grads.shape[2:])

    def grad_vec(layer, place, value):
        grad_vecs[layer, place : place + 1, :] = value

    m.grad_mat, m.grad_vec, m.grad_pair = grad_mat, grad_vec, grad_pair

    groups = [
        Weights(spot, w, layer, first, count, index, (wz0, wz1), (wp0, wp1), (wc0, wc1))
        for index, (layer, first, count) in enumerate(((0, 0, 1), (0, 1, 1), (0, 2, 1), (0, 3, 3), (1, 0, 3), (1, 3, 3)))
    ]
    sems = ((gc0, gc1), (gp0, gp1), (gz0, gz1), (ga0, ga1), (gb0, gb1))

    pairs = width // PAIR

    def feed_piece(layer):
        i = layers - 1 - layer
        return Piece(spot, grads, core_in.at[i], plane_in.at[i], mine.at[i], shard_in.at[i], total.at[i], i, *sems)

    def pair_piece(layer, pair):
        i = (layers - 1 - layer) * pairs + pair
        return Piece(spot, pair_grads.at[pair], core_in_p.at[i], plane_in_p.at[i], mine_p.at[i], shard_in_p.at[i],
                     total_p.at[i], layers + i, *sems)

    def feed_out(layer):
        i = layers - 1 - layer
        return pltpu.make_async_copy(total.at[i], tot_hbm.at[layer, 3:6], feed_sem.at[i])

    def pair_out(layer, pair):
        i = (layers - 1 - layer) * pairs + pair
        cols = pl.ds(pl.multiple_of(pair * PAIR, PAIR), PAIR)
        return pltpu.make_async_copy(total_p.at[i], tot_hbm.at[layer, 0:3, :, :, :, cols], pair_sem.at[i])

    feed1, feed0 = feed_piece(1), feed_piece(0)
    vecs = Piece(spot, grads_vec, core_in_v, plane_in_v, mine_v, shard_in_v, total_v, layers * (pairs + 1), *sems)

    x_copy = pltpu.make_async_copy(x_hbm, x_ref, x_sem.at[0])
    cot_copy = pltpu.make_async_copy(cot_hbm, m.du, x_sem.at[1])
    stages = [
        pltpu.make_async_copy(w_hbm.at[g // 2, 3 * (g % 2) : 3 * (g % 2) + 3], stage.at[g], stage_sem.at[g])
        for g in range(4)
    ]
    for copy in stages:
        copy.start()
    x_copy.start()
    cot_copy.start()

    barrier = pltpu.get_barrier_semaphore()
    for step in range(1, 2 * planes):
        pl.semaphore_signal(barrier, inc=1, device_id=(lax.rem(spot.d + step, 2 * planes), spot.z), device_id_type=MESH)
    for step in range(1, shards):
        pl.semaphore_signal(barrier, inc=1, device_id=(spot.d, spot.shard(step)), device_id_type=MESH)

    def cast(g):
        stages[g].wait()
        for place in range(3):
            low = stage[g, place].astype(bf16)
            w[g // 2, 3 * (g % 2) + place, spot.z] = low.reshape(w.shape[3:])

    cast(0)
    vec_all[...] = jnp.zeros_like(vec_all)
    for layer in range(layers):
        for place in range(vec_in.shape[0]):
            vec_all[layer, place : place + 1, 0:share] = vec_in[place, layer : layer + 1, :]
        vec_own[spot.z, layer] = vec_all[layer, :, 0:share].astype(bf16)
    pl.semaphore_wait(barrier, 2 * planes - 1 + shards - 1)
    for g in range(3):
        groups[g].send_z()

    def v_copy(step):
        part = vec_own.at[spot.z]
        return remote(part, part, (vz0, vz1), (step - 1,), (spot.d, spot.shard(step)))

    for step in range(1, shards):
        v_copy(step).start()
    for g in range(1, 4):
        cast(g)
    length, klass = length_ref[0], class_ref[0]
    known = jnp.where(klass == 0, length, (length + 1) // 2)
    fill_bias(m, known)
    grad_vecs[...] = jnp.zeros_like(grad_vecs)
    grads_vec[...] = jnp.zeros_like(grads_vec)

    groups[0].send_p()
    groups[1].send_p()
    groups[0].send_c()
    groups[2].send_p()
    groups[1].send_c()
    groups[3].send_z()
    groups[2].send_c()
    for step in range(1, shards):
        v_copy(step).wait_recv()
    for other in range(shards):
        vec_all[:, :, other * share : (other + 1) * share] = vec_own[other].astype(f32)
    x_copy.wait()
    for place in range(3):
        groups[place].arrive()
        project_one(m, 0, place, x_ref)
    groups[3].send_p()
    groups[4].send_z()

    def on(index, value, action):
        pl.when(index == value)(action)

    def hook_forward(pair):
        def first():
            groups[3].send_c()
            groups[4].send_p()

        def third():
            groups[4].send_c()
            groups[5].send_p()

        on(pair, 1, first)
        on(pair, 2, groups[5].send_z)
        on(pair, 3, third)

    attend(m, 0, known, hook_forward)

    def keep_next(rows, value):
        m.g[rows, :] = value
        m.x1[rows, :] = value.astype(bf16)

    groups[3].arrive()
    feed_forward(m, 0, lambda rows: x_ref[rows, :].astype(f32), keep_next)
    groups[5].send_c()
    groups[4].arrive()
    project(m, 1, m.x1)
    attend(m, 1, known)
    probs_copy(m, 1, 0, 0, False).start()
    cot_copy.wait()

    def finish(rows, value):
        valid = lax.broadcasted_iota(jnp.int32, (RB, 1), 0) + rows.start < length
        m.probs[1, 0, rows, 0:width] = jnp.where(valid, value, 0.0).astype(bf16)
        m.g[rows, :] = jnp.where(valid, m.du[rows, :].astype(f32), 0.0)

    groups[5].arrive()
    feed_forward(m, 1, lambda rows: m.g[rows, :], finish)
    act_copy = pltpu.make_async_copy(m.probs.at[1, 0, :, 0:width], act_hbm, x_sem.at[2])
    act_copy.start()

    rows_back(m, 1)
    feed1.send_c()
    act_copy.wait()

    def hook_of(layer, feed):
        def hook(pair, place):
            if place == 0:
                on(pair, 0, feed.send_p)
                pl.when(pair >= 1)(pair_piece(layer, pair - 1).send_p)
                on(pair, 2, feed.send_z)
                pl.when(pair >= 2)(pair_piece(layer, pair - 2).send_z)
                pl.when(pair >= 3)(pair_piece(layer, pair - 3).send_a)
                if layer == 0:
                    on(pair, 0, feed1.send_b)
            else:
                pair_piece(layer, pair).send_c()
                on(pair, 3, feed.send_a)
                if layer == 0:
                    pair_piece(1, pair).send_b()

        return hook

    last = pairs - 1
    attend_back(m, 1, hook_of(1, feed1), m.x1)
    probs_copy(m, 0, 0, 0, False).start()

    def hook_dx1(index):
        def second():
            pair_piece(1, last).send_p()
            pair_piece(1, last - 1).send_z()
            pair_piece(1, last - 2).send_a()

        on(index, 2, second)

    project_back(m, 1, hook=hook_dx1)

    def hook_rows(index):
        def first():
            pair_piece(1, last).send_z()
            pair_piece(1, last - 1).send_a()

        on(index, 1, first)
        on(index, 3, pair_piece(1, last).send_a)

    rows_back(m, 0, hook_rows)
    feed0.send_c()
    attend_back(m, 0, hook_of(0, feed0), x_ref)

    def ready_last():
        for layer in range(layers):
            for other in range(shards):
                part = grad_vecs[layer, :, other * share : (other + 1) * share]
                grads_vec[0, other, layer, 0] = part.astype(bf16)
        vecs.send_c()

    def hook_dx0(index):
        def first():
            vecs.send_p()
            pair_piece(0, last - 1).send_z()
            pair_piece(0, last - 2).send_a()

        def third():
            pair_piece(0, last).send_z()
            vecs.send_z()
            pair_piece(0, last - 1).send_a()

        on(index, 0, pair_piece(0, last).send_p)
        on(index, 1, first)
        on(index, 3, third)

    project_back(m, 0, ready=ready_last, hook=hook_dx0)
    dx_copy = pltpu.make_async_copy(m.g, dx_hbm, out_sem)
    dx_copy.start()
    feed0.send_b()
    pair_piece(0, 0).send_b()
    pair_piece(0, last).send_a()
    vecs.send_a()
    for pair in range(1, last):
        pair_piece(0, pair).send_b()
    pair_piece(0, last).send_b()
    vecs.send_b()
    for layer, feed in ((1, feed1), (0, feed0)):
        feed.arrive()
        feed_out(layer).start()
        for pair in range(pairs):
            pair_piece(layer, pair).arrive()
            pair_out(layer, pair).start()
    vecs.arrive()
    vec_copy = pltpu.make_async_copy(total_v.at[0, :, 0], tot_vec, vec_sem)
    vec_copy.start()
    for group in groups:
        group.close()
    for step in range(1, shards):
        v_copy(step).wait_send()
    for layer, feed in ((1, feed1), (0, feed0)):
        feed.close()
        for pair in range(pairs):
            pair_piece(layer, pair).close()
    vecs.close()
    for layer in (1, 0):
        feed_out(layer).wait()
        for pair in range(pairs):
            pair_out(layer, pair).wait()
    vec_copy.wait()
    dx_copy.wait()


CHUNKS = 6


def last_kernel(act_in, dx_in, total_in, w_in, first_in, second_in, tot_vec, vec_ref, vec_first, vec_second,
                act_out, dx_out, new_w, low_w, new_first, new_second, vec_out, first_out, second_out, query_out,
                act, dx, total, w, first, second, low, token_load, token_store, loads, stores):
    rows = w.shape[0] // CHUNKS

    def piece(chunk):
        return pl.ds(pl.multiple_of(chunk * rows, rows), rows)

    def load(chunk):
        part = piece(chunk)
        return [
            pltpu.make_async_copy(source.at[part], here.at[part], loads.at[which, chunk])
            for which, (source, here) in enumerate(((w_in, w), (total_in, total), (first_in, first), (second_in, second)))
        ]

    def store(chunk):
        part = piece(chunk)
        return [
            pltpu.make_async_copy(here.at[part], target.at[part], stores.at[which, chunk])
            for which, (here, target) in enumerate(((w, new_w), (low, low_w), (first, new_first), (second, new_second)))
        ]

    ins = [pltpu.make_async_copy(dx_in, dx, token_load.at[0]), pltpu.make_async_copy(act_in, act, token_load.at[1])]
    outs = [pltpu.make_async_copy(dx, dx_out, token_store.at[0]), pltpu.make_async_copy(act, act_out, token_store.at[1])]
    for copy in load(0) + ins:
        copy.start()
    for chunk in range(1, CHUNKS):
        for copy in load(chunk):
            copy.start()

    def one(chunk, carry):
        for copy in load(chunk):
            copy.wait()

        def block(index, inner):
            part = pl.ds(pl.multiple_of(chunk * rows + index * 16, 16), 16)
            param, one_moment, two_moment = adam_update(
                w[part, :], total[part, :].astype(f32), first[part, :], second[part, :], learn_rate
            )
            w[part, :] = param
            low[part, :] = param.astype(bf16)
            first[part, :] = one_moment
            second[part, :] = two_moment
            return inner

        lax.fori_loop(0, rows // 16, block, 0)
        for copy in store(chunk):
            copy.start()
        for which in range(2):

            @pl.when(chunk == which)
            def _():
                ins[which].wait()
                outs[which].start()

        return carry

    lax.fori_loop(0, CHUNKS, one, 0)
    count, layers = vec_ref.shape[:2]
    for layer in range(layers):
        grads = tot_vec[layer].astype(f32)
        for place in range(count):
            one = slice(layer, layer + 1)
            grad = grads[place : place + 1]
            param, one_moment, two_moment = adam_update(
                vec_ref[place, one, :], grad, vec_first[place, one, :], vec_second[place, one, :], vector_rate
            )
            vec_out[place, one, :] = param
            first_out[place, one, :] = one_moment
            second_out[place, one, :] = two_moment
            if place == 0:
                query_out[one, :] = grad
    for copy in outs:
        copy.wait()
    for chunk in range(CHUNKS):
        for copy in store(chunk):
            copy.wait()


def finish_step(parts, weights, vectors, first_weights, second_weights, first_vectors, second_vectors):
    act, dx, total_mats, total_vecs = parts
    count, width = act.shape
    layers, places, share = vectors.shape
    flat = lambda value: value.reshape(-1, width)
    turned = lambda value: jnp.transpose(value, (1, 0, 2))
    mat_rows = weights.size // width
    hbm = pl.BlockSpec(memory_space=pl.ANY)
    vmem = pl.BlockSpec(memory_space=pltpu.VMEM)
    dma = pltpu.SemaphoreType.DMA
    shape = jax.ShapeDtypeStruct
    mat, low = (mat_rows, width), pltpu.VMEM((mat_rows, width), bf16)
    outs = pl.pallas_call(
        last_kernel,
        out_shape=[
            shape(act.shape, bf16), shape(dx.shape, f32), shape(mat, f32), shape(mat, bf16), shape(mat, f32), shape(mat, f32),
            shape((places, layers, share), f32), shape((places, layers, share), f32), shape((places, layers, share), f32),
            shape((layers, share), f32),
        ],
        in_specs=[hbm] * 6 + [vmem] * 4,
        out_specs=[hbm] * 6 + [vmem] * 4,
        scratch_shapes=[
            pltpu.VMEM(act.shape, bf16), pltpu.VMEM(dx.shape, f32), low, pltpu.VMEM(mat, f32), pltpu.VMEM(mat, f32),
            pltpu.VMEM(mat, f32), low, dma((2,)), dma((2,)), dma((4, CHUNKS)), dma((4, CHUNKS)),
        ],
        compiler_params=pltpu.CompilerParams(vmem_limit_bytes=67043328),
    )(act, dx, flat(total_mats), flat(weights), flat(first_weights), flat(second_weights), total_vecs,
      turned(vectors), turned(first_vectors), turned(second_vectors))
    mats = [value.reshape(weights.shape) for value in outs[2:6]]
    vecs = [turned(value) for value in outs[6:9]]
    return (outs[0][None], outs[1][None], *mats, *vecs, outs[9])


def full_body(planes, shards, tokens, lengths, classes, cotangent, weights, vectors, first_weights, second_weights, first_vectors,
              second_vectors):
    _, count, width = tokens.shape
    layers = weights.shape[0]
    rows = width // (2 * planes * shards)
    share = width // shards
    pairs = width // PAIR
    sent = layers * (pairs + 1) + 1
    vmem = pl.BlockSpec(memory_space=pltpu.VMEM)
    smem = pl.BlockSpec(memory_space=pltpu.SMEM)
    hbm = pl.BlockSpec(memory_space=pl.ANY)
    dma = pltpu.SemaphoreType.DMA

    def pieces(lead, mats, columns):
        return [
            pltpu.VMEM(lead + (mats, shards, planes, rows, columns), bf16),
            pltpu.VMEM(lead + (planes - 1, mats, shards, rows, columns), bf16),
            pltpu.VMEM(lead + (mats, shards, rows, columns), bf16),
            pltpu.VMEM(lead + (shards - 1, mats, rows, columns), bf16),
            pltpu.VMEM(lead + (mats, 2, planes, rows, columns), bf16),
        ]

    def twice(*shape):
        return [dma(shape), dma(shape)]

    scratch = shared_scratch(layers, count, width) + [
        pltpu.VMEM((count, width), bf16),
        pltpu.VMEM((layers, 6, shards, planes, 2, rows, width), bf16),
        pltpu.VMEM((shards, layers, 16, share), bf16),
        pltpu.VMEM((layers, 16, width), f32),
        pltpu.VMEM((3, shards, 2, planes, rows, width), bf16),
        pltpu.VMEM((pairs, 3, shards, 2, planes, rows, PAIR), bf16),
        pltpu.VMEM((layers, 16, width), f32),
        pltpu.VMEM((1, shards, 2, planes, rows, share), bf16),
        *pieces((layers,), 3, width),
        *pieces((layers * pairs,), 3, PAIR),
        *pieces((), 1, share),
        pltpu.VMEM((4, 3, share, width), f32),
        dma((3,)), dma((4,)), dma((layers,)), dma((layers * pairs,)), dma, dma,
        *twice(shards - 1),
        *twice(6, shards - 1), *twice(6, shards - 1, planes - 1), *twice(6, shards - 1),
        *twice(sent), *twice(sent, planes - 1), *twice(sent, shards - 1), *twice(sent, planes - 1), *twice(sent),
    ]
    shape = jax.ShapeDtypeStruct
    outs = pl.pallas_call(
        functools.partial(full_kernel, planes, shards),
        out_shape=[
            shape((count, width), bf16), shape((count, width), f32), shape((layers, 6, 2, planes, rows, width), bf16),
            shape((layers, rows, share), bf16), shape((layers, pairs, 2, count, count), bf16),
        ],
        in_specs=[smem, smem] + [hbm] * 3 + [vmem],
        out_specs=[hbm] * 5,
        scratch_shapes=scratch,
        compiler_params=pltpu.CompilerParams(vmem_limit_bytes=67043328, collective_id=0, has_side_effects=True),
    )(lengths, classes, tokens[0], cotangent[0], weights, jnp.transpose(vectors, (1, 0, 2)))
    return finish_step(outs[:4], weights, vectors, first_weights, second_weights, first_vectors, second_vectors)


def solution(mesh):
    devices, shards = mesh.shape["dp"], mesh.shape["shard"]

    def body(*args):
        width = args[0].shape[-1]
        layers = args[4].shape[0]
        rows, left = divmod(width, devices * shards)
        if devices % 2 == 0 and devices > 2 and shards > 1 and left == 0 and rows == 16 and layers == 2 and width // shards % PAIR == 0:
            return full_body(devices // 2, shards, *args)
        return plain_body(*args)

    cell = P(("dp", "shard"), None, None)
    mats = P(None, None, "shard", None)
    vecs = P(None, None, "shard")
    one = P(("dp", "shard"))
    in_specs = (cell, one, one, cell, mats, vecs, mats, mats, vecs, vecs)
    out_specs = (cell, cell, mats, mats, mats, mats, vecs, vecs, vecs, P(None, "shard"))
    return jax.shard_map(body, mesh=mesh, in_specs=in_specs, out_specs=out_specs, check_vma=False)
```

```python
import functools
import math

import jax
import jax.numpy as jnp
from jax import lax
from jax.experimental import pallas as pl
from jax.experimental.pallas import tpu as pltpu
from jax.sharding import PartitionSpec as P

HEADS = 8
beta_first = 0.5
beta_second = 0.55
learn_rate = 0.05
vector_rate = 0.25
decay_rate = 0.01
adam_eps = 1e-08
adam_step = 3.0
norm_eps = 1e-05

LOG2E = 1.4426950408889634
LN2 = 0.6931471805599453
NEG = -1e30
f32 = jnp.float32
bf16 = jnp.bfloat16
PAIR = 128
RB = 256


def dot(left, right):
    return jnp.dot(left, right, preferred_element_type=f32)


def dot_nt(left, right):
    return lax.dot_general(left, right, (((1,), (1,)), ((), ())), preferred_element_type=f32)


def dot_tn(left, right):
    return lax.dot_general(left, right, (((0,), (0,)), ((), ())), preferred_element_type=f32)


def gelu_parts(value):
    size = jnp.abs(value) * (1.0 / math.sqrt(2.0))
    step = 1.0 / (1.0 + 0.3275911 * size)
    bell = jnp.exp2(value * value * (-0.5 * LOG2E))
    poly = step * (0.254829592 + step * (-0.284496736 + step * (1.421413741 + step * (-1.453152027 + step * 1.061405429))))
    tail = 0.5 * poly * bell
    below = jnp.where(value < 0.0, tail, 1.0 - tail)
    return value * below, below + value * bell * (1.0 / math.sqrt(2.0 * math.pi))


def normalize(value):
    center = jnp.mean(value, axis=-1, keepdims=True)
    centered = value - center
    spread = jnp.mean(centered * centered, axis=-1, keepdims=True)
    inverse = lax.rsqrt(spread + norm_eps)
    return centered * inverse, inverse


def norm_back(grad, normed, inverse, gain):
    scaled = grad * gain
    return inverse * (
        scaled
        - jnp.mean(scaled, axis=-1, keepdims=True)
        - normed * jnp.mean(scaled * normed, axis=-1, keepdims=True)
    )


def lane_masks(rows=1):
    lane = lax.broadcasted_iota(jnp.int32, (rows, PAIR), 1)
    low = jnp.where(lane < 64, 1.0, 0.0)
    return low.astype(bf16), (1.0 - low).astype(bf16)


class Refs:
    pass


def fill_bias(m, known):
    tokens = m.key_bias.shape[0]
    row = lax.broadcasted_iota(jnp.int32, (tokens, PAIR), 0)
    lane = lax.broadcasted_iota(jnp.int32, (tokens, PAIR), 1)
    m.key_bias[...] = jnp.where((lane == 0) & (row >= known), NEG, 0.0).astype(bf16)


def project_one(m, layer, place, xb):
    tokens = xb.shape[0]
    scale = LOG2E / 8.0

    def block(index, carry):
        rows = pl.ds(pl.multiple_of(index * 2 * RB, 2 * RB), 2 * RB)
        value = dot(xb[rows, :], m.mat(layer, place))
        if place == 0:
            m.q[layer, rows, :] = ((value + m.vec(layer, 0)) * scale).astype(bf16)
        elif place == 1:
            m.k[layer, rows, :] = value.astype(bf16)
        else:
            m.v[layer, rows, :] = (value + m.vec(layer, 1)).astype(bf16)
        return carry

    lax.fori_loop(0, tokens // (2 * RB), block, 0)


def project(m, layer, xb):
    tokens = xb.shape[0]
    scale = LOG2E / 8.0

    def block(index, carry):
        rows = pl.ds(pl.multiple_of(index * 2 * RB, 2 * RB), 2 * RB)
        low = xb[rows, :]
        m.q[layer, rows, :] = ((dot(low, m.mat(layer, 0)) + m.vec(layer, 0)) * scale).astype(bf16)
        m.k[layer, rows, :] = dot(low, m.mat(layer, 1)).astype(bf16)
        m.v[layer, rows, :] = (dot(low, m.mat(layer, 2)) + m.vec(layer, 1)).astype(bf16)
        return carry

    lax.fori_loop(0, tokens // (2 * RB), block, 0)


def probs_copy(m, layer, pair, slot, out):
    here, there = m.probs.at[slot], m.probs_hbm.at[layer, pair]
    if out:
        return pltpu.make_async_copy(here, there, m.probs_sem.at[slot])
    return pltpu.make_async_copy(there, here, m.probs_sem.at[slot])


def attend(m, layer, known, hook=None):
    tokens, width = m.q.shape[1:]
    pairs = width // PAIR
    masks = lane_masks()
    lane = lax.broadcasted_iota(jnp.int32, (RB, PAIR), 1)
    ones_lane = jnp.where(lane == 0, 1.0, 0.0).astype(bf16)
    eye = lax.broadcasted_iota(jnp.int32, (RB, RB), 0) == lax.broadcasted_iota(jnp.int32, (RB, RB), 1)
    col = lax.broadcasted_iota(jnp.int32, (1, RB), 1)
    blocks = tokens // RB

    def one_pair(pair, carry):
        if hook is not None:
            hook(pair)
        slot = lax.rem(pair, 2)
        cols = pl.ds(pl.multiple_of(pair * PAIR, PAIR), PAIR)

        @pl.when(pair >= 2)
        def _():
            probs_copy(m, layer, pair - 2, slot, True).wait()

        keys = m.k[layer, :, cols]
        keys_wide = jnp.concatenate([keys, m.key_bias[...]], axis=1)
        values = m.v[layer, :, cols]
        mixed = []
        for head in range(2):
            for block in range(blocks):
                rows = slice(block * RB, (block + 1) * RB)
                query = m.q[layer, rows, cols] * masks[head]
                query_wide = jnp.concatenate([query, ones_lane], axis=1)
                parts = []
                for other in range(blocks):
                    keys_rows = slice(other * RB, (other + 1) * RB)
                    if other == block:
                        part = dot_nt(query, keys[keys_rows])
                        hidden = jnp.where(col + block * RB >= known, NEG, 0.0)
                        part = jnp.where(eye, part, part + hidden)
                    else:
                        part = dot_nt(query_wide, keys_wide[keys_rows])
                    parts.append(part)
                scores = jnp.concatenate(parts, axis=1)
                peak = jnp.max(scores, axis=1, keepdims=True)
                m.probs[slot, head, rows, :] = jnp.exp2(scores - peak).astype(bf16)
            values_wide = values * masks[head] + masks[1 - head]
            mixed.append(dot(m.probs[slot, head], values_wide))
        probs_copy(m, layer, pair, slot, True).start()
        low = lax.broadcasted_iota(jnp.int32, (tokens, PAIR), 1) < 64
        raw = jnp.where(low, mixed[0], mixed[1])
        total = pltpu.roll(jnp.where(low, mixed[1], mixed[0]), 64, 1)
        inverse = 1.0 / total
        m.inv_total[layer, :, cols] = inverse.astype(bf16)
        mean = raw * inverse
        high = mean.astype(bf16)
        m.o[layer, :, cols] = high
        m.o_low[layer, :, cols] = (mean - high.astype(f32)).astype(bf16)
        return carry

    lax.fori_loop(0, pairs, one_pair, 0)
    for pair in (pairs - 2, pairs - 1):
        probs_copy(m, layer, pair, pair % 2, True).wait()


def feed_forward(m, layer, x_of, y_to):
    tokens = m.q.shape[1]

    def block(index, carry):
        rows = pl.ds(pl.multiple_of(index * RB, RB), RB)
        branch = dot(m.o[layer, rows, :], m.mat(layer, 3)) + m.vec(layer, 2)
        normed, inverse = normalize(x_of(rows) + branch)
        m.n1[layer, rows, :] = normed.astype(bf16)
        m.inv[rows, 2 * layer : 2 * layer + 1] = inverse
        first = normed * m.vec(layer, 5) + m.vec(layer, 6)
        pre = dot(first.astype(bf16), m.mat(layer, 4)) + m.vec(layer, 3)
        hidden, slope = gelu_parts(pre)
        low = hidden.astype(bf16)
        m.r[layer, rows, :] = low
        m.slope[layer, rows, :] = slope.astype(bf16)
        feed = dot(low, m.mat(layer, 5)) + m.vec(layer, 4)
        normed, inverse = normalize(first + feed)
        m.n2[layer, rows, :] = normed.astype(bf16)
        m.inv[rows, 2 * layer + 1 : 2 * layer + 2] = inverse
        y_to(rows, normed * m.vec(layer, 7) + m.vec(layer, 8))
        return carry

    lax.fori_loop(0, tokens // RB, block, 0)


def column_sum(value):
    rows, width = value.shape
    return jnp.sum(value.reshape(rows // 8, 8, width), axis=0)


def rows_back(m, layer, hook=None, ready=None):
    tokens = m.q.shape[1]
    for row in range(8):
        m.sums[row] = jnp.zeros_like(m.sums[row])

    def block(index, carry):
        if hook is not None:
            hook(index)
        rows = pl.ds(pl.multiple_of(index * RB, RB), RB)
        grad = m.g[rows, :]
        normed = m.n2[layer, rows, :].astype(f32)
        m.sums[0] += column_sum(grad * normed)
        m.sums[1] += column_sum(grad)
        back = norm_back(grad, normed, m.inv[rows, 2 * layer + 1 : 2 * layer + 2], m.vec(layer, 7))
        m.sums[2] += column_sum(back)
        low = back.astype(bf16)
        m.n2[layer, rows, :] = low
        pre = dot_nt(low, m.mat(layer, 5)) * m.slope[layer, rows, :].astype(f32)
        m.sums[3] += column_sum(pre)
        low = pre.astype(bf16)
        m.du[rows, :] = low
        grad = back + dot_nt(low, m.mat(layer, 4))
        normed = m.n1[layer, rows, :].astype(f32)
        m.sums[4] += column_sum(grad * normed)
        m.sums[5] += column_sum(grad)
        back = norm_back(grad, normed, m.inv[rows, 2 * layer : 2 * layer + 1], m.vec(layer, 5))
        m.sums[6] += column_sum(back)
        m.g[rows, :] = back
        low = back.astype(bf16)
        m.n1[layer, rows, :] = low
        m.inv_total[layer, rows, :] = (dot_nt(low, m.mat(layer, 3)) * m.inv_total[layer, rows, :].astype(f32)).astype(bf16)
        first = normed * m.vec(layer, 5) + m.vec(layer, 6)
        m.slope[layer, rows, :] = first.astype(bf16)
        return carry

    lax.fori_loop(0, tokens // RB, block, 0)
    for row, place in ((0, 7), (1, 8), (2, 4), (3, 3), (4, 5), (5, 6), (6, 2)):
        m.grad_vec(layer, place, jnp.sum(m.sums[row], axis=0, keepdims=True))
    if ready is not None:
        ready()
    m.grad_mat(layer, 5, dot_tn(m.r[layer], m.n2[layer]))
    m.grad_mat(layer, 4, dot_tn(m.slope[layer], m.du[...]))
    m.grad_mat(layer, 3, dot_tn(m.o[layer], m.n1[layer]))


def attend_back(m, layer, hook=None, xb=None):
    tokens, width = m.q.shape[1:]
    pairs = width // PAIR
    masks = lane_masks()
    blocks = tokens // RB

    def one_pair(pair, carry):
        slot = lax.rem(pair, 2)
        cols = pl.ds(pl.multiple_of(pair * PAIR, PAIR), PAIR)
        probs_copy(m, layer, pair, slot, False).wait()

        @pl.when(pair + 1 < pairs)
        def _():
            probs_copy(m, layer, pair + 1, 1 - slot, False).start()

        grad = m.inv_total[layer, :, cols]
        turned = pltpu.roll(
            grad.astype(f32) * (m.o[layer, :, cols].astype(f32) + m.o_low[layer, :, cols].astype(f32)), 64, 1
        )
        turned_high = turned.astype(bf16)
        turned_low = (turned - turned_high.astype(f32)).astype(bf16)
        values = m.v[layer, :, cols]
        keys = m.k[layer, :, cols]
        query_turned = m.q[layer, :, cols].T
        grad_turned = grad.T
        grad_query, grad_keys, grad_values = [], [], []
        for head in range(2):
            part = slice(head * 64, (head + 1) * 64)
            wide = jnp.concatenate(
                [grad * masks[head] - turned_high * masks[1 - head], -turned_low * masks[1 - head]], axis=1
            )
            values_wide = jnp.concatenate(
                [values * masks[head] + masks[1 - head], jnp.broadcast_to(masks[1 - head], values.shape)], axis=1
            )
            grad_values.append(dot(grad_turned[part], m.probs[slot, head]))
            for block in range(blocks):
                rows = slice(block * RB, (block + 1) * RB)
                score = dot_nt(wide[rows], values_wide)
                m.probs[slot, head, rows, :] = (score * m.probs[slot, head, rows, :].astype(f32)).astype(bf16)
            grad_keys.append(dot(query_turned[part], m.probs[slot, head]))
            grad_query.append(dot(m.probs[slot, head], keys))
            if hook is not None and head == 0:
                hook(pair, 0)
        low = lax.broadcasted_iota(jnp.int32, (tokens, PAIR), 1) < 64
        back_query = (jnp.where(low, grad_query[0], grad_query[1]) * 0.125).astype(bf16)
        back_keys = (jnp.concatenate(grad_keys, axis=0) * LN2).astype(bf16)
        back_values = jnp.concatenate(grad_values, axis=0).astype(bf16)
        m.q[layer, :, cols] = back_query
        m.k[layer, :, cols] = back_keys.T
        m.v[layer, :, cols] = back_values.T
        if xb is not None:
            m.grad_pair(layer, pair, dot(jnp.concatenate([back_query.T, back_keys, back_values], axis=0), xb[...]))
        if hook is not None:
            hook(pair, 1)
        return carry

    lax.fori_loop(0, pairs, one_pair, 0)


def project_back(m, layer, xb=None, ready=None, hook=None):
    tokens = m.q.shape[1]
    ones = jnp.ones((8, tokens), bf16)
    m.grad_vec(layer, 0, dot(ones, m.q[layer])[0:1])
    m.grad_vec(layer, 1, dot(ones, m.v[layer])[0:1])
    if xb is not None:
        m.grad_mat(layer, 0, dot_tn(xb[...], m.q[layer]))
        m.grad_mat(layer, 1, dot_tn(xb[...], m.k[layer]))
        m.grad_mat(layer, 2, dot_tn(xb[...], m.v[layer]))
    if ready is not None:
        ready()

    def block(index, carry):
        if hook is not None:
            hook(index)
        rows = pl.ds(pl.multiple_of(index * RB, RB), RB)
        m.g[rows, :] = (
            m.g[rows, :]
            + dot_nt(m.q[layer, rows, :], m.mat(layer, 0))
            + dot_nt(m.k[layer, rows, :], m.mat(layer, 1))
            + dot_nt(m.v[layer, rows, :], m.mat(layer, 2))
        )
        return carry

    lax.fori_loop(0, tokens // RB, block, 0)


def start_refs(q, k, v, o, o_low, inv_total, n1, n2, inv, r, slope, g, x1, du, sums, key_bias,
               probs, probs_sem, probs_hbm):
    m = Refs()
    m.q, m.k, m.v, m.o, m.o_low, m.inv_total = q, k, v, o, o_low, inv_total
    m.n1, m.n2, m.inv, m.r, m.slope, m.g, m.x1 = n1, n2, inv, r, slope, g, x1
    m.du, m.sums, m.key_bias = du, sums, key_bias
    m.probs, m.probs_sem, m.probs_hbm = probs, probs_sem, probs_hbm
    return m


def shared_scratch(layers, count, width):
    both = (layers, count, width)
    one = (count, width)
    return [
        pltpu.VMEM(both, bf16), pltpu.VMEM(both, bf16), pltpu.VMEM(both, bf16), pltpu.VMEM(both, bf16),
        pltpu.VMEM(both, bf16), pltpu.VMEM(both, bf16), pltpu.VMEM(both, bf16), pltpu.VMEM(both, bf16),
        pltpu.VMEM((count, 2 * layers), f32),
        pltpu.VMEM(both, bf16), pltpu.VMEM(both, bf16),
        pltpu.VMEM(one, f32), pltpu.VMEM(one, bf16),
        pltpu.VMEM(one, bf16),
        pltpu.VMEM((8, 8, width), f32),
        pltpu.VMEM((count, PAIR), bf16),
        pltpu.VMEM((2, 2, count, count), bf16),
        pltpu.SemaphoreType.DMA((2,)),
    ]


SHARED = 18


def plain_kernel(length_ref, class_ref, x_ref, cot_ref, w_ref, vec_ref, act_ref, dx_ref, mats_ref, vecs_ref, probs_hbm, *rest):
    m = start_refs(*rest[:SHARED], probs_hbm)
    out_sem = rest[SHARED]
    m.mat = lambda layer, place: w_ref[layer, place]
    m.vec = lambda layer, place: vec_ref[layer, place : place + 1, :]

    def grad_mat(layer, place, value):
        mats_ref[layer, place] = value.astype(bf16)

    def grad_vec(layer, place, value):
        vecs_ref[layer, place : place + 1, :] = value

    m.grad_mat, m.grad_vec = grad_mat, grad_vec
    length, klass = length_ref[0], class_ref[0]
    known = jnp.where(klass == 0, length, (length + 1) // 2)
    fill_bias(m, known)
    project(m, 0, x_ref)
    attend(m, 0, known)

    def keep_next(rows, value):
        m.g[rows, :] = value
        m.x1[rows, :] = value.astype(bf16)

    feed_forward(m, 0, lambda rows: x_ref[rows, :].astype(f32), keep_next)
    project(m, 1, m.x1)
    attend(m, 1, known)
    probs_copy(m, 1, 0, 0, False).start()

    def finish(rows, value):
        valid = lax.broadcasted_iota(jnp.int32, (RB, 1), 0) + rows.start < length
        act_ref[rows, :] = jnp.where(valid, value, 0.0).astype(bf16)
        m.g[rows, :] = jnp.where(valid, cot_ref[rows, :].astype(f32), 0.0)

    feed_forward(m, 1, lambda rows: m.g[rows, :], finish)
    for layer, xb in ((1, m.x1), (0, x_ref)):
        rows_back(m, layer)
        attend_back(m, layer)
        if layer:
            probs_copy(m, layer - 1, 0, 0, False).start()
        project_back(m, layer, xb)
    copy = pltpu.make_async_copy(m.g, dx_ref, out_sem)
    copy.start()
    copy.wait()


def plain_pass(lengths, classes, tokens, cotangent, mats, vecs):
    count, width = tokens.shape
    layers = mats.shape[0]
    vmem = pl.BlockSpec(memory_space=pltpu.VMEM)
    smem = pl.BlockSpec(memory_space=pltpu.SMEM)
    hbm = pl.BlockSpec(memory_space=pl.ANY)
    outs = pl.pallas_call(
        plain_kernel,
        out_shape=[
            jax.ShapeDtypeStruct((count, width), bf16),
            jax.ShapeDtypeStruct((count, width), f32),
            jax.ShapeDtypeStruct(mats.shape, bf16),
            jax.ShapeDtypeStruct((layers, 16, width), f32),
            jax.ShapeDtypeStruct((layers, width // PAIR, 2, count, count), bf16),
        ],
        in_specs=[smem, smem, vmem, vmem, vmem, vmem],
        out_specs=[vmem, hbm, vmem, vmem, hbm],
        scratch_shapes=shared_scratch(layers, count, width) + [pltpu.SemaphoreType.DMA],
        compiler_params=pltpu.CompilerParams(vmem_limit_bytes=67043328),
    )(lengths, classes, tokens, cotangent, mats, vecs)
    return outs[:4]


def adam_update(param, grad, first, second, rate):
    first_new = beta_first * first + (1.0 - beta_first) * grad
    second_new = beta_second * second + (1.0 - beta_second) * grad * grad
    first_hat = first_new * (1.0 / (1.0 - beta_first**adam_step))
    second_hat = second_new * (1.0 / (1.0 - beta_second**adam_step))
    param_new = param - rate * (first_hat / (jnp.sqrt(second_hat) + adam_eps) + decay_rate * param)
    return (param_new, first_new, second_new)


def plain_body(tokens, lengths, classes, cotangent, weights, vectors, first_weights, second_weights, first_vectors, second_vectors):
    mats = lax.all_gather(weights.astype(bf16), "shard", axis=2, tiled=True)
    vecs = lax.all_gather(vectors.astype(bf16), "shard", axis=2, tiled=True).astype(f32)
    vecs = jnp.pad(vecs, ((0, 0), (0, 16 - vecs.shape[1]), (0, 0)))
    activations, input_grad, grad_mats, grad_vecs = plain_pass(lengths, classes, tokens[0], cotangent[0], mats, vecs)
    grad_vecs = grad_vecs[:, : vectors.shape[1]]
    total_mats = lax.psum_scatter(grad_mats, "shard", scatter_dimension=2, tiled=True)
    total_vecs = lax.psum_scatter(grad_vecs.astype(bf16), "shard", scatter_dimension=2, tiled=True)
    total_mats = lax.psum(total_mats, "dp").astype(f32)
    total_vecs = lax.psum(total_vecs, "dp").astype(f32)
    new_weights, new_first_weights, new_second_weights = adam_update(
        weights, total_mats, first_weights, second_weights, learn_rate
    )
    new_vectors, new_first_vectors, new_second_vectors = adam_update(
        vectors, total_vecs, first_vectors, second_vectors, vector_rate
    )
    return (
        activations[None], input_grad[None], new_weights, new_weights.astype(bf16), new_first_weights, new_second_weights,
        new_vectors, new_first_vectors, new_second_vectors, total_vecs[:, 0],
    )


MESH = pl.DeviceIdType.MESH


def remote(src, dst, sems, place, device):
    return pltpu.make_async_remote_copy(
        src_ref=src, dst_ref=dst, send_sem=sems[0].at[place], recv_sem=sems[1].at[place], device_id=device, device_id_type=MESH
    )


class Spot:
    def __init__(self, planes, shards):
        self.planes, self.shards = planes, shards
        self.d, self.z = lax.axis_index("dp"), lax.axis_index("shard")
        self.c, self.t = lax.rem(self.d, 2), lax.div(self.d, 2)

    def plane(self, step):
        return lax.rem(self.t + step, self.planes)

    def shard(self, step):
        return lax.rem(self.z + step, self.shards)

    def partner(self, step):
        if self.shards != 4:
            return self.shard(self.shards - step)
        odd, half = step % 2, step // 2
        low, high = lax.rem(self.z, 2), lax.div(self.z, 2)
        return low + odd - 2 * odd * low + 2 * (high + half - 2 * half * high)

    def target(self, step):
        return self.partner(step) if self.shards == 4 else self.shard(step)

    def sibling(self):
        return (self.t * 2 + 1 - self.c, self.z)


class Weights:
    def __init__(self, spot, w, layer, first, count, index, z_sems, p_sems, c_sems):
        self.spot, self.index = spot, index
        self.z_sems, self.p_sems, self.c_sems = z_sems, p_sems, c_sems
        self.view = w.at[layer, first : first + count]

    def z_copy(self, step):
        s = self.spot
        piece = self.view.at[:, s.z, s.t, s.c]
        return remote(piece, piece, self.z_sems, (self.index, step - 1), (s.d, s.target(step)))

    def p_copy(self, z_step, t_step):
        s = self.spot
        piece = self.view.at[:, s.partner(z_step), s.t, s.c]
        place = (self.index, z_step - 1, t_step - 1)
        return remote(piece, piece, self.p_sems, place, (s.plane(t_step) * 2 + s.c, s.z))

    def c_copy(self, z_step):
        s = self.spot
        piece = self.view.at[:, s.partner(z_step), :, s.c]
        return remote(piece, piece, self.c_sems, (self.index, z_step - 1), s.sibling())

    def steps(self):
        return range(1, self.spot.shards)

    def send_z(self):
        for step in self.steps():
            self.z_copy(step).start()

    def send_p(self):
        for step in self.steps():
            self.z_copy(step).wait_recv()
            for other in range(1, self.spot.planes):
                self.p_copy(step, other).start()

    def send_c(self):
        for step in self.steps():
            for other in range(1, self.spot.planes):
                self.p_copy(step, other).wait_recv()
            self.c_copy(step).start()

    def arrive(self):
        for step in self.steps():
            self.c_copy(step).wait_recv()

    def close(self):
        for step in self.steps():
            self.z_copy(step).wait_send()
            self.c_copy(step).wait_send()
            for other in range(1, self.spot.planes):
                self.p_copy(step, other).wait_send()


class Piece:
    def __init__(self, spot, grads, from_core, from_plane, mine, from_shard, total, index, c_sems, p_sems, z_sems, a_sems, b_sems):
        self.spot, self.index = spot, index
        self.grads, self.from_core, self.from_plane = grads, from_core, from_plane
        self.mine, self.from_shard, self.total = mine, from_shard, total
        self.c_sems, self.p_sems, self.z_sems, self.a_sems, self.b_sems = c_sems, p_sems, z_sems, a_sems, b_sems

    def c_copy(self):
        s = self.spot
        return remote(self.grads.at[:, :, 1 - s.c], self.from_core, self.c_sems, (self.index,), s.sibling())

    def p_copy(self, step):
        s = self.spot
        other = s.plane(step)
        return remote(
            self.from_core.at[:, :, other], self.from_plane.at[step - 1], self.p_sems, (self.index, step - 1), (other * 2 + s.c, s.z)
        )

    def z_copy(self, step):
        s = self.spot
        other = s.target(step)
        return remote(self.mine.at[:, other], self.from_shard.at[step - 1], self.z_sems, (self.index, step - 1), (s.d, other))

    def a_copy(self, step):
        s = self.spot
        part = self.total.at[:, s.c, s.t]
        return remote(part, part, self.a_sems, (self.index, step - 1), (s.plane(step) * 2 + s.c, s.z))

    def b_copy(self):
        s = self.spot
        part = self.total.at[:, s.c]
        return remote(part, part, self.b_sems, (self.index,), s.sibling())

    def send_c(self):
        self.c_copy().start()

    def send_p(self):
        s = self.spot
        self.c_copy().wait()
        for mat in range(self.grads.shape[0]):
            own = self.grads[mat, :, s.c].astype(f32)
            self.from_core[mat] = (self.from_core[mat].astype(f32) + own).astype(bf16)
        for step in range(1, s.planes):
            self.p_copy(step).start()

    def send_z(self):
        s = self.spot
        for step in range(1, s.planes):
            self.p_copy(step).wait_recv()
        total = self.from_core[:, :, s.t].astype(f32)
        for step in range(1, s.planes):
            total = total + self.from_plane[step - 1].astype(f32)
        self.mine[...] = total.astype(bf16)
        for step in range(1, s.shards):
            self.z_copy(step).start()

    def send_a(self):
        s = self.spot
        for step in range(1, s.shards):
            self.z_copy(step).wait_recv()
        total = self.mine[:, s.z].astype(f32)
        for step in range(1, s.shards):
            total = total + self.from_shard[step - 1].astype(f32)
        self.total[:, s.c, s.t] = total.astype(bf16)
        for step in range(1, s.planes):
            self.a_copy(step).start()

    def send_b(self):
        for step in range(1, self.spot.planes):
            self.a_copy(step).wait_recv()
        self.b_copy().start()

    def arrive(self):
        self.b_copy().wait_recv()

    def close(self):
        for step in range(1, self.spot.planes):
            self.p_copy(step).wait_send()
            self.a_copy(step).wait_send()
        for step in range(1, self.spot.shards):
            self.z_copy(step).wait_send()
        self.b_copy().wait_send()


def full_kernel(planes, shards,
                length_ref, class_ref, x_hbm, cot_hbm, w_hbm, vec_in, act_hbm, dx_hbm, tot_hbm, tot_vec, probs_hbm, *rest):
    m = start_refs(*rest[:SHARED], probs_hbm)
    (x_ref, w, vec_own, vec_all, grads, pair_grads, grad_vecs, grads_vec,
     core_in, plane_in, mine, shard_in, total,
     core_in_p, plane_in_p, mine_p, shard_in_p, total_p,
     core_in_v, plane_in_v, mine_v, shard_in_v, total_v,
     stage,
     x_sem, stage_sem, feed_sem, pair_sem, vec_sem, out_sem,
     vz0, vz1, wz0, wz1, wp0, wp1, wc0, wc1,
     gc0, gc1, gp0, gp1, gz0, gz1, ga0, ga1, gb0, gb1) = rest[SHARED:]
    spot = Spot(planes, shards)
    tokens, width = x_ref.shape
    layers = w.shape[0]
    share = width // shards

    def mat(layer, place):
        return w[layer, place].reshape(width, width)

    m.mat = mat
    m.vec = lambda layer, place: vec_all[layer, place : place + 1, :]

    def grad_mat(layer, place, value):
        grads[place - 3] = value.astype(bf16).reshape(grads.shape[1:])

    def grad_pair(layer, pair, value):
        turned = value.astype(bf16).T
        for place in range(3):
            part = turned[:, place * PAIR : (place + 1) * PAIR]
            pair_grads[pair, place] = part.reshape(pair_grads.shape[2:])

    def grad_vec(layer, place, value):
        grad_vecs[layer, place : place + 1, :] = value

    m.grad_mat, m.grad_vec, m.grad_pair = grad_mat, grad_vec, grad_pair

    groups = [
        Weights(spot, w, layer, first, count, index, (wz0, wz1), (wp0, wp1), (wc0, wc1))
        for index, (layer, first, count) in enumerate(((0, 0, 1), (0, 1, 1), (0, 2, 1), (0, 3, 3), (1, 0, 3), (1, 3, 3)))
    ]
    sems = ((gc0, gc1), (gp0, gp1), (gz0, gz1), (ga0, ga1), (gb0, gb1))

    pairs = width // PAIR

    def feed_piece(layer):
        i = layers - 1 - layer
        return Piece(spot, grads, core_in.at[i], plane_in.at[i], mine.at[i], shard_in.at[i], total.at[i], i, *sems)

    def pair_piece(layer, pair):
        i = (layers - 1 - layer) * pairs + pair
        return Piece(spot, pair_grads.at[pair], core_in_p.at[i], plane_in_p.at[i], mine_p.at[i], shard_in_p.at[i],
                     total_p.at[i], layers + i, *sems)

    def feed_out(layer):
        i = layers - 1 - layer
        return pltpu.make_async_copy(total.at[i], tot_hbm.at[layer, 3:6], feed_sem.at[i])

    def pair_out(layer, pair):
        i = (layers - 1 - layer) * pairs + pair
        cols = pl.ds(pl.multiple_of(pair * PAIR, PAIR), PAIR)
        return pltpu.make_async_copy(total_p.at[i], tot_hbm.at[layer, 0:3, :, :, :, cols], pair_sem.at[i])

    feed1, feed0 = feed_piece(1), feed_piece(0)
    vecs = Piece(spot, grads_vec, core_in_v, plane_in_v, mine_v, shard_in_v, total_v, layers * (pairs + 1), *sems)

    x_copy = pltpu.make_async_copy(x_hbm, x_ref, x_sem.at[0])
    cot_copy = pltpu.make_async_copy(cot_hbm, m.du, x_sem.at[1])
    stages = [
        pltpu.make_async_copy(w_hbm.at[g // 2, 3 * (g % 2) : 3 * (g % 2) + 3], stage.at[g], stage_sem.at[g])
        for g in range(4)
    ]
    for copy in stages:
        copy.start()
    x_copy.start()
    cot_copy.start()

    barrier = pltpu.get_barrier_semaphore()
    for step in range(1, 2 * planes):
        pl.semaphore_signal(barrier, inc=1, device_id=(lax.rem(spot.d + step, 2 * planes), spot.z), device_id_type=MESH)
    for step in range(1, shards):
        pl.semaphore_signal(barrier, inc=1, device_id=(spot.d, spot.shard(step)), device_id_type=MESH)

    def cast(g):
        stages[g].wait()
        for place in range(3):
            low = stage[g, place].astype(bf16)
            w[g // 2, 3 * (g % 2) + place, spot.z] = low.reshape(w.shape[3:])

    cast(0)
    vec_all[...] = jnp.zeros_like(vec_all)
    for layer in range(layers):
        for place in range(vec_in.shape[0]):
            vec_all[layer, place : place + 1, 0:share] = vec_in[place, layer : layer + 1, :]
        vec_own[spot.z, layer] = vec_all[layer, :, 0:share].astype(bf16)
    pl.semaphore_wait(barrier, 2 * planes - 1 + shards - 1)
    for g in range(3):
        groups[g].send_z()

    def v_copy(step):
        part = vec_own.at[spot.z]
        return remote(part, part, (vz0, vz1), (step - 1,), (spot.d, spot.target(step)))

    for step in range(1, shards):
        v_copy(step).start()
    for g in range(1, 4):
        cast(g)
    length, klass = length_ref[0], class_ref[0]
    known = jnp.where(klass == 0, length, (length + 1) // 2)
    fill_bias(m, known)
    grad_vecs[...] = jnp.zeros_like(grad_vecs)
    grads_vec[...] = jnp.zeros_like(grads_vec)

    groups[0].send_p()
    groups[1].send_p()
    groups[0].send_c()
    groups[2].send_p()
    groups[1].send_c()
    groups[3].send_z()
    groups[2].send_c()
    for step in range(1, shards):
        v_copy(step).wait_recv()
    for other in range(shards):
        vec_all[:, :, other * share : (other + 1) * share] = vec_own[other].astype(f32)
    x_copy.wait()
    for place in range(3):
        groups[place].arrive()
        project_one(m, 0, place, x_ref)
    groups[3].send_p()
    groups[4].send_z()

    def on(index, value, action):
        pl.when(index == value)(action)

    def hook_forward(pair):
        def first():
            groups[3].send_c()
            groups[4].send_p()

        def third():
            groups[4].send_c()
            groups[5].send_p()

        on(pair, 1, first)
        on(pair, 2, groups[5].send_z)
        on(pair, 3, third)

    attend(m, 0, known, hook_forward)

    def keep_next(rows, value):
        m.g[rows, :] = value
        m.x1[rows, :] = value.astype(bf16)

    groups[3].arrive()
    feed_forward(m, 0, lambda rows: x_ref[rows, :].astype(f32), keep_next)
    groups[5].send_c()
    groups[4].arrive()
    project(m, 1, m.x1)
    attend(m, 1, known)
    probs_copy(m, 1, 0, 0, False).start()
    cot_copy.wait()

    def finish(rows, value):
        valid = lax.broadcasted_iota(jnp.int32, (RB, 1), 0) + rows.start < length
        m.probs[1, 0, rows, 0:width] = jnp.where(valid, value, 0.0).astype(bf16)
        m.g[rows, :] = jnp.where(valid, m.du[rows, :].astype(f32), 0.0)

    groups[5].arrive()
    feed_forward(m, 1, lambda rows: m.g[rows, :], finish)
    act_copy = pltpu.make_async_copy(m.probs.at[1, 0, :, 0:width], act_hbm, x_sem.at[2])
    act_copy.start()

    rows_back(m, 1)
    feed1.send_c()
    act_copy.wait()

    def hook_of(layer, feed):
        def hook(pair, place):
            if place == 0:
                on(pair, 0, feed.send_p)
                pl.when(pair >= 1)(pair_piece(layer, pair - 1).send_p)
                on(pair, 2, feed.send_z)
                pl.when(pair >= 2)(pair_piece(layer, pair - 2).send_z)
                pl.when(pair >= 3)(pair_piece(layer, pair - 3).send_a)
                if layer == 0:
                    on(pair, 0, feed1.send_b)
            else:
                pair_piece(layer, pair).send_c()
                on(pair, 3, feed.send_a)
                if layer == 0:
                    pair_piece(1, pair).send_b()

        return hook

    last = pairs - 1
    attend_back(m, 1, hook_of(1, feed1), m.x1)
    probs_copy(m, 0, 0, 0, False).start()

    def hook_dx1(index):
        def second():
            pair_piece(1, last).send_p()
            pair_piece(1, last - 1).send_z()
            pair_piece(1, last - 2).send_a()

        on(index, 2, second)

    project_back(m, 1, hook=hook_dx1)

    def hook_rows(index):
        def first():
            pair_piece(1, last).send_z()
            pair_piece(1, last - 1).send_a()

        on(index, 1, first)
        on(index, 3, pair_piece(1, last).send_a)

    rows_back(m, 0, hook_rows)
    feed0.send_c()
    attend_back(m, 0, hook_of(0, feed0), x_ref)

    def ready_last():
        for layer in range(layers):
            for other in range(shards):
                part = grad_vecs[layer, :, other * share : (other + 1) * share]
                grads_vec[0, other, layer, 0] = part.astype(bf16)
        vecs.send_c()

    def hook_dx0(index):
        def first():
            vecs.send_p()
            pair_piece(0, last - 1).send_z()
            pair_piece(0, last - 2).send_a()

        def third():
            pair_piece(0, last).send_z()
            vecs.send_z()
            pair_piece(0, last - 1).send_a()

        on(index, 0, pair_piece(0, last).send_p)
        on(index, 1, first)
        on(index, 3, third)

    project_back(m, 0, ready=ready_last, hook=hook_dx0)
    dx_copy = pltpu.make_async_copy(m.g, dx_hbm, out_sem)
    dx_copy.start()
    feed0.send_b()
    pair_piece(0, 0).send_b()
    pair_piece(0, last).send_a()
    vecs.send_a()
    for pair in range(1, last):
        pair_piece(0, pair).send_b()
    pair_piece(0, last).send_b()
    vecs.send_b()
    for layer, feed in ((1, feed1), (0, feed0)):
        feed.arrive()
        feed_out(layer).start()
        for pair in range(pairs):
            pair_piece(layer, pair).arrive()
            pair_out(layer, pair).start()
    vecs.arrive()
    vec_copy = pltpu.make_async_copy(total_v.at[0, :, 0], tot_vec, vec_sem)
    vec_copy.start()
    for group in groups:
        group.close()
    for step in range(1, shards):
        v_copy(step).wait_send()
    for layer, feed in ((1, feed1), (0, feed0)):
        feed.close()
        for pair in range(pairs):
            pair_piece(layer, pair).close()
    vecs.close()
    for layer in (1, 0):
        feed_out(layer).wait()
        for pair in range(pairs):
            pair_out(layer, pair).wait()
    vec_copy.wait()
    dx_copy.wait()


CHUNKS = 6


def last_kernel(act_in, dx_in, total_in, w_in, first_in, second_in, tot_vec, vec_ref, vec_first, vec_second,
                act_out, dx_out, new_w, low_w, new_first, new_second, vec_out, first_out, second_out, query_out,
                act, dx, total, w, first, second, low, token_load, token_store, loads, stores):
    rows = w.shape[0] // CHUNKS

    def piece(chunk):
        return pl.ds(pl.multiple_of(chunk * rows, rows), rows)

    def load(chunk):
        part = piece(chunk)
        return [
            pltpu.make_async_copy(source.at[part], here.at[part], loads.at[which, chunk])
            for which, (source, here) in enumerate(((w_in, w), (total_in, total), (first_in, first), (second_in, second)))
        ]

    def store(chunk):
        part = piece(chunk)
        return [
            pltpu.make_async_copy(here.at[part], target.at[part], stores.at[which, chunk])
            for which, (here, target) in enumerate(((w, new_w), (low, low_w), (first, new_first), (second, new_second)))
        ]

    ins = [pltpu.make_async_copy(dx_in, dx, token_load.at[0]), pltpu.make_async_copy(act_in, act, token_load.at[1])]
    outs = [pltpu.make_async_copy(dx, dx_out, token_store.at[0]), pltpu.make_async_copy(act, act_out, token_store.at[1])]
    for copy in load(0) + ins:
        copy.start()
    for chunk in range(1, CHUNKS):
        for copy in load(chunk):
            copy.start()

    def one(chunk, carry):
        for copy in load(chunk):
            copy.wait()

        def block(index, inner):
            part = pl.ds(pl.multiple_of(chunk * rows + index * 16, 16), 16)
            param, one_moment, two_moment = adam_update(
                w[part, :], total[part, :].astype(f32), first[part, :], second[part, :], learn_rate
            )
            w[part, :] = param
            low[part, :] = param.astype(bf16)
            first[part, :] = one_moment
            second[part, :] = two_moment
            return inner

        lax.fori_loop(0, rows // 16, block, 0)
        for copy in store(chunk):
            copy.start()
        for which in range(2):

            @pl.when(chunk == which)
            def _():
                ins[which].wait()
                outs[which].start()

        return carry

    lax.fori_loop(0, CHUNKS, one, 0)
    count, layers = vec_ref.shape[:2]
    for layer in range(layers):
        grads = tot_vec[layer].astype(f32)
        for place in range(count):
            one = slice(layer, layer + 1)
            grad = grads[place : place + 1]
            param, one_moment, two_moment = adam_update(
                vec_ref[place, one, :], grad, vec_first[place, one, :], vec_second[place, one, :], vector_rate
            )
            vec_out[place, one, :] = param
            first_out[place, one, :] = one_moment
            second_out[place, one, :] = two_moment
            if place == 0:
                query_out[one, :] = grad
    for copy in outs:
        copy.wait()
    for chunk in range(CHUNKS):
        for copy in store(chunk):
            copy.wait()


def finish_step(parts, weights, vectors, first_weights, second_weights, first_vectors, second_vectors):
    act, dx, total_mats, total_vecs = parts
    count, width = act.shape
    layers, places, share = vectors.shape
    flat = lambda value: value.reshape(-1, width)
    turned = lambda value: jnp.transpose(value, (1, 0, 2))
    mat_rows = weights.size // width
    hbm = pl.BlockSpec(memory_space=pl.ANY)
    vmem = pl.BlockSpec(memory_space=pltpu.VMEM)
    dma = pltpu.SemaphoreType.DMA
    shape = jax.ShapeDtypeStruct
    mat, low = (mat_rows, width), pltpu.VMEM((mat_rows, width), bf16)
    outs = pl.pallas_call(
        last_kernel,
        out_shape=[
            shape(act.shape, bf16), shape(dx.shape, f32), shape(mat, f32), shape(mat, bf16), shape(mat, f32), shape(mat, f32),
            shape((places, layers, share), f32), shape((places, layers, share), f32), shape((places, layers, share), f32),
            shape((layers, share), f32),
        ],
        in_specs=[hbm] * 6 + [vmem] * 4,
        out_specs=[hbm] * 6 + [vmem] * 4,
        scratch_shapes=[
            pltpu.VMEM(act.shape, bf16), pltpu.VMEM(dx.shape, f32), low, pltpu.VMEM(mat, f32), pltpu.VMEM(mat, f32),
            pltpu.VMEM(mat, f32), low, dma((2,)), dma((2,)), dma((4, CHUNKS)), dma((4, CHUNKS)),
        ],
        compiler_params=pltpu.CompilerParams(vmem_limit_bytes=67043328),
    )(act, dx, flat(total_mats), flat(weights), flat(first_weights), flat(second_weights), total_vecs,
      turned(vectors), turned(first_vectors), turned(second_vectors))
    mats = [value.reshape(weights.shape) for value in outs[2:6]]
    vecs = [turned(value) for value in outs[6:9]]
    return (outs[0][None], outs[1][None], *mats, *vecs, outs[9])


def full_body(planes, shards, tokens, lengths, classes, cotangent, weights, vectors, first_weights, second_weights, first_vectors,
              second_vectors):
    _, count, width = tokens.shape
    layers = weights.shape[0]
    rows = width // (2 * planes * shards)
    share = width // shards
    pairs = width // PAIR
    sent = layers * (pairs + 1) + 1
    vmem = pl.BlockSpec(memory_space=pltpu.VMEM)
    smem = pl.BlockSpec(memory_space=pltpu.SMEM)
    hbm = pl.BlockSpec(memory_space=pl.ANY)
    dma = pltpu.SemaphoreType.DMA

    def pieces(lead, mats, columns):
        return [
            pltpu.VMEM(lead + (mats, shards, planes, rows, columns), bf16),
            pltpu.VMEM(lead + (planes - 1, mats, shards, rows, columns), bf16),
            pltpu.VMEM(lead + (mats, shards, rows, columns), bf16),
            pltpu.VMEM(lead + (shards - 1, mats, rows, columns), bf16),
            pltpu.VMEM(lead + (mats, 2, planes, rows, columns), bf16),
        ]

    def twice(*shape):
        return [dma(shape), dma(shape)]

    scratch = shared_scratch(layers, count, width) + [
        pltpu.VMEM((count, width), bf16),
        pltpu.VMEM((layers, 6, shards, planes, 2, rows, width), bf16),
        pltpu.VMEM((shards, layers, 16, share), bf16),
        pltpu.VMEM((layers, 16, width), f32),
        pltpu.VMEM((3, shards, 2, planes, rows, width), bf16),
        pltpu.VMEM((pairs, 3, shards, 2, planes, rows, PAIR), bf16),
        pltpu.VMEM((layers, 16, width), f32),
        pltpu.VMEM((1, shards, 2, planes, rows, share), bf16),
        *pieces((layers,), 3, width),
        *pieces((layers * pairs,), 3, PAIR),
        *pieces((), 1, share),
        pltpu.VMEM((4, 3, share, width), f32),
        dma((3,)), dma((4,)), dma((layers,)), dma((layers * pairs,)), dma, dma,
        *twice(shards - 1),
        *twice(6, shards - 1), *twice(6, shards - 1, planes - 1), *twice(6, shards - 1),
        *twice(sent), *twice(sent, planes - 1), *twice(sent, shards - 1), *twice(sent, planes - 1), *twice(sent),
    ]
    shape = jax.ShapeDtypeStruct
    outs = pl.pallas_call(
        functools.partial(full_kernel, planes, shards),
        out_shape=[
            shape((count, width), bf16), shape((count, width), f32), shape((layers, 6, 2, planes, rows, width), bf16),
            shape((layers, rows, share), bf16), shape((layers, pairs, 2, count, count), bf16),
        ],
        in_specs=[smem, smem] + [hbm] * 3 + [vmem],
        out_specs=[hbm] * 5,
        scratch_shapes=scratch,
        compiler_params=pltpu.CompilerParams(vmem_limit_bytes=67043328, collective_id=0, has_side_effects=True),
    )(lengths, classes, tokens[0], cotangent[0], weights, jnp.transpose(vectors, (1, 0, 2)))
    return finish_step(outs[:4], weights, vectors, first_weights, second_weights, first_vectors, second_vectors)


def solution(mesh):
    devices, shards = mesh.shape["dp"], mesh.shape["shard"]

    def body(*args):
        width = args[0].shape[-1]
        layers = args[4].shape[0]
        rows, left = divmod(width, devices * shards)
        if devices % 2 == 0 and devices > 2 and shards > 1 and left == 0 and rows == 16 and layers == 2 and width // shards % PAIR == 0:
            return full_body(devices // 2, shards, *args)
        return plain_body(*args)

    cell = P(("dp", "shard"), None, None)
    mats = P(None, None, "shard", None)
    vecs = P(None, None, "shard")
    one = P(("dp", "shard"))
    in_specs = (cell, one, one, cell, mats, vecs, mats, mats, vecs, vecs)
    out_specs = (cell, cell, mats, mats, mats, mats, vecs, vecs, vecs, P(None, "shard"))
    return jax.shard_map(body, mesh=mesh, in_specs=in_specs, out_specs=out_specs, check_vma=False)
```
